32 devices in a mesh: fsdp: 4 (over y, x), ctx: 4 (over z), tp: 2 (over core).
Axes of the slice: x: 2, y: 2, z: 4, core: 2. Of those that a mesh axis runs over, the one named last changes fastest.
Arguments:
- inputs: bfloat16 [4, 2048, 1024], P('fsdp', 'ctx'), may hold values from -6 to 6
- encoder_states: bfloat16 [4, 256, 1024], P('fsdp', 'ctx'), may hold values from -6 to 6
- seq_lengths: int32 [4], P('fsdp'), may hold values from 512 to 2048, as said below
- enc_lengths: int32 [4], P('fsdp'), may hold values from 64 to 256, as said below
- cotangent: bfloat16 [4, 2048, 1024], P('fsdp', 'ctx'), may hold values from -6 to 6
- norm_gains: bfloat16 [4, 1024], P(None, ('fsdp', 'ctx')), may hold values from 0.5 to 1.5
- norm_biases: bfloat16 [4, 1024], P(None, ('fsdp', 'ctx')), may hold values from -3 to 3
- w_query: bfloat16 [1024, 1024], P(('fsdp', 'ctx'), 'tp'), may hold values from -0.1875 to 0.1875
- w_key: bfloat16 [1024, 1024], P(('fsdp', 'ctx'), 'tp'), may hold values from -0.1875 to 0.1875
- w_value: bfloat16 [1024, 1024], P(('fsdp', 'ctx'), 'tp'), may hold values from -0.1875 to 0.1875
- w_out: bfloat16 [1024, 1024], P('tp', ('fsdp', 'ctx')), may hold values from -1.5 to 1.5
- w_cross_query: bfloat16 [1024, 1024], P(('fsdp', 'ctx'), 'tp'), may hold values from -0.1875 to 0.1875
- w_cross_key: bfloat16 [1024, 1024], P(('fsdp', 'ctx'), 'tp'), may hold values from -0.1875 to 0.1875
- w_cross_value: bfloat16 [1024, 1024], P(('fsdp', 'ctx'), 'tp'), may hold values from -0.1875 to 0.1875
- w_cross_out: bfloat16 [1024, 1024], P('tp', ('fsdp', 'ctx')), may hold values from -1 to 1
- w_inner: bfloat16 [1024, 4096], P(('fsdp', 'ctx'), 'tp'), may hold values from -0.1875 to 0.1875
- w_outer: bfloat16 [4096, 1024], P('tp', ('fsdp', 'ctx')), may hold values from -0.125 to 0.125
Outputs:
- output: float32 [4, 2048, 1024], P('fsdp', 'ctx')
- input_grad: float32 [4, 2048, 1024], P('fsdp', 'ctx')
- encoder_grad: float32 [4, 256, 1024], P('fsdp', 'ctx')
- grad_norm_gains: float32 [4, 1024], P(None, ('fsdp', 'ctx'))
- grad_norm_biases: float32 [4, 1024], P(None, ('fsdp', 'ctx'))
- grad_query: float32 [1024, 1024], P(('fsdp', 'ctx'), 'tp')
- grad_key: float32 [1024, 1024], P(('fsdp', 'ctx'), 'tp')
- grad_value: float32 [1024, 1024], P(('fsdp', 'ctx'), 'tp')
- grad_out: float32 [1024, 1024], P('tp', ('fsdp', 'ctx'))
- grad_cross_query: float32 [1024, 1024], P(('fsdp', 'ctx'), 'tp')
- grad_cross_key: float32 [1024, 1024], P(('fsdp', 'ctx'), 'tp')
- grad_cross_value: float32 [1024, 1024], P(('fsdp', 'ctx'), 'tp')
- grad_cross_out: float32 [1024, 1024], P('tp', ('fsdp', 'ctx'))
- grad_inner: float32 [1024, 4096], P(('fsdp', 'ctx'), 'tp')
- grad_outer: float32 [4096, 1024], P('tp', ('fsdp', 'ctx'))
The draws below stay inside these ranges and needn't reach their ends.
Inputs may be any that keep to these rules, and one draw needn't show every extreme that they name: `seq_lengths`: each sequence's valid slots are its first ones; some sequence has exactly 2048 and some exactly 512. `enc_lengths`: each sequence's valid encoder rows are its first ones; some sequence has exactly 256 and some exactly 64.
All inputs are finite; a program needn't handle non-finite values.
Results may differ from the reference program's by a relative error of at most 0.018.
Values may be sent and summed in bfloat16 or wider, within the bound.
No kernel may reach another device: no remote copies, remote signals or barrier semaphores. Data moves between devices by JAX's collectives and lax.ppermute only.
A program may use at most 192 MiB of HBM per device.

```python
import jax
import jax.numpy as jnp
from jax import lax

D = 1024
HEADS = 16
HEAD_DIM = 64
FF = 4096
LEN = 2048
ENC = 256
SEQS = 4


def edge_lengths(key, count, least, most):
    first, second = jax.random.split(key)
    values = jax.random.randint(first, (count,), least, most + 1)
    pick = jax.random.randint(second, (), 0, count)
    slots = jnp.arange(count)
    values = jnp.where(slots == pick, most, values)
    values = jnp.where(slots == (pick + 1) % count, least, values)
    return values.astype(jnp.int32)


def draw_seq_lengths(key, part):
    return edge_lengths(jax.random.fold_in(key, 11), SEQS, LEN // 4, LEN)


def draw_enc_lengths(key, part):
    return edge_lengths(jax.random.fold_in(key, 23), SEQS, ENC // 4, ENC)


def level_of(own_key, dims, shards, low, largest):
    level, own = 1.0, jax.random.fold_in(own_key, 6)
    for axis_at, parts in shards:
        draws = jnp.exp(jax.random.uniform(jax.random.fold_in(own, axis_at), (parts,), jnp.float32, low / len(shards), largest / len(shards)))
        level = level * jnp.repeat(draws, dims[axis_at] // parts).reshape([-1 if axis == axis_at else 1 for axis in range(len(dims))])
    return level


def scatter_about(stream_key, shape, width, bound, pieces=(), held_as=jnp.bfloat16):
    values = width * jax.random.normal(stream_key, shape, jnp.float32)
    if pieces:
        values = values * level_of(stream_key, shape, pieces, -0.22, 0.18)
    return jnp.clip(values, -bound, bound).astype(held_as)


def setup_inputs(seed: int = 0) -> dict:
    seeds = jax.random.split(jax.random.key(seed), 18)
    return {
        "inputs": scatter_about(seeds[0], (SEQS, LEN, D), 1.0, 6.0, ((0, 4), (1, 4))),
        "encoder_states": scatter_about(seeds[1], (SEQS, ENC, D), 1.0, 6.0, ((0, 4), (1, 4))),
        "seq_lengths": draw_seq_lengths(jax.random.fold_in(seeds[17], 71), 0),
        "enc_lengths": draw_enc_lengths(jax.random.fold_in(seeds[17], 71), 0),
        "cotangent": scatter_about(seeds[4], (SEQS, LEN, D), 1.0, 6.0, ((0, 4), (1, 4))),
        "norm_gains": jnp.clip(1.0 + 0.1 * jax.random.normal(seeds[5], (4, D), jnp.float32), 0.5, 1.5).astype(jnp.bfloat16),
        "norm_biases": scatter_about(seeds[6], (4, D), 0.5, 3.0, ((1, 16),)),
        "w_query": scatter_about(seeds[7], (D, D), D ** -0.5, 0.1875, ((0, 16), (1, 2))),
        "w_key": scatter_about(seeds[8], (D, D), D ** -0.5, 0.1875, ((0, 16), (1, 2))),
        "w_value": scatter_about(seeds[9], (D, D), D ** -0.5, 0.1875, ((0, 16), (1, 2))),
        "w_out": scatter_about(seeds[10], (D, D), (D // 64) ** -0.5, 1.5, ((0, 2), (1, 16))),
        "w_cross_query": scatter_about(seeds[11], (D, D), D ** -0.5, 0.1875, ((0, 16), (1, 2))),
        "w_cross_key": scatter_about(seeds[12], (D, D), D ** -0.5, 0.1875, ((0, 16), (1, 2))),
        "w_cross_value": scatter_about(seeds[13], (D, D), D ** -0.5, 0.1875, ((0, 16), (1, 2))),
        "w_cross_out": scatter_about(seeds[14], (D, D), (D // 32) ** -0.5, 1.0, ((0, 2), (1, 16))),
        "w_inner": scatter_about(seeds[15], (D, FF), D ** -0.5, 0.1875, ((0, 16), (1, 2))),
        "w_outer": scatter_about(seeds[16], (FF, D), (FF // 2) ** -0.5, 0.125, ((0, 2), (1, 16))),
    }


@jax.custom_vjp
def low(v):
    return lax.optimization_barrier(v.astype(jnp.bfloat16)).astype(jnp.float32)

@jax.custom_vjp
def low_back(v):
    return v

def low_keep(v):
    return (low(v), None)

def low_pass(kept, grad):
    return (grad,)

def back_keep(v):
    return (v, None)

def back_low(kept, grad):
    return (low(grad),)
low.defvjp(low_keep, low_pass)
low_back.defvjp(back_keep, back_low)
EPS = 1e-05
HIGH = lax.Precision.HIGHEST

def smooth_gate(values):
    return 0.5 * values * (1.0 + jnp.tanh(0.7978845608028654 * (values + 0.044715 * values * values * values)))

def layer_norm(values, gain, bias):
    mean = lax.optimization_barrier(jnp.mean(values, axis=-1, keepdims=True))
    centred = values - mean
    variance = lax.optimization_barrier(jnp.mean(centred * centred, axis=-1, keepdims=True))
    return centred * lax.rsqrt(variance + EPS) * gain + bias

def matmul(left, right):
    return jnp.dot(left, right, precision=HIGH)

def attention(query, keys, values, limit, causal):
    rows = query.shape[0]
    block = min(512, rows)
    query_heads = query.reshape(rows // block, block, HEADS, HEAD_DIM)
    places = jnp.arange(rows, dtype=jnp.int32).reshape(rows // block, block)
    key_heads = keys.reshape(keys.shape[0], HEADS, HEAD_DIM)
    value_heads = values.reshape(values.shape[0], HEADS, HEAD_DIM)
    key_places = jnp.arange(keys.shape[0], dtype=jnp.int32)

    def one_block(item):
        query_part, place_part = item
        score = low_back(jnp.einsum('qhe,khe->hqk', query_part, key_heads, precision=HIGH) * HEAD_DIM ** (-0.5))
        allowed = key_places[None, :] < limit
        if causal:
            allowed = allowed & (key_places[None, :] <= place_part[:, None])
        score = jnp.where(allowed[None], score, -1e+30)
        top = lax.optimization_barrier(jnp.max(score, axis=-1, keepdims=True))
        weights = jnp.where(allowed[None], jnp.exp(score - top), 0.0)
        chance = weights / lax.optimization_barrier(jnp.sum(weights, axis=-1, keepdims=True))
        mixed = jnp.einsum('hqk,khe->qhe', low(chance), value_heads, precision=HIGH)
        return mixed.reshape(query_part.shape[0], HEADS * HEAD_DIM)
    mixed_all = lax.map(jax.checkpoint(one_block), (query_heads, places))
    return mixed_all.reshape(rows, HEADS * HEAD_DIM)

def layer(params, inputs, encoder, seq_limit, enc_limit):
    gains, biases, w_query, w_key, w_value, w_out, w_cross_query, w_cross_key, w_cross_value, w_cross_out, w_inner, w_outer = params
    valid = (jnp.arange(LEN, dtype=jnp.int32) < seq_limit).astype(inputs.dtype)[:, None]
    attn_in = low(layer_norm(inputs, gains[0], biases[0]))
    query = low(low_back(matmul(attn_in, w_query)))
    key = low(low_back(matmul(attn_in, w_key)))
    value = low(low_back(matmul(attn_in, w_value)))
    attn = low(low_back(attention(query, key, value, seq_limit, True)))
    first = inputs + low_back(matmul(attn, w_out))
    cross_in = low(layer_norm(first, gains[1], biases[1]))
    cross_q = low(low_back(matmul(cross_in, w_cross_query)))
    cross_k = low(low_back(matmul(encoder, w_cross_key)))
    cross_v = low(low_back(matmul(encoder, w_cross_value)))
    cross = low(low_back(attention(cross_q, cross_k, cross_v, enc_limit, False)))
    second = first + low_back(matmul(cross, w_cross_out))
    ffn_in = low(layer_norm(second, gains[2], biases[2]))
    inner = low_back(matmul(ffn_in, w_inner))
    active = low(smooth_gate(inner))
    third = second + low_back(matmul(active, w_outer))
    return layer_norm(third, gains[3], biases[3]) * valid

def reference(inputs, encoder_states, seq_lengths, enc_lengths, cotangent, norm_gains, norm_biases, w_query, w_key, w_value, w_out, w_cross_query, w_cross_key, w_cross_value, w_cross_out, w_inner, w_outer):
    params = tuple((weight.astype(jnp.float32) for weight in (norm_gains, norm_biases, w_query, w_key, w_value, w_out, w_cross_query, w_cross_key, w_cross_value, w_cross_out, w_inner, w_outer)))

    def one_sequence(totals, item):
        seq_inputs, seq_encoder, seq_limit, enc_limit, seq_cotangent = item

        def forward(weights, values, encoder):
            return layer(weights, values, encoder, seq_limit, enc_limit)
        result, pullback = jax.vjp(forward, params, seq_inputs.astype(jnp.float32), seq_encoder.astype(jnp.float32))
        grad_params, grad_inputs, grad_encoder = pullback(seq_cotangent.astype(jnp.float32))
        totals = jax.tree.map(jnp.add, totals, grad_params)
        return (totals, (result, grad_inputs, grad_encoder))
    zeros = tuple((jnp.zeros_like(weight) for weight in params))
    totals, (outputs, input_grads, encoder_grads) = lax.scan(one_sequence, zeros, (inputs, encoder_states, seq_lengths, enc_lengths, cotangent))
    return (outputs, input_grads, encoder_grads, totals[0], totals[1], totals[2], totals[3], totals[4], totals[5], totals[6], totals[7], totals[8], totals[9], totals[10], totals[11])
```

```python
import functools

import jax
import jax.numpy as jnp
from jax import lax
from jax.experimental import pallas as pl
from jax.experimental.pallas import tpu as pltpu
from jax.sharding import PartitionSpec as P

HEAD_DIM = 64
PAIR = 2 * HEAD_DIM
EPS = 1e-05
GELU_A = 0.7978845608028654
GELU_B = 0.044715
BF = jnp.bfloat16
F32 = jnp.float32
LOW = -1e30


def nn(left, right):
    return jnp.dot(left, right, preferred_element_type=F32)


def tn(left, right):
    return lax.dot_general(left, right, (((0,), (0,)), ((), ())), preferred_element_type=F32)


def nt(left, right):
    return lax.dot_general(left, right, (((1,), (1,)), ((), ())), preferred_element_type=F32)


def smooth_gate(values):
    return 0.5 * values * (1.0 + jnp.tanh(GELU_A * (values + GELU_B * values * values * values)))


def norm_parts(values):
    mean = jnp.mean(values, axis=-1, keepdims=True)
    centred = values - mean
    scale = lax.rsqrt(jnp.mean(centred * centred, axis=-1, keepdims=True) + EPS)
    return (centred * scale, scale)


def norm_back(grad_result, normed, scale, gain):
    grad_normed = grad_result * gain
    grad_input = scale * (
        grad_normed
        - jnp.mean(grad_normed, axis=-1, keepdims=True)
        - normed * jnp.mean(grad_normed * normed, axis=-1, keepdims=True)
    )
    return (grad_input, jnp.sum(grad_result * normed, axis=0), jnp.sum(grad_result, axis=0))


def shift(value, axis, step):
    n = lax.axis_size(axis)
    return lax.ppermute(value, axis, [(i, (i + step) % n) for i in range(n)])


def swap(value):
    return shift(value, "tp", 1)


def in_order(pieces, axis):
    n = len(pieces)
    me = lax.axis_index(axis)
    return [lax.select_n(me, *[pieces[(m - j) % n] for m in range(n)]) for j in range(n)]


def gather_direct(value, axis):
    n = lax.axis_size(axis)
    return [value] + [shift(value, axis, s) for s in range(1, n)]


def gather_line(value, axis):
    n = lax.axis_size(axis)
    me = lax.axis_index(axis)
    ups, downs = [value], [value]
    for s in range(1, n):
        ups.append(lax.ppermute(ups[-1], axis, [(i, i + 1) for i in range(s - 1, n - 1)]))
        downs.append(lax.ppermute(downs[-1], axis, [(i, i - 1) for i in range(1, n - s + 1)]))
    return [value] + [jnp.where(me >= s, ups[s], downs[n - s]) for s in range(1, n)]


def exchange_direct(blocks, axis):
    n = lax.axis_size(axis)
    me = lax.axis_index(axis)

    def pick(d):
        return lax.dynamic_index_in_dim(blocks, d, 0, keepdims=False)

    return [pick(me)] + [shift(pick((me + s) % n), axis, s) for s in range(1, n)]


def total(pieces):
    out = pieces[0].astype(F32)
    for piece in pieces[1:]:
        out = out + piece.astype(F32)
    return out


def bits_of(axis, low_first):
    n = lax.axis_size(axis)
    order = list(range(n.bit_length() - 1))
    return order if low_first else order[::-1]


def gather_double(value, axis, low_first):
    n = lax.axis_size(axis)
    count = n.bit_length() - 1
    me = lax.axis_index(axis)
    held = value.reshape((1,) * count + value.shape)
    for bit in bits_of(axis, low_first):
        other = lax.ppermute(held, axis, [(i, i ^ (1 << bit)) for i in range(n)])
        mine = (me >> bit) & 1
        held = jnp.concatenate(
            [jnp.where(mine == 0, held, other), jnp.where(mine == 0, other, held)],
            axis=count - 1 - bit,
        )
    return held.reshape((n * value.shape[0],) + value.shape[1:])


def scatter_double(value, axis, low_first):
    n = lax.axis_size(axis)
    count = n.bit_length() - 1
    me = lax.axis_index(axis)
    rows = value.shape[0] // n
    held = value.reshape((2,) * count + (rows,) + value.shape[1:])
    for bit in bits_of(axis, low_first):
        dim = count - 1 - bit
        mine = (me >> bit) & 1
        away = lax.dynamic_slice_in_dim(held, 1 - mine, 1, dim)
        keep = lax.dynamic_slice_in_dim(held, mine, 1, dim)
        came = lax.ppermute(away, axis, [(i, i ^ (1 << bit)) for i in range(n)])
        held = (keep.astype(F32) + came.astype(F32)).astype(value.dtype)
    return held.reshape((rows,) + value.shape[1:])


def scatter_direct(value, axis):
    n = lax.axis_size(axis)
    blocks = value.reshape((n, value.shape[0] // n) + value.shape[1:])
    return total(exchange_direct(blocks, axis))


def fetch_rows(shard, low_first):
    held = jnp.concatenate(in_order(gather_line(shard, "ctx"), "ctx"), axis=0)
    return gather_double(held, "fsdp", low_first)


def return_rows(grad, low_first):
    return scatter_direct(scatter_double(grad, "fsdp", low_first), "ctx")


def lanes_of(head, shape):
    lane = lax.broadcasted_iota(jnp.int32, shape, len(shape) - 1)
    return (lane // HEAD_DIM) == head


def spans(count, block):
    half = block // 2
    return half


def self_forward_kernel(n, block, info, qkv, mixed, logs, q_s, k_s, v_s):
    limit, me_c, me_t = info[0], info[1], info[2]
    half = block // 2
    for c in range(n):
        for t in range(2):
            place = lax.rem(me_c - c + n, n) * block + (me_t ^ t) * half
            place = pl.multiple_of(place, half)
            to = slice(c * block + t * half, c * block + t * half + half)
            rows = qkv[pl.ds(place, half), :]
            q_s[to, :] = rows[:, :PAIR] * jnp.asarray(HEAD_DIM**-0.5, BF)
            keys = rows[:, PAIR : 2 * PAIR]
            for h in range(2):
                k_s[h, to, :] = jnp.where(lanes_of(h, keys.shape), keys, jnp.zeros_like(keys))
            v_s[:, to] = rows[:, 2 * PAIR :].astype(F32).T.astype(BF)

    def one(i, _):
        at_q = pl.multiple_of(i * block, block)
        query = q_s[pl.ds(at_q, block), :]

        def step(masked, j, state):
            at_k = pl.multiple_of(j * block, block)
            out = []
            for h in range(2):
                top, tot, acc = state[h]
                score = nt(k_s[h, pl.ds(at_k, block), :], query)
                if masked:
                    key_at = at_k + lax.broadcasted_iota(jnp.int32, score.shape, 0)
                    slot_at = at_q + lax.broadcasted_iota(jnp.int32, score.shape, 1)
                    score = jnp.where((key_at <= slot_at) & (key_at < limit), score, LOW)
                new_top = jnp.maximum(top, jnp.max(score, axis=0, keepdims=True))
                fade = jnp.exp(top - new_top)
                chance = jnp.exp(score - new_top)
                tot = tot * fade + jnp.sum(chance, axis=0, keepdims=True)
                part = nn(
                    v_s[h * HEAD_DIM : (h + 1) * HEAD_DIM, pl.ds(at_k, block)], chance.astype(BF)
                )
                out.append((new_top, tot, acc * fade + part))
            return tuple(out)

        start = tuple(
            (
                jnp.full((1, block), LOW, F32),
                jnp.zeros((1, block), F32),
                jnp.zeros((HEAD_DIM, block), F32),
            )
            for _ in range(2)
        )
        whole = jnp.minimum(i, limit // block)
        last = jnp.minimum(i + 1, (limit + block - 1) // block)
        state = lax.fori_loop(0, whole, functools.partial(step, False), start)
        state = lax.fori_loop(whole, last, functools.partial(step, True), state)
        both = jnp.concatenate([acc / tot for _, tot, acc in state], axis=0)
        place = pl.multiple_of(lax.rem(me_c - i + n, n) * block, block)
        mixed[pl.ds(place, block), :] = both.T.astype(BF)
        for h in range(2):
            top, tot, _ = state[h]
            logs[h : h + 1, pl.ds(at_q, block)] = top + jnp.log(tot)
        return 0

    lax.fori_loop(0, n, one, 0)


def self_backward_kernel(
    n, block, info, qkv, mixed, grad, logs, grads, q_s, k_s, v_s, kt_s, d_s, delta_s, dq_s
):
    limit, me_c, me_t = info[0], info[1], info[2]
    half = block // 2
    for c in range(n):
        for t in range(2):
            place = lax.rem(me_c - c + n, n) * block + (me_t ^ t) * half
            place = pl.multiple_of(place, half)
            to = slice(c * block + t * half, c * block + t * half + half)
            rows = qkv[pl.ds(place, half), :]
            q_s[to, :] = rows[:, :PAIR] * jnp.asarray(HEAD_DIM**-0.5, BF)
            keys = rows[:, PAIR : 2 * PAIR]
            values = rows[:, 2 * PAIR :]
            for h in range(2):
                k_s[h, to, :] = jnp.where(lanes_of(h, keys.shape), keys, jnp.zeros_like(keys))
                v_s[h, to, :] = jnp.where(lanes_of(h, keys.shape), values, jnp.zeros_like(keys))
            kt_s[:, to] = keys.astype(F32).T.astype(BF)
            at = pl.multiple_of(lax.rem(me_c - c + n, n) * block + t * half, half)
            dout = grad[pl.ds(at, half), :]
            d_s[to, :] = dout
            both = (dout.astype(F32) * mixed[pl.ds(at, half), :].astype(F32)).T
            for h in range(2):
                delta_s[h : h + 1, to] = jnp.sum(
                    both[h * HEAD_DIM : (h + 1) * HEAD_DIM, :], axis=0, keepdims=True
                )
    dq_s[...] = jnp.zeros_like(dq_s)

    def one(j, _):
        at_k = pl.multiple_of(j * block, block)

        def step(masked, i, state):
            at_q = pl.multiple_of(i * block, block)
            query = q_s[pl.ds(at_q, block), :]
            dout = d_s[pl.ds(at_q, block), :]
            out = []
            for h in range(2):
                dk, dv = state[h]
                score = nt(k_s[h, pl.ds(at_k, block), :], query)
                if masked:
                    key_at = at_k + lax.broadcasted_iota(jnp.int32, score.shape, 0)
                    slot_at = at_q + lax.broadcasted_iota(jnp.int32, score.shape, 1)
                    score = jnp.where((key_at <= slot_at) & (key_at < limit), score, LOW)
                chance = jnp.exp(score - logs[h : h + 1, pl.ds(at_q, block)])
                slopes = nt(v_s[h, pl.ds(at_k, block), :], dout)
                bend = (chance * (slopes - delta_s[h : h + 1, pl.ds(at_q, block)])).astype(BF)
                dv = dv + nn(chance.astype(BF), dout)
                dk = dk + nn(bend, query)
                side = slice(h * HEAD_DIM, (h + 1) * HEAD_DIM)
                dq_s[side, pl.ds(at_q, block)] += nn(kt_s[side, pl.ds(at_k, block)], bend)
                out.append((dk, dv))
            return tuple(out)

        start = tuple(
            (jnp.zeros((block, PAIR), F32), jnp.zeros((block, PAIR), F32)) for _ in range(2)
        )
        end = jnp.where(j * block < limit, n, j)
        middle = jnp.where((j + 1) * block <= limit, jnp.minimum(j + 1, end), end)
        state = lax.fori_loop(j, middle, functools.partial(step, True), start)
        state = lax.fori_loop(middle, end, functools.partial(step, False), state)
        first_head = lanes_of(0, (block, PAIR))
        dk = jnp.where(first_head, state[0][0], state[1][0]).astype(BF)
        dv = jnp.where(first_head, state[0][1], state[1][1]).astype(BF)
        for t in range(2):
            place = lax.rem(me_c - j + n, n) * block + (me_t ^ t) * half
            place = pl.multiple_of(place, half)
            grads[pl.ds(place, half), PAIR : 2 * PAIR] = dk[t * half : (t + 1) * half, :]
            grads[pl.ds(place, half), 2 * PAIR :] = dv[t * half : (t + 1) * half, :]
        return 0

    lax.fori_loop(0, n, one, 0)
    for c in range(n):
        dq = (dq_s[:, c * block : (c + 1) * block] * HEAD_DIM**-0.5).T.astype(BF)
        for t in range(2):
            place = lax.rem(me_c - c + n, n) * block + (me_t ^ t) * half
            place = pl.multiple_of(place, half)
            grads[pl.ds(place, half), :PAIR] = dq[t * half : (t + 1) * half, :]


def cross_scores(limit, keys, query):
    score = nt(keys, query)
    key_at = lax.broadcasted_iota(jnp.int32, score.shape, 0)
    return jnp.where(key_at < limit, score, LOW)


def masked_pair(values, head):
    return jnp.where(lanes_of(head, values.shape), values, jnp.zeros_like(values))


def cross_forward_kernel(info, query_ref, kv, mixed, logs):
    limit = info[0]
    query = query_ref[...] * jnp.asarray(HEAD_DIM**-0.5, BF)
    keys = kv[0, :, :PAIR]
    values = kv[0, :, PAIR:].astype(F32).T.astype(BF)
    outs = []
    for h in range(2):
        score = cross_scores(limit, masked_pair(keys, h), query)
        top = jnp.max(score, axis=0, keepdims=True)
        chance = jnp.exp(score - top)
        tot = jnp.sum(chance, axis=0, keepdims=True)
        outs.append(nn(values[h * HEAD_DIM : (h + 1) * HEAD_DIM, :], chance.astype(BF)) / tot)
        logs[0, h : h + 1, :] = top + jnp.log(tot)
    mixed[...] = jnp.concatenate(outs, axis=0).T.astype(BF)


def cross_backward_kernel(info, query_ref, kv, mixed, grad, logs, dq_ref, dkv):
    limit = info[0]
    query = query_ref[...] * jnp.asarray(HEAD_DIM**-0.5, BF)
    keys = kv[0, :, :PAIR]
    values = kv[0, :, PAIR:]
    keys_t = keys.astype(F32).T.astype(BF)
    dout = grad[...]
    both = (dout.astype(F32) * mixed[...].astype(F32)).T
    dqs, dks, dvs = [], [], []
    for h in range(2):
        side = slice(h * HEAD_DIM, (h + 1) * HEAD_DIM)
        delta = jnp.sum(both[side, :], axis=0, keepdims=True)
        score = cross_scores(limit, masked_pair(keys, h), query)
        chance = jnp.exp(score - logs[0, h : h + 1, :])
        slopes = nt(masked_pair(values, h), dout)
        bend = (chance * (slopes - delta)).astype(BF)
        dvs.append(nn(chance.astype(BF), dout))
        dks.append(nn(bend, query))
        dqs.append(nn(keys_t[side, :], bend))
    dq_ref[...] = (jnp.concatenate(dqs, axis=0) * HEAD_DIM**-0.5).T.astype(BF)
    first_head = lanes_of(0, dks[0].shape)
    dkv[0, :, :PAIR] = jnp.where(first_head, dks[0], dks[1]).astype(BF)
    dkv[0, :, PAIR:] = jnp.where(first_head, dvs[0], dvs[1]).astype(BF)


VMEM_LIMIT = 48 * 1024 * 1024


def vmem_spec():
    return pl.BlockSpec(memory_space=pltpu.VMEM)


def smem_spec():
    return pl.BlockSpec(memory_space=pltpu.SMEM)


def self_forward(info, qkv, n):
    slots = qkv.shape[0]
    block = slots // n
    pairs = slots * slots
    return pl.pallas_call(
        functools.partial(self_forward_kernel, n, block),
        out_shape=(
            jax.ShapeDtypeStruct((slots, PAIR), BF),
            jax.ShapeDtypeStruct((2, slots), F32),
        ),
        in_specs=[smem_spec(), vmem_spec()],
        out_specs=(vmem_spec(), vmem_spec()),
        scratch_shapes=[
            pltpu.VMEM((slots, PAIR), BF),
            pltpu.VMEM((2, slots, PAIR), BF),
            pltpu.VMEM((PAIR, slots), BF),
        ],
        compiler_params=pltpu.CompilerParams(vmem_limit_bytes=VMEM_LIMIT),
        cost_estimate=pl.CostEstimate(
            flops=pairs * PAIR * 4, transcendentals=pairs, bytes_accessed=slots * PAIR * 8
        ),
        name="self_forward",
    )(info, qkv)


def self_backward(info, qkv, mixed, grad, logs, n):
    slots = qkv.shape[0]
    block = slots // n
    pairs = slots * slots
    return pl.pallas_call(
        functools.partial(self_backward_kernel, n, block),
        out_shape=jax.ShapeDtypeStruct((slots, 3 * PAIR), BF),
        in_specs=[smem_spec()] + [vmem_spec()] * 4,
        out_specs=vmem_spec(),
        scratch_shapes=[
            pltpu.VMEM((slots, PAIR), BF),
            pltpu.VMEM((2, slots, PAIR), BF),
            pltpu.VMEM((2, slots, PAIR), BF),
            pltpu.VMEM((PAIR, slots), BF),
            pltpu.VMEM((slots, PAIR), BF),
            pltpu.VMEM((2, slots), F32),
            pltpu.VMEM((PAIR, slots), F32),
        ],
        compiler_params=pltpu.CompilerParams(vmem_limit_bytes=VMEM_LIMIT),
        cost_estimate=pl.CostEstimate(
            flops=pairs * PAIR * 10, transcendentals=pairs, bytes_accessed=slots * PAIR * 20
        ),
        name="self_backward",
    )(info, qkv, mixed, grad, logs)


def cross_forward(info, query, kv, n):
    rows, keys = query.shape[0], kv.shape[1]
    pairs = rows * keys * n
    grid_spec = pltpu.PrefetchScalarGridSpec(
        num_scalar_prefetch=1,
        grid=(n,),
        in_specs=[
            pl.BlockSpec((rows, PAIR), lambda j, info: (0, j)),
            pl.BlockSpec((1, keys, 2 * PAIR), lambda j, info: (lax.rem(info[1] - j + n, n), 0, 0)),
        ],
        out_specs=[
            pl.BlockSpec((rows, PAIR), lambda j, info: (0, j)),
            pl.BlockSpec((1, 2, rows), lambda j, info: (j, 0, 0)),
        ],
    )
    return pl.pallas_call(
        cross_forward_kernel,
        grid_spec=grid_spec,
        out_shape=(
            jax.ShapeDtypeStruct((rows, PAIR * n), BF),
            jax.ShapeDtypeStruct((n, 2, rows), F32),
        ),
        compiler_params=pltpu.CompilerParams(vmem_limit_bytes=VMEM_LIMIT),
        cost_estimate=pl.CostEstimate(
            flops=pairs * PAIR * 8, transcendentals=2 * pairs, bytes_accessed=rows * PAIR * n * 6
        ),
        name="cross_forward",
    )(info, query, kv)


def cross_backward(info, query, kv, mixed, grad, logs, n):
    rows, keys = query.shape[0], kv.shape[1]
    pairs = rows * keys * n
    col = pl.BlockSpec((rows, PAIR), lambda j, info: (0, j))
    grid_spec = pltpu.PrefetchScalarGridSpec(
        num_scalar_prefetch=1,
        grid=(n,),
        in_specs=[
            col,
            pl.BlockSpec((1, keys, 2 * PAIR), lambda j, info: (lax.rem(info[1] - j + n, n), 0, 0)),
            col,
            col,
            pl.BlockSpec((1, 2, rows), lambda j, info: (j, 0, 0)),
        ],
        out_specs=[
            col,
            pl.BlockSpec((1, keys, 2 * PAIR), lambda j, info: (lax.rem(j - info[1] + n, n), 0, 0)),
        ],
    )
    return pl.pallas_call(
        cross_backward_kernel,
        grid_spec=grid_spec,
        out_shape=(
            jax.ShapeDtypeStruct((rows, PAIR * n), BF),
            jax.ShapeDtypeStruct((n, keys, 2 * PAIR), BF),
        ),
        compiler_params=pltpu.CompilerParams(vmem_limit_bytes=VMEM_LIMIT),
        cost_estimate=pl.CostEstimate(
            flops=pairs * PAIR * 20, transcendentals=2 * pairs, bytes_accessed=rows * PAIR * n * 10
        ),
        name="cross_backward",
    )(info, query, kv, mixed, grad, logs)


def tp_total(partial):
    mine = partial.astype(BF)
    return mine.astype(F32) + swap(mine).astype(F32)


def tp_join(mine):
    me = lax.axis_index("tp")
    other = swap(mine)
    return jnp.concatenate(
        [jnp.where(me == 0, mine, other), jnp.where(me == 0, other, mine)], axis=0
    )


def body(
    inputs,
    encoder_states,
    seq_lengths,
    enc_lengths,
    cotangent,
    norm_gains,
    norm_biases,
    w_query,
    w_key,
    w_value,
    w_out,
    w_cross_query,
    w_cross_key,
    w_cross_value,
    w_cross_out,
    w_inner,
    w_outer,
):
    n = lax.axis_size("ctx")
    me_c, me_t = lax.axis_index("ctx"), lax.axis_index("tp")
    rows, width = inputs.shape[1], inputs.shape[2]
    half = rows // 2
    wide = w_query.shape[1]
    shard = w_query.shape[0]
    seq_limit, enc_limit = seq_lengths[0], enc_lengths[0]
    self_info = jnp.stack([seq_limit, me_c, me_t]).astype(jnp.int32)
    cross_info = jnp.stack([enc_limit, me_c, me_t]).astype(jnp.int32)

    params = jnp.concatenate([norm_gains, norm_biases], axis=0)
    params = jnp.concatenate(in_order(gather_direct(params, "ctx"), "ctx"), axis=1)
    params = jnp.concatenate(in_order(gather_direct(params, "fsdp"), "fsdp"), axis=1)
    params = params.astype(F32)
    gains, biases = params[:4], params[4:]

    five = jnp.stack([w_query, w_key, w_value, w_cross_key, w_cross_value], axis=1)
    five = five.reshape(shard, 5, n, PAIR).transpose(2, 0, 1, 3).reshape(n, shard, 5 * PAIR)
    five = jnp.concatenate(in_order(exchange_direct(five, "ctx"), "ctx"), axis=0)
    five = jnp.concatenate(in_order(gather_direct(five, "fsdp"), "fsdp"), axis=0)
    w_qkv, w_ckv = five[:, : 3 * PAIR], five[:, 3 * PAIR :]

    hidden_x = inputs[0].astype(F32)
    normed_a, scale_a = norm_parts(hidden_x)
    attn_in = (normed_a * gains[0] + biases[0]).astype(BF)
    own = lax.dynamic_slice_in_dim(attn_in, me_t * half, half, 0)
    rest = lax.dynamic_slice_in_dim(attn_in, (1 - me_t) * half, half, 0)
    came = gather_line(own, "ctx")[1:]
    came_other = swap(jnp.concatenate(came, axis=0))
    blocks = [own, rest]
    for s in range(n - 1):
        blocks += [came[s], came_other[s * half : (s + 1) * half]]
    attn_all = jnp.concatenate(blocks, axis=0)

    enc_half = encoder_states.shape[1] // 2
    enc_own = lax.dynamic_slice_in_dim(encoder_states[0], me_t * enc_half, enc_half, 0)
    enc_came = jnp.stack(in_order(gather_direct(enc_own, "ctx"), "ctx"), axis=0)
    enc_came_other = swap(enc_came)
    enc_all = jnp.stack(
        [
            jnp.where(me_t == 0, enc_came, enc_came_other),
            jnp.where(me_t == 0, enc_came_other, enc_came),
        ],
        axis=1,
    ).reshape(-1, width)

    w_out_t = fetch_rows(w_out.T, False)
    w_cq_co = fetch_rows(jnp.concatenate([w_cross_query, w_cross_out.T], axis=1), True)
    w_cq, w_co_t = w_cq_co[:, :wide], w_cq_co[:, wide:]
    w_in = fetch_rows(w_inner, True)
    w_outer_t = fetch_rows(w_outer.T, False)

    qkv = nn(attn_all, w_qkv).astype(BF)
    mixed, logs = self_forward(self_info, qkv, n)
    pieces = [mixed[:rows]] + [
        shift(mixed[s * rows : (s + 1) * rows], "ctx", -s) for s in range(1, n)
    ]
    attn_flat = jnp.concatenate(in_order([pieces[(n - s) % n] for s in range(n)], "ctx"), axis=1)
    first = hidden_x + tp_total(nt(attn_flat, w_out_t))

    ckv_own = nn(enc_all, w_ckv).astype(BF)
    ckv = jnp.stack(gather_direct(ckv_own, "ctx"), axis=0)
    normed_c, scale_c = norm_parts(first)
    cross_in = (normed_c * gains[1] + biases[1]).astype(BF)
    cross_query = nn(cross_in, w_cq).astype(BF)
    cross_flat, cross_logs = cross_forward(cross_info, cross_query, ckv, n)
    second = first + tp_total(nt(cross_flat, w_co_t))

    normed_f, scale_f = norm_parts(second)
    ffn_in = (normed_f * gains[2] + biases[2]).astype(BF)
    inner = nn(ffn_in, w_in)
    gated, gate_pullback = jax.vjp(smooth_gate, inner)
    active = gated.astype(BF)
    third = second + tp_total(nt(active, w_outer_t))

    positions = me_c * rows + lax.iota(jnp.int32, rows)
    valid = (positions < seq_limit).astype(F32)[:, None]
    normed_y, scale_y = norm_parts(third)
    output = (normed_y * gains[3] + biases[3]) * valid

    grad_y = cotangent[0].astype(F32) * valid
    grad_third, gain_y, bias_y = norm_back(grad_y, normed_y, scale_y, gains[3])
    g3 = grad_third.astype(BF)
    grad_active = gate_pullback(nn(g3, w_outer_t))[0].astype(BF)
    grad_outer = return_rows(tn(g3, active).astype(BF), True).T
    grad_inner = return_rows(tn(ffn_in, grad_active).astype(BF), False)
    grad_ffn_in = tp_total(nt(grad_active, w_in))
    part_f, gain_f, bias_f = norm_back(grad_ffn_in, normed_f, scale_f, gains[2])
    grad_second = grad_third + part_f
    g2 = grad_second.astype(BF)

    grad_cross = nn(g2, w_co_t).astype(BF)
    grad_cq, dkv = cross_backward(
        cross_info, cross_query, ckv, cross_flat, grad_cross, cross_logs, n
    )
    grad_ckv = total([dkv[0]] + [shift(dkv[s], "ctx", s) for s in range(1, n)]).astype(BF)
    pair = jnp.concatenate(
        [tn(cross_in, grad_cq).astype(BF), tn(g2, cross_flat).astype(BF)], axis=1
    )
    pair = return_rows(pair, True)
    grad_w_cq, grad_w_co = pair[:, :wide], pair[:, wide:].T
    grad_cross_in = tp_total(nt(grad_cq, w_cq))
    part_c, gain_c, bias_c = norm_back(grad_cross_in, normed_c, scale_c, gains[1])
    grad_first = grad_second + part_c
    g1 = grad_first.astype(BF)

    enc_part = tp_total(nt(grad_ckv, w_ckv)).astype(BF).reshape(n, 2, enc_half, width)
    enc_part = lax.dynamic_index_in_dim(enc_part, me_t, 1, keepdims=False)
    grad_encoder = tp_join(total(exchange_direct(enc_part, "ctx")))

    grad_w_out = return_rows(tn(g1, attn_flat).astype(BF), False).T
    grad_attn = nn(g1, w_out_t).astype(BF)
    grad_attn = grad_attn.reshape(rows, n, PAIR).transpose(1, 0, 2)
    dmixed = jnp.concatenate(exchange_direct(grad_attn, "ctx"), axis=0)
    dqkv = self_backward(self_info, qkv, mixed, dmixed, logs, n)
    part = nt(dqkv, w_qkv).astype(BF).reshape(n, 2, half, width)
    part = (part[:, 0].astype(F32) + swap(part[:, 1]).astype(F32)).astype(BF)
    grad_attn_in = total([part[0]] + [shift(part[s], "ctx", -s) for s in range(1, n)])

    dfive = jnp.concatenate([tn(attn_all, dqkv), tn(enc_all, grad_ckv)], axis=1).astype(BF)
    f = lax.axis_size("fsdp")
    dfive = total(exchange_direct(dfive.reshape(f, n * shard, 5 * PAIR), "fsdp")).astype(BF)
    dfive = in_order(exchange_direct(dfive.reshape(n, shard, 5 * PAIR), "ctx"), "ctx")
    dfive = jnp.stack(dfive, axis=0).reshape(n, shard, 5, PAIR).transpose(2, 1, 0, 3)
    dfive = dfive.reshape(5, shard, wide).astype(F32)

    def mine(values):
        return lax.dynamic_slice_in_dim(values, me_t * half, half, 0)

    part_a, gain_a, bias_a = norm_back(grad_attn_in, mine(normed_a), mine(scale_a), gains[0])
    grad_inputs = tp_join(mine(grad_first) + part_a)
    pair_a = jnp.stack([gain_a, bias_a])
    pair_a = pair_a + swap(pair_a)
    norm_grads = jnp.stack(
        [pair_a[0], gain_c, gain_f, gain_y, pair_a[1], bias_c, bias_f, bias_y]
    )
    norm_grads = norm_grads.reshape(8, f, n * shard).transpose(1, 0, 2)
    norm_grads = total(exchange_direct(norm_grads, "fsdp"))
    norm_grads = norm_grads.reshape(8, n, shard).transpose(1, 0, 2)
    norm_grads = total(exchange_direct(norm_grads, "ctx"))

    return (
        output[None],
        grad_inputs[None],
        grad_encoder[None],
        norm_grads[:4],
        norm_grads[4:],
        dfive[0],
        dfive[1],
        dfive[2],
        grad_w_out,
        grad_w_cq,
        dfive[3],
        dfive[4],
        grad_w_co,
        grad_inner,
        grad_outer,
    )


def solution(mesh):
    tokens = P("fsdp", "ctx", None)
    norms = P(None, ("fsdp", "ctx"))
    by_rows = P(("fsdp", "ctx"), "tp")
    by_cols = P("tp", ("fsdp", "ctx"))
    return jax.shard_map(
        body,
        mesh=mesh,
        in_specs=(
            tokens,
            tokens,
            P("fsdp"),
            P("fsdp"),
            tokens,
            norms,
            norms,
            by_rows,
            by_rows,
            by_rows,
            by_cols,
            by_rows,
            by_rows,
            by_rows,
            by_cols,
            by_rows,
            by_cols,
        ),
        out_specs=(
            tokens,
            tokens,
            tokens,
            norms,
            norms,
            by_rows,
            by_rows,
            by_rows,
            by_cols,
            by_rows,
            by_rows,
            by_rows,
            by_cols,
            by_rows,
            by_cols,
        ),
        check_vma=False,
    )
```

```python
import functools

import jax
import jax.numpy as jnp
from jax import lax
from jax.experimental import pallas as pl
from jax.experimental.pallas import tpu as pltpu
from jax.sharding import PartitionSpec as P

HEAD_DIM = 64
PAIR = 2 * HEAD_DIM
EPS = 1e-05
GELU_A = 0.7978845608028654
GELU_B = 0.044715
BF = jnp.bfloat16
F32 = jnp.float32
LOW = -1e30


def nn(left, right):
    return jnp.dot(left, right, preferred_element_type=F32)


def tn(left, right):
    return lax.dot_general(left, right, (((0,), (0,)), ((), ())), preferred_element_type=F32)


def nt(left, right):
    return lax.dot_general(left, right, (((1,), (1,)), ((), ())), preferred_element_type=F32)


def smooth_gate(values):
    return 0.5 * values * (1.0 + jnp.tanh(GELU_A * (values + GELU_B * values * values * values)))


def norm_parts(values):
    mean = jnp.mean(values, axis=-1, keepdims=True)
    centred = values - mean
    scale = lax.rsqrt(jnp.mean(centred * centred, axis=-1, keepdims=True) + EPS)
    return (centred * scale, scale)


def norm_back(grad_result, normed, scale, gain):
    grad_normed = grad_result * gain
    grad_input = scale * (
        grad_normed
        - jnp.mean(grad_normed, axis=-1, keepdims=True)
        - normed * jnp.mean(grad_normed * normed, axis=-1, keepdims=True)
    )
    return (grad_input, jnp.sum(grad_result * normed, axis=0), jnp.sum(grad_result, axis=0))


def flip(value, axis, mask):
    n = lax.axis_size(axis)
    return lax.ppermute(value, axis, [(i, i ^ mask) for i in range(n)])


def swap(value):
    return flip(value, "tp", 1)


def tie(value, *others):
    return lax.optimization_barrier((value,) + others)[0]


def bits_of(axis, low_first):
    n = lax.axis_size(axis)
    order = list(range(n.bit_length() - 1))
    return order if low_first else order[::-1]


def bit_at(axis, bit):
    return (lax.axis_index(axis) >> bit) & 1


class Gathering:
    def __init__(self, value, axis, low_first):
        self.axis, self.order = axis, bits_of(axis, low_first)
        self.blocks, self.came = {0: value}, None

    def start(self, *others):
        bit = self.order[0]
        keys = sorted(self.blocks)
        sent = [self.blocks[k] for k in keys]
        sent = sent[0] if len(sent) == 1 else jnp.concatenate(sent, axis=0)
        if others:
            sent = tie(sent, *others)
        self.came = flip(sent, self.axis, 1 << bit)
        return self.came

    def join(self):
        bit = self.order.pop(0)
        mine = bit_at(self.axis, bit)
        keys = sorted(self.blocks)
        rows = self.came.shape[0] // len(keys)
        blocks = {}
        for place, k in enumerate(keys):
            held, other = self.blocks[k], self.came[place * rows : (place + 1) * rows]
            blocks[k] = jnp.where(mine == 0, held, other)
            blocks[k | 1 << bit] = jnp.where(mine == 0, other, held)
        self.blocks = blocks

    def step(self, *others):
        self.join()
        return self.start(*others)

    def end(self):
        self.join()
        return jnp.concatenate([self.blocks[k] for k in sorted(self.blocks)], axis=0)


class Doubling:
    def __init__(self, value, *others):
        cut = value.shape[0] // 2
        self.parts = [
            Gathering(value[:cut], "fsdp", True),
            Gathering(value[cut:], "fsdp", False),
        ]
        self.start(*others)

    def start(self, *others):
        self.came = [g.start(*others) for g in self.parts]

    def after(self, *others):
        for g in self.parts:
            g.came = tie(g.came, *others)

    def step(self, *others):
        self.after(*others)
        for g in self.parts:
            g.join()
        self.start()

    def end(self, *others):
        self.after(*others)
        for g in self.parts:
            g.join()
        keys = sorted(self.parts[0].blocks)
        return jnp.concatenate([g.blocks[k] for k in keys for g in self.parts], axis=0)


def gather_offsets(value, axis, low_first, seen=None, late=None):
    found = {0: value}
    order = bits_of(axis, low_first)
    for bit in order:
        keys = sorted(found)
        sent = [found[k] for k in keys]
        sent = sent[0] if len(sent) == 1 else jnp.concatenate(sent, axis=0)
        if late is not None and bit == order[-1]:
            sent = tie(sent, late)
        came = flip(sent, axis, 1 << bit)
        rows = value.shape[0]
        if seen is not None:
            seen.append(came)
        for place, k in enumerate(keys):
            found[k ^ (1 << bit)] = came[place * rows : (place + 1) * rows]
    return [found[k] for k in range(lax.axis_size(axis))]


def natural(pieces, axis, dim=0):
    n = len(pieces)
    me = lax.axis_index(axis)
    return jnp.concatenate(
        [lax.select_n(me, *[pieces[j ^ m] for m in range(n)]) for j in range(n)], axis=dim
    )


def gather_direct(value, axis):
    n = lax.axis_size(axis)
    return natural([value] + [flip(value, axis, k) for k in range(1, n)], axis)


def exchange_direct(blocks, axis):
    me = lax.axis_index(axis)
    out = [lax.dynamic_index_in_dim(blocks, me ^ k, 0, keepdims=False) for k in range(len(blocks))]
    return out[:1] + [flip(out[k], axis, k) for k in range(1, len(blocks))]


def half_rows(held, index, bit, bits):
    rows = held.shape[0] // 2
    if bits[0] == bit:
        return lax.dynamic_slice_in_dim(held, index * rows, rows, 0)
    before = 1 << bits.index(bit)
    view = held.reshape(before, 2, rows // before, held.shape[1])
    return lax.dynamic_slice_in_dim(view, index, 1, 1).reshape(rows, held.shape[1])


class Scattering:
    def __init__(self, legs, away, held, bits, first):
        self.legs = [(axis, bit) for axis, low in legs for bit in bits_of(axis, low)][1:]
        self.bits = [b for b in bits if b != first]
        self.held, self.axis = held, legs[0][0]
        self.came = flip(away, legs[0][0], 1 << first)

    def step(self):
        axis, bit = self.legs.pop(0)
        if axis != self.axis:
            self.axis, self.bits = axis, bits_of(axis, False)
        mine = bit_at(axis, bit)

        def part(index):
            held = half_rows(self.held, index, bit, self.bits).astype(F32)
            return (held + half_rows(self.came, index, bit, self.bits).astype(F32)).astype(BF)

        away, held = part(1 - mine), part(mine)
        self.bits = [b for b in self.bits if b != bit]
        self.came, self.held = flip(away, axis, 1 << bit), held

    def end(self):
        return self.held.astype(F32) + self.came.astype(F32)


def scatter_value(value, legs):
    axis, low = legs[0]
    bit, bits = bits_of(axis, low)[0], bits_of(axis, False)
    mine = bit_at(axis, bit)
    return Scattering(
        legs, half_rows(value, 1 - mine, bit, bits), half_rows(value, mine, bit, bits), bits, bit
    )


class Halving:
    def __init__(self, pairs, *others):
        n = lax.axis_size("fsdp")
        bits = bits_of("fsdp", False)
        firsts = [bits_of("fsdp", True)[0], bits_of("fsdp", False)[0]]

        def product(flipped):
            out = []
            for left, right in pairs:
                rows = left.shape[1] // n
                cut = rows // 2
                chosen = []
                for place, bit in enumerate(firsts):
                    index = bit_at("fsdp", bit) ^ flipped
                    sides = [
                        jnp.concatenate(
                            [
                                left[:, b * rows + place * cut : b * rows + (place + 1) * cut]
                                for b in range(n)
                                if b >> bit & 1 == v
                            ],
                            axis=1,
                        )
                        for v in range(2)
                    ]
                    chosen.append(jnp.where(index == 0, sides[0], sides[1]))
                out.append(tn(jnp.concatenate(chosen, axis=1), right).astype(BF))
            return out[0] if len(out) == 1 else jnp.concatenate(out, axis=1)

        away, keep = product(1), product(0)
        if others:
            away = tie(away, *others)
        cut = away.shape[0] // 2
        self.parts = [
            Scattering(
                [("fsdp", low)],
                away[place * cut : (place + 1) * cut],
                keep[place * cut : (place + 1) * cut],
                bits,
                firsts[place],
            )
            for place, low in enumerate((True, False))
        ]
        self.ctx = False

    def after(self, *others):
        for p in self.parts:
            p.came = tie(p.came, *others)

    def flight(self):
        return [p.came for p in self.parts]

    def held(self):
        return [p.held for p in self.parts]

    def over(self):
        return not self.parts[0].legs

    def step(self, *others):
        if others:
            self.after(*others)
        if not self.over():
            while not self.over():
                for p in self.parts:
                    p.step()
        elif not self.ctx:
            value = jnp.concatenate([p.end().astype(BF) for p in self.parts], axis=0)
            self.parts, self.ctx = [scatter_value(value, [("ctx", True)])], True

    def end(self, *others):
        if others:
            self.after(*others)
        return self.parts[0].end()


def scatter_offsets(pieces, axis, seen=None):
    n = lax.axis_size(axis)
    held = dict(enumerate(pieces))
    for bit in bits_of(axis, True):
        last = n == 2 << bit
        away = [held[k].astype(BF) for k in sorted(held) if k >> bit & 1]
        came = flip(away[0] if len(away) == 1 else jnp.concatenate(away, axis=0), axis, 1 << bit)
        rows = pieces[0].shape[0]
        if seen is not None:
            seen.append(came)
        held = {k: v for k, v in held.items() if not k >> bit & 1}
        for place, k in enumerate(sorted(held)):
            held[k] = held[k].astype(F32) + came[place * rows : (place + 1) * rows].astype(F32)
            if not last:
                held[k] = held[k].astype(BF)
    return held[0]


def lanes_of(head, shape):
    lane = lax.broadcasted_iota(jnp.int32, shape, len(shape) - 1)
    return (lane // HEAD_DIM) == head


def project_kernel(x_ref, scales, weight, kept, out):
    x = x_ref[...].astype(F32)
    width = x.shape[1]
    centred = x - jnp.sum(x, axis=1, keepdims=True) * (1.0 / width)
    spread = jnp.sum(centred * centred, axis=1, keepdims=True) * (1.0 / width)
    normed = centred * lax.rsqrt(spread + EPS)
    attn_in = (normed * scales[0:1, :] + scales[1:2, :]).astype(BF)
    kept[:, :width] = attn_in
    kept[:, width:] = normed.astype(BF)
    out[...] = nn(attn_in, weight[...]).astype(BF)


def project(x_all, scales, weight):
    slots, width = x_all.shape
    cols = weight.shape[1]
    block = min(256, slots)
    return pl.pallas_call(
        project_kernel,
        grid=(slots // block,),
        in_specs=[
            pl.BlockSpec((block, width), lambda i: (i, 0)),
            pl.BlockSpec((2, width), lambda i: (0, 0)),
            pl.BlockSpec((width, cols), lambda i: (0, 0)),
        ],
        out_specs=[
            pl.BlockSpec((block, 2 * width), lambda i: (i, 0)),
            pl.BlockSpec((block, cols), lambda i: (i, 0)),
        ],
        out_shape=[
            jax.ShapeDtypeStruct((slots, 2 * width), BF),
            jax.ShapeDtypeStruct((slots, cols), BF),
        ],
        compiler_params=pltpu.CompilerParams(vmem_limit_bytes=VMEM_LIMIT),
        cost_estimate=pl.CostEstimate(
            flops=slots * width * cols * 4, transcendentals=0, bytes_accessed=slots * width * 8
        ),
        name="project",
    )(x_all, scales, weight)


def self_forward_kernel(n, block, info, qkv, mixed, logs, q_s, k_s, v_s):
    limit, me_c, me_t = info[0], info[1], info[2]
    half = block // 2
    for c in range(n):
        for t in range(2):
            place = (me_c ^ c) * block + (me_t ^ t) * half
            place = pl.multiple_of(place, half)
            to = slice(c * block + t * half, c * block + t * half + half)
            rows = qkv[pl.ds(place, half), :]
            q_s[to, :] = rows[:, :PAIR] * jnp.asarray(HEAD_DIM**-0.5, BF)
            keys = rows[:, PAIR : 2 * PAIR]
            for h in range(2):
                k_s[h, to, :] = jnp.where(lanes_of(h, keys.shape), keys, jnp.zeros_like(keys))
            v_s[:, to] = rows[:, 2 * PAIR :].astype(F32).T.astype(BF)

    def one(i, _):
        at_q = pl.multiple_of(i * block, block)
        query = q_s[pl.ds(at_q, block), :]

        def step(masked, j, state):
            at_k = pl.multiple_of(j * block, block)
            out = []
            for h in range(2):
                top, tot, acc = state[h]
                score = nt(k_s[h, pl.ds(at_k, block), :], query)
                if masked:
                    key_at = at_k + lax.broadcasted_iota(jnp.int32, score.shape, 0)
                    slot_at = at_q + lax.broadcasted_iota(jnp.int32, score.shape, 1)
                    score = jnp.where((key_at <= slot_at) & (key_at < limit), score, LOW)
                new_top = jnp.maximum(top, jnp.max(score, axis=0, keepdims=True))
                fade = jnp.exp(top - new_top)
                chance = jnp.exp(score - new_top)
                tot = tot * fade + jnp.sum(chance, axis=0, keepdims=True)
                part = nn(
                    v_s[h * HEAD_DIM : (h + 1) * HEAD_DIM, pl.ds(at_k, block)], chance.astype(BF)
                )
                out.append((new_top, tot, acc * fade + part))
            return tuple(out)

        start = tuple(
            (
                jnp.full((1, block), LOW, F32),
                jnp.zeros((1, block), F32),
                jnp.zeros((HEAD_DIM, block), F32),
            )
            for _ in range(2)
        )
        whole = jnp.minimum(i, limit // block)
        last = jnp.minimum(i + 1, (limit + block - 1) // block)
        state = lax.fori_loop(0, whole, functools.partial(step, False), start)
        state = lax.fori_loop(whole, last, functools.partial(step, True), state)
        both = jnp.concatenate([acc / tot for _, tot, acc in state], axis=0)
        place = pl.multiple_of((me_c ^ i) * block, block)
        mixed[pl.ds(place, block), :] = both.T.astype(BF)
        for h in range(2):
            top, tot, _ = state[h]
            logs[h : h + 1, pl.ds(at_q, block)] = top + jnp.log(tot)
        return 0

    lax.fori_loop(0, n, one, 0)


def self_backward_kernel(
    n, block, info, qkv, mixed, grad, logs, grads, q_s, k_s, v_s, kt_s, d_s, delta_s, dq_s
):
    limit, me_c, me_t = info[0], info[1], info[2]
    half = block // 2
    for c in range(n):
        for t in range(2):
            place = (me_c ^ c) * block + (me_t ^ t) * half
            place = pl.multiple_of(place, half)
            to = slice(c * block + t * half, c * block + t * half + half)
            rows = qkv[pl.ds(place, half), :]
            q_s[to, :] = rows[:, :PAIR] * jnp.asarray(HEAD_DIM**-0.5, BF)
            keys = rows[:, PAIR : 2 * PAIR]
            values = rows[:, 2 * PAIR :]
            for h in range(2):
                k_s[h, to, :] = jnp.where(lanes_of(h, keys.shape), keys, jnp.zeros_like(keys))
                v_s[h, to, :] = jnp.where(lanes_of(h, keys.shape), values, jnp.zeros_like(keys))
            kt_s[:, to] = keys.astype(F32).T.astype(BF)
            at = pl.multiple_of((me_c ^ c) * block + t * half, half)
            dout = grad[pl.ds(at, half), :]
            d_s[to, :] = dout
            both = (dout.astype(F32) * mixed[pl.ds(at, half), :].astype(F32)).T
            for h in range(2):
                delta_s[h : h + 1, to] = jnp.sum(
                    both[h * HEAD_DIM : (h + 1) * HEAD_DIM, :], axis=0, keepdims=True
                )
    dq_s[...] = jnp.zeros_like(dq_s)

    def one(j, _):
        at_k = pl.multiple_of(j * block, block)

        def step(masked, i, state):
            at_q = pl.multiple_of(i * block, block)
            query = q_s[pl.ds(at_q, block), :]
            dout = d_s[pl.ds(at_q, block), :]
            out = []
            for h in range(2):
                dk, dv = state[h]
                score = nt(k_s[h, pl.ds(at_k, block), :], query)
                if masked:
                    key_at = at_k + lax.broadcasted_iota(jnp.int32, score.shape, 0)
                    slot_at = at_q + lax.broadcasted_iota(jnp.int32, score.shape, 1)
                    score = jnp.where((key_at <= slot_at) & (key_at < limit), score, LOW)
                chance = jnp.exp(score - logs[h : h + 1, pl.ds(at_q, block)])
                slopes = nt(v_s[h, pl.ds(at_k, block), :], dout)
                bend = (chance * (slopes - delta_s[h : h + 1, pl.ds(at_q, block)])).astype(BF)
                dv = dv + nn(chance.astype(BF), dout)
                dk = dk + nn(bend, query)
                side = slice(h * HEAD_DIM, (h + 1) * HEAD_DIM)
                dq_s[side, pl.ds(at_q, block)] += nn(kt_s[side, pl.ds(at_k, block)], bend)
                out.append((dk, dv))
            return tuple(out)

        start = tuple(
            (jnp.zeros((block, PAIR), F32), jnp.zeros((block, PAIR), F32)) for _ in range(2)
        )
        end = jnp.where(j * block < limit, n, j)
        middle = jnp.where((j + 1) * block <= limit, jnp.minimum(j + 1, end), end)
        state = lax.fori_loop(j, middle, functools.partial(step, True), start)
        state = lax.fori_loop(middle, end, functools.partial(step, False), state)
        first_head = lanes_of(0, (block, PAIR))
        dk = jnp.where(first_head, state[0][0], state[1][0]).astype(BF)
        dv = jnp.where(first_head, state[0][1], state[1][1]).astype(BF)
        for t in range(2):
            place = (me_c ^ j) * block + (me_t ^ t) * half
            place = pl.multiple_of(place, half)
            grads[pl.ds(place, half), PAIR : 2 * PAIR] = dk[t * half : (t + 1) * half, :]
            grads[pl.ds(place, half), 2 * PAIR :] = dv[t * half : (t + 1) * half, :]
        return 0

    lax.fori_loop(0, n, one, 0)
    for c in range(n):
        dq = (dq_s[:, c * block : (c + 1) * block] * HEAD_DIM**-0.5).T.astype(BF)
        for t in range(2):
            place = (me_c ^ c) * block + (me_t ^ t) * half
            place = pl.multiple_of(place, half)
            grads[pl.ds(place, half), :PAIR] = dq[t * half : (t + 1) * half, :]


def cross_scores(limit, keys, query):
    score = nt(keys, query)
    key_at = lax.broadcasted_iota(jnp.int32, score.shape, 0)
    return jnp.where(key_at < limit, score, LOW)


def masked_pair(values, head):
    return jnp.where(lanes_of(head, values.shape), values, jnp.zeros_like(values))


def cross_forward_kernel(info, query_ref, kv, mixed, logs):
    limit = info[0]
    query = query_ref[...] * jnp.asarray(HEAD_DIM**-0.5, BF)
    keys = kv[0, :, :PAIR]
    values = kv[0, :, PAIR:].astype(F32).T.astype(BF)
    outs = []
    for h in range(2):
        score = cross_scores(limit, masked_pair(keys, h), query)
        top = jnp.max(score, axis=0, keepdims=True)
        chance = jnp.exp(score - top)
        tot = jnp.sum(chance, axis=0, keepdims=True)
        outs.append(nn(values[h * HEAD_DIM : (h + 1) * HEAD_DIM, :], chance.astype(BF)) / tot)
        logs[0, h : h + 1, :] = top + jnp.log(tot)
    mixed[...] = jnp.concatenate(outs, axis=0).T.astype(BF)


def cross_backward_kernel(info, query_ref, kv, mixed, grad, logs, dq_ref, dkv):
    limit = info[0]
    query = query_ref[...] * jnp.asarray(HEAD_DIM**-0.5, BF)
    keys = kv[0, :, :PAIR]
    values = kv[0, :, PAIR:]
    keys_t = keys.astype(F32).T.astype(BF)
    dout = grad[...]
    both = (dout.astype(F32) * mixed[...].astype(F32)).T
    dqs, dks, dvs = [], [], []
    for h in range(2):
        side = slice(h * HEAD_DIM, (h + 1) * HEAD_DIM)
        delta = jnp.sum(both[side, :], axis=0, keepdims=True)
        score = cross_scores(limit, masked_pair(keys, h), query)
        chance = jnp.exp(score - logs[0, h : h + 1, :])
        slopes = nt(masked_pair(values, h), dout)
        bend = (chance * (slopes - delta)).astype(BF)
        dvs.append(nn(chance.astype(BF), dout))
        dks.append(nn(bend, query))
        dqs.append(nn(keys_t[side, :], bend))
    dq_ref[...] = (jnp.concatenate(dqs, axis=0) * HEAD_DIM**-0.5).T.astype(BF)
    first_head = lanes_of(0, dks[0].shape)
    dkv[0, :, :PAIR] = jnp.where(first_head, dks[0], dks[1]).astype(BF)
    dkv[0, :, PAIR:] = jnp.where(first_head, dvs[0], dvs[1]).astype(BF)


VMEM_LIMIT = 48 * 1024 * 1024


def vmem_spec():
    return pl.BlockSpec(memory_space=pltpu.VMEM)


def smem_spec():
    return pl.BlockSpec(memory_space=pltpu.SMEM)


def self_forward(info, qkv, n):
    slots = qkv.shape[0]
    block = slots // n
    pairs = slots * slots
    return pl.pallas_call(
        functools.partial(self_forward_kernel, n, block),
        out_shape=(
            jax.ShapeDtypeStruct((slots, PAIR), BF),
            jax.ShapeDtypeStruct((2, slots), F32),
        ),
        in_specs=[smem_spec(), vmem_spec()],
        out_specs=(vmem_spec(), vmem_spec()),
        scratch_shapes=[
            pltpu.VMEM((slots, PAIR), BF),
            pltpu.VMEM((2, slots, PAIR), BF),
            pltpu.VMEM((PAIR, slots), BF),
        ],
        compiler_params=pltpu.CompilerParams(vmem_limit_bytes=VMEM_LIMIT),
        cost_estimate=pl.CostEstimate(
            flops=pairs * PAIR * 4, transcendentals=pairs, bytes_accessed=slots * PAIR * 8
        ),
        name="self_forward",
    )(info, qkv)


def self_backward(info, qkv, mixed, grad, logs, n):
    slots = qkv.shape[0]
    block = slots // n
    pairs = slots * slots
    return pl.pallas_call(
        functools.partial(self_backward_kernel, n, block),
        out_shape=jax.ShapeDtypeStruct((slots, 3 * PAIR), BF),
        in_specs=[smem_spec()] + [vmem_spec()] * 4,
        out_specs=vmem_spec(),
        scratch_shapes=[
            pltpu.VMEM((slots, PAIR), BF),
            pltpu.VMEM((2, slots, PAIR), BF),
            pltpu.VMEM((2, slots, PAIR), BF),
            pltpu.VMEM((PAIR, slots), BF),
            pltpu.VMEM((slots, PAIR), BF),
            pltpu.VMEM((2, slots), F32),
            pltpu.VMEM((PAIR, slots), F32),
        ],
        compiler_params=pltpu.CompilerParams(vmem_limit_bytes=VMEM_LIMIT),
        cost_estimate=pl.CostEstimate(
            flops=pairs * PAIR * 10, transcendentals=pairs, bytes_accessed=slots * PAIR * 20
        ),
        name="self_backward",
    )(info, qkv, mixed, grad, logs)


def cross_forward(info, query, kv, n):
    rows, keys = query.shape[0], kv.shape[1]
    pairs = rows * keys * n
    grid_spec = pltpu.PrefetchScalarGridSpec(
        num_scalar_prefetch=1,
        grid=(n,),
        in_specs=[
            pl.BlockSpec((rows, PAIR), lambda j, info: (0, j)),
            pl.BlockSpec((1, keys, 2 * PAIR), lambda j, info: (info[1] ^ j, 0, 0)),
        ],
        out_specs=[
            pl.BlockSpec((rows, PAIR), lambda j, info: (0, j)),
            pl.BlockSpec((1, 2, rows), lambda j, info: (j, 0, 0)),
        ],
    )
    return pl.pallas_call(
        cross_forward_kernel,
        grid_spec=grid_spec,
        out_shape=(
            jax.ShapeDtypeStruct((rows, PAIR * n), BF),
            jax.ShapeDtypeStruct((n, 2, rows), F32),
        ),
        compiler_params=pltpu.CompilerParams(vmem_limit_bytes=VMEM_LIMIT),
        cost_estimate=pl.CostEstimate(
            flops=pairs * PAIR * 8, transcendentals=2 * pairs, bytes_accessed=rows * PAIR * n * 6
        ),
        name="cross_forward",
    )(info, query, kv)


def cross_backward(info, query, kv, mixed, grad, logs, n):
    rows, keys = query.shape[0], kv.shape[1]
    pairs = rows * keys * n
    col = pl.BlockSpec((rows, PAIR), lambda j, info: (0, j))
    grid_spec = pltpu.PrefetchScalarGridSpec(
        num_scalar_prefetch=1,
        grid=(n,),
        in_specs=[
            col,
            pl.BlockSpec((1, keys, 2 * PAIR), lambda j, info: (info[1] ^ j, 0, 0)),
            col,
            col,
            pl.BlockSpec((1, 2, rows), lambda j, info: (j, 0, 0)),
        ],
        out_specs=[
            col,
            pl.BlockSpec((1, keys, 2 * PAIR), lambda j, info: (info[1] ^ j, 0, 0)),
        ],
    )
    return pl.pallas_call(
        cross_backward_kernel,
        grid_spec=grid_spec,
        out_shape=(
            jax.ShapeDtypeStruct((rows, PAIR * n), BF),
            jax.ShapeDtypeStruct((n, keys, 2 * PAIR), BF),
        ),
        compiler_params=pltpu.CompilerParams(vmem_limit_bytes=VMEM_LIMIT),
        cost_estimate=pl.CostEstimate(
            flops=pairs * PAIR * 20, transcendentals=2 * pairs, bytes_accessed=rows * PAIR * n * 10
        ),
        name="cross_backward",
    )(info, query, kv, mixed, grad, logs)


def tp_total(partial):
    mine = partial.astype(BF)
    return mine.astype(F32) + swap(mine).astype(F32)


def tp_join(mine):
    me = lax.axis_index("tp")
    other = swap(mine)
    return jnp.concatenate(
        [jnp.where(me == 0, mine, other), jnp.where(me == 0, other, mine)], axis=0
    )


def body(
    inputs,
    encoder_states,
    seq_lengths,
    enc_lengths,
    cotangent,
    norm_gains,
    norm_biases,
    w_query,
    w_key,
    w_value,
    w_out,
    w_cross_query,
    w_cross_key,
    w_cross_value,
    w_cross_out,
    w_inner,
    w_outer,
):
    n, f = lax.axis_size("ctx"), lax.axis_size("fsdp")
    me_c, me_t = lax.axis_index("ctx"), lax.axis_index("tp")
    rows, width = inputs.shape[1], inputs.shape[2]
    half = rows // 2
    wide = w_query.shape[1]
    shard = w_query.shape[0]
    seq_limit, enc_limit = seq_lengths[0], enc_lengths[0]
    self_info = jnp.stack([seq_limit, me_c, me_t]).astype(jnp.int32)
    cross_info = jnp.stack([enc_limit, me_c, me_t]).astype(jnp.int32)

    enc_half = encoder_states.shape[1] // 2

    def side(t):
        return jnp.concatenate(
            [
                lax.dynamic_slice_in_dim(inputs[0], t * half, half, 0),
                lax.dynamic_slice_in_dim(encoder_states[0], t * enc_half, enc_half, 0),
            ],
            axis=0,
        )

    five = jnp.stack([w_query, w_key, w_value, w_cross_key, w_cross_value], axis=1)
    five = five.reshape(shard, 5, n, PAIR).transpose(2, 0, 1, 3).reshape(n, shard, 5 * PAIR)
    params = jnp.concatenate([norm_gains, norm_biases], axis=0).reshape(1, 1, 8 * shard)
    params = jnp.pad(params, ((0, 0), (0, 15), (0, 5 * PAIR - 8 * shard)))
    five = jnp.concatenate([five, jnp.broadcast_to(params, (n,) + params.shape[1:])], axis=1)
    five = natural(exchange_direct(five, "ctx"), "ctx")
    in_z = Gathering(w_inner, "ctx", False)
    in_seen = [in_z.start()]
    five = gather_direct(five, "fsdp")
    while len(in_z.order) > 1:
        in_seen.append(in_z.step())

    seen_x = []
    mine_rows = gather_offsets(tie(side(me_t), in_seen[0]), "ctx", False, seen_x, in_seen[-1])
    w_in = Doubling(in_z.end())

    w_three = jnp.concatenate([w_out.T, w_cross_query, w_cross_out.T], axis=1)
    three_z = Gathering(w_three, "ctx", False)
    three_z.start(seen_x[0])
    outer_z = Gathering(w_outer.T, "ctx", False)
    outer_z.start(seen_x[0])
    while len(w_in.parts[0].order) > 1:
        w_in.step(seen_x[0])
    while len(three_z.order) > 1:
        three_seen = three_z.step(seen_x[-1])
        outer_z.step(three_seen)
    w_three = Doubling(three_z.end())

    came_rows = swap(jnp.concatenate(mine_rows[1:], axis=0))
    size = half + enc_half
    five = five.reshape(f * n, shard + 16, 5 * PAIR)
    params = five[:, shard, : 8 * shard].reshape(f * n, 8, shard)
    params = params.transpose(1, 0, 2).reshape(8, width).astype(F32)
    gains, biases = params[:4], params[4:]
    five = five[:, :shard].reshape(width, 5 * PAIR)
    w_qkv, w_ckv = five[:, : 3 * PAIR], five[:, 3 * PAIR :]
    their_rows = [side(1 - me_t)] + [came_rows[k * size : (k + 1) * size] for k in range(n - 1)]
    x_all = jnp.concatenate([v[:half] for k in range(n) for v in (mine_rows[k], their_rows[k])])
    enc_found = [[v[half:] for v in (mine_rows[k], their_rows[k])] for k in range(n)]
    enc_at = [[lax.select_n(me_t, e[0], e[1]), lax.select_n(me_t, e[1], e[0])] for e in enc_found]
    enc_all = natural([jnp.concatenate(e, axis=0) for e in enc_at], "ctx")
    ckv_own = nn(enc_all, w_ckv).astype(BF)
    seen_ckv = []
    ckv = jnp.stack(gather_offsets(ckv_own, "ctx", False, seen_ckv), axis=0)

    scales = jnp.concatenate([gains[:1], biases[:1]], axis=0)
    kept, qkv = project(tie(x_all, ckv_own, *w_in.came), scales, w_qkv)
    outer_z.came = tie(outer_z.came, qkv)
    w_outer_t = Doubling(outer_z.end())
    three_first = w_three.came
    while len(w_three.parts[0].order) > 1:
        w_three.step(qkv)
    mixed, logs = self_forward(self_info, tie(qkv, *three_first, seen_ckv[0]), n)
    w_in = w_in.end(mixed)
    w_three = w_three.end(mixed)
    w_out_t, w_cq, w_co_t = w_three[:, :wide], w_three[:, wide : 2 * wide], w_three[:, 2 * wide :]
    while len(w_outer_t.parts[0].order) > 1:
        w_outer_t.step(mixed)
    pieces = [mixed[:rows]] + [flip(mixed[k * rows : (k + 1) * rows], "ctx", k) for k in range(1, n)]
    attn_flat = natural(pieces, "ctx", 1)
    hidden_x = inputs[0].astype(F32)
    first = hidden_x + tp_total(nt(attn_flat, w_out_t))

    normed_c, scale_c = norm_parts(first)
    cross_in = (normed_c * gains[1] + biases[1]).astype(BF)
    cross_query = nn(cross_in, w_cq).astype(BF)
    cross_flat, cross_logs = cross_forward(cross_info, cross_query, ckv, n)
    second = first + tp_total(nt(cross_flat, w_co_t))
    w_outer_t = w_outer_t.end(cross_flat)

    normed_f, scale_f = norm_parts(second)
    ffn_in = (normed_f * gains[2] + biases[2]).astype(BF)
    inner = nn(ffn_in, w_in)
    gated, gate_pullback = jax.vjp(smooth_gate, inner)
    active = gated.astype(BF)
    third = second + tp_total(nt(active, w_outer_t))

    positions = me_c * rows + lax.iota(jnp.int32, rows)
    valid = (positions < seq_limit).astype(F32)[:, None]
    normed_y, scale_y = norm_parts(third)
    output = (normed_y * gains[3] + biases[3]) * valid

    grad_y = cotangent[0].astype(F32) * valid
    grad_third, gain_y, bias_y = norm_back(grad_y, normed_y, scale_y, gains[3])
    g3 = grad_third.astype(BF)
    outer = Halving([(g3, active)])
    grad_active = gate_pullback(nn(g3, w_outer_t))[0].astype(BF)
    partial = nt(grad_active, w_in).astype(BF)
    inside = Halving([(tie(ffn_in, partial), grad_active)], *outer.flight())
    grad_ffn_in = partial.astype(F32) + swap(partial).astype(F32)
    part_f, gain_f, bias_f = norm_back(grad_ffn_in, normed_f, scale_f, gains[2])
    grad_second = grad_third + part_f
    g2 = grad_second.astype(BF)

    grad_cross = nn(g2, w_co_t).astype(BF)
    grad_cq, dkv = cross_backward(
        cross_info,
        cross_query,
        ckv,
        cross_flat,
        tie(grad_cross, *outer.held(), *inside.held()),
        cross_logs,
        n,
    )
    partial = nt(grad_cq, w_cq).astype(BF)
    outer.step(partial)
    grad_cross_in = partial.astype(F32) + swap(partial).astype(F32)
    grad_cross_in = tie(grad_cross_in, *outer.held())
    part_c, gain_c, bias_c = norm_back(grad_cross_in, normed_c, scale_c, gains[1])
    grad_first = grad_second + part_c
    g1 = grad_first.astype(BF)

    grad_attn = nn(g1, w_out_t).astype(BF)
    grad_attn = grad_attn.reshape(rows, n, PAIR).transpose(1, 0, 2)
    dmixed = exchange_direct(grad_attn, "ctx")
    outer.step(dmixed[0])
    three = Halving(
        [(tie(g1, dmixed[0]), attn_flat), (cross_in, grad_cq), (g2, cross_flat)], *inside.flight()
    )
    inside.step(dmixed[0])

    grad_ckv = scatter_offsets([tie(dkv, dmixed[0])[k] for k in range(n)], "ctx").astype(BF)

    dmixed = tie(
        jnp.concatenate(dmixed, axis=0), *outer.held(), *inside.held(), *three.held(), grad_ckv
    )
    dqkv = self_backward(self_info, qkv, mixed, dmixed, logs, n)

    part = nt(tie(dqkv, *three.flight(), *inside.flight(), *outer.flight()), w_qkv).astype(BF)
    away = jnp.concatenate([part[(2 * k + 1) * half : (2 * k + 2) * half] for k in range(n)])
    came_part = swap(away)
    inside.step(away)
    for leg in outer.parts:
        leg.came = tie(leg.came, away)
        while leg.legs:
            leg.step()
    three.step(away)
    came_part = tie(came_part, *outer.held(), *inside.held(), *three.held())
    part = [
        (
            part[2 * k * half : (2 * k + 1) * half].astype(F32)
            + came_part[k * half : (k + 1) * half].astype(F32)
        ).astype(BF)
        for k in range(n)
    ]
    dqkv_late = tie(dqkv, *part)
    seen_part = []
    grad_attn_in = scatter_offsets(part, "ctx", seen_part)

    both = tn(kept, dqkv_late)
    gain_a = jnp.sum(both[width:] * w_qkv.astype(F32), axis=1)
    bias_a = nt(jnp.sum(dqkv_late.astype(F32), axis=0, keepdims=True), w_qkv.astype(F32))[0]
    norm_grads = jnp.stack(
        [gain_a, 0.5 * gain_c, 0.5 * gain_f, 0.5 * gain_y]
        + [bias_a, 0.5 * bias_c, 0.5 * bias_f, 0.5 * bias_y]
    )
    norm_grads = norm_grads + swap(norm_grads)
    norm_grads = norm_grads.reshape(8, f * n, shard).transpose(1, 0, 2).reshape(f * n, 1, 8 * shard)
    norm_grads = jnp.pad(norm_grads, ((0, 0), (0, 15), (0, 5 * PAIR - 8 * shard)))
    dfive = jnp.concatenate([both[:width], tn(enc_all, grad_ckv)], axis=1)
    dfive = jnp.concatenate([dfive.reshape(f * n, shard, 5 * PAIR), norm_grads], axis=1).astype(BF)
    dfive = scatter_value(dfive.reshape(f * n * (shard + 16), 5 * PAIR), [("fsdp", True)])
    while dfive.legs:
        dfive.step()
    dfive = dfive.end().astype(BF).reshape(n, shard + 16, 5 * PAIR)
    dfive = natural([v[None] for v in exchange_direct(dfive, "ctx")], "ctx")
    norm_grads = jnp.sum(dfive[:, shard, : 8 * shard].astype(F32), axis=0).reshape(8, shard)
    dfive = dfive[:, :shard].reshape(n, shard, 5, PAIR).transpose(2, 1, 0, 3)
    dfive = dfive.reshape(5, shard, wide).astype(F32)

    three.step(both)
    for leg in inside.parts + three.parts:
        leg.came = tie(leg.came, seen_part[0])
        while leg.legs:
            leg.step()
    three = three.end()
    grad_outer, grad_inner = outer.end(seen_part[0]).T, inside.end()
    enc_part = tp_total(nt(tie(grad_ckv, *part), w_ckv)).astype(BF)
    enc = scatter_value(enc_part, [("ctx", True)])
    while len(enc.legs) > 0:
        enc.step()
    grad_encoder = enc.end()

    def mine(values):
        return lax.dynamic_slice_in_dim(values, me_t * half, half, 0)

    normed_a, scale_a = norm_parts(mine(hidden_x))
    part_a, _, _ = norm_back(grad_attn_in, normed_a, scale_a, gains[0])
    grad_inputs = tp_join(mine(grad_first) + part_a)

    return (
        output[None],
        grad_inputs[None],
        grad_encoder[None],
        norm_grads[:4],
        norm_grads[4:],
        dfive[0],
        dfive[1],
        dfive[2],
        three[:, :wide].T,
        three[:, wide : 2 * wide],
        dfive[3],
        dfive[4],
        three[:, 2 * wide :].T,
        grad_inner,
        grad_outer,
    )


def solution(mesh):
    tokens = P("fsdp", "ctx", None)
    norms = P(None, ("fsdp", "ctx"))
    by_rows = P(("fsdp", "ctx"), "tp")
    by_cols = P("tp", ("fsdp", "ctx"))
    return jax.shard_map(
        body,
        mesh=mesh,
        in_specs=(
            tokens,
            tokens,
            P("fsdp"),
            P("fsdp"),
            tokens,
            norms,
            norms,
            by_rows,
            by_rows,
            by_rows,
            by_cols,
            by_rows,
            by_rows,
            by_rows,
            by_cols,
            by_rows,
            by_cols,
        ),
        out_specs=(
            tokens,
            tokens,
            tokens,
            norms,
            norms,
            by_rows,
            by_rows,
            by_rows,
            by_cols,
            by_rows,
            by_rows,
            by_rows,
            by_cols,
            by_rows,
            by_cols,
        ),
        check_vma=False,
    )
```

```python
import functools

import jax
import jax.numpy as jnp
from jax import lax
from jax.experimental import pallas as pl
from jax.experimental.pallas import tpu as pltpu
from jax.sharding import PartitionSpec as P

HEAD_DIM = 64
PAIR = 2 * HEAD_DIM
EPS = 1e-05
GELU_A = 0.7978845608028654
GELU_B = 0.044715
BF = jnp.bfloat16
F32 = jnp.float32
LOW = -1e30


def nn(left, right):
    return jnp.dot(left, right, preferred_element_type=F32)


def tn(left, right):
    return lax.dot_general(left, right, (((0,), (0,)), ((), ())), preferred_element_type=F32)


def nt(left, right):
    return lax.dot_general(left, right, (((1,), (1,)), ((), ())), preferred_element_type=F32)


def smooth_gate(values):
    return 0.5 * values * (1.0 + jnp.tanh(GELU_A * (values + GELU_B * values * values * values)))


def norm_parts(values):
    mean = jnp.mean(values, axis=-1, keepdims=True)
    centred = values - mean
    scale = lax.rsqrt(jnp.mean(centred * centred, axis=-1, keepdims=True) + EPS)
    return (centred * scale, scale)


def norm_back(grad_result, normed, scale, gain):
    grad_normed = grad_result * gain
    grad_input = scale * (
        grad_normed
        - jnp.mean(grad_normed, axis=-1, keepdims=True)
        - normed * jnp.mean(grad_normed * normed, axis=-1, keepdims=True)
    )
    return (grad_input, jnp.sum(grad_result * normed, axis=0), jnp.sum(grad_result, axis=0))


def flip(value, axis, mask):
    n = lax.axis_size(axis)
    return lax.ppermute(value, axis, [(i, i ^ mask) for i in range(n)])


def swap(value):
    return flip(value, "tp", 1)


def tie(value, *others):
    token = lax.optimization_barrier((lax.create_token(),) + others)[0]
    return lax.optimization_barrier((token, value))[1]


def gate(value):
    return swap(value[:16, :PAIR])


def bits_of(axis, low_first):
    n = lax.axis_size(axis)
    order = list(range(n.bit_length() - 1))
    return order if low_first else order[::-1]


def bit_at(axis, bit):
    return (lax.axis_index(axis) >> bit) & 1


class Gathering:
    def __init__(self, value, axis, low_first):
        self.axis, self.order = axis, bits_of(axis, low_first)
        self.blocks, self.came = {0: value}, None

    def start(self, *others):
        bit = self.order[0]
        keys = sorted(self.blocks)
        sent = [self.blocks[k] for k in keys]
        sent = sent[0] if len(sent) == 1 else jnp.concatenate(sent, axis=0)
        if others:
            sent = tie(sent, *others)
        self.came = flip(sent, self.axis, 1 << bit)
        return self.came

    def join(self):
        bit = self.order.pop(0)
        mine = bit_at(self.axis, bit)
        keys = sorted(self.blocks)
        rows = self.came.shape[0] // len(keys)
        blocks = {}
        for place, k in enumerate(keys):
            held, other = self.blocks[k], self.came[place * rows : (place + 1) * rows]
            blocks[k] = jnp.where(mine == 0, held, other)
            blocks[k | 1 << bit] = jnp.where(mine == 0, other, held)
        self.blocks = blocks

    def step(self, *others):
        self.join()
        return self.start(*others)

    def end(self):
        self.join()
        return jnp.concatenate([self.blocks[k] for k in sorted(self.blocks)], axis=0)


class Doubling:
    def __init__(self, value, *others):
        cut = value.shape[0] // 2
        self.parts = [
            Gathering(value[:cut], "fsdp", True),
            Gathering(value[cut:], "fsdp", False),
        ]
        self.start(*others)

    def start(self, *others):
        self.came = [g.start(*others) for g in self.parts]

    def after(self, *others):
        for g in self.parts:
            g.came = tie(g.came, *others)

    def step(self, *others):
        self.after(*others)
        for g in self.parts:
            g.join()
        self.start()

    def end(self, *others):
        self.after(*others)
        for g in self.parts:
            g.join()
        keys = sorted(self.parts[0].blocks)
        return jnp.concatenate([g.blocks[k] for k in keys for g in self.parts], axis=0)


def gather_offsets(value, axis, low_first, seen=None, late=None):
    found = {0: value}
    order = bits_of(axis, low_first)
    for bit in order:
        keys = sorted(found)
        sent = [found[k] for k in keys]
        sent = sent[0] if len(sent) == 1 else jnp.concatenate(sent, axis=0)
        if late is not None and bit == order[-1]:
            sent = tie(sent, late)
        came = flip(sent, axis, 1 << bit)
        rows = value.shape[0]
        if seen is not None:
            seen.append(came)
        for place, k in enumerate(keys):
            found[k ^ (1 << bit)] = came[place * rows : (place + 1) * rows]
    return [found[k] for k in range(lax.axis_size(axis))]


def natural(pieces, axis, dim=0):
    n = len(pieces)
    me = lax.axis_index(axis)
    return jnp.concatenate(
        [lax.select_n(me, *[pieces[j ^ m] for m in range(n)]) for j in range(n)], axis=dim
    )


def gather_direct(value, axis):
    n = lax.axis_size(axis)
    return natural([value] + [flip(value, axis, k) for k in range(1, n)], axis)


def exchange_direct(blocks, axis):
    me = lax.axis_index(axis)
    out = [lax.dynamic_index_in_dim(blocks, me ^ k, 0, keepdims=False) for k in range(len(blocks))]
    return out[:1] + [flip(out[k], axis, k) for k in range(1, len(blocks))]


def half_rows(held, index, bit, bits):
    rows = held.shape[0] // 2
    if bits[0] == bit:
        return lax.dynamic_slice_in_dim(held, index * rows, rows, 0)
    before = 1 << bits.index(bit)
    view = held.reshape(before, 2, rows // before, held.shape[1])
    return lax.dynamic_slice_in_dim(view, index, 1, 1).reshape(rows, held.shape[1])


class Scattering:
    def __init__(self, legs, away, held, bits, first):
        self.legs = [(axis, bit) for axis, low in legs for bit in bits_of(axis, low)][1:]
        self.bits = [b for b in bits if b != first]
        self.held, self.axis = held, legs[0][0]
        self.came = flip(away, legs[0][0], 1 << first)

    def step(self):
        axis, bit = self.legs.pop(0)
        if axis != self.axis:
            self.axis, self.bits = axis, bits_of(axis, False)
        mine = bit_at(axis, bit)

        def part(index):
            held = half_rows(self.held, index, bit, self.bits).astype(F32)
            return (held + half_rows(self.came, index, bit, self.bits).astype(F32)).astype(BF)

        away, held = part(1 - mine), part(mine)
        self.bits = [b for b in self.bits if b != bit]
        self.came, self.held = flip(away, axis, 1 << bit), held

    def end(self):
        return self.held.astype(F32) + self.came.astype(F32)


def scatter_value(value, legs):
    axis, low = legs[0]
    bit, bits = bits_of(axis, low)[0], bits_of(axis, False)
    mine = bit_at(axis, bit)
    return Scattering(
        legs, half_rows(value, 1 - mine, bit, bits), half_rows(value, mine, bit, bits), bits, bit
    )


class Halving:
    def __init__(self, pairs, *others):
        n = lax.axis_size("fsdp")
        bits = bits_of("fsdp", False)
        firsts = [bits_of("fsdp", True)[0], bits_of("fsdp", False)[0]]

        def product(flipped):
            out = []
            for left, right in pairs:
                rows = left.shape[1] // n
                cut = rows // 2
                chosen = []
                for place, bit in enumerate(firsts):
                    index = bit_at("fsdp", bit) ^ flipped
                    sides = [
                        jnp.concatenate(
                            [
                                left[:, b * rows + place * cut : b * rows + (place + 1) * cut]
                                for b in range(n)
                                if b >> bit & 1 == v
                            ],
                            axis=1,
                        )
                        for v in range(2)
                    ]
                    chosen.append(jnp.where(index == 0, sides[0], sides[1]))
                out.append(tn(jnp.concatenate(chosen, axis=1), right).astype(BF))
            return out[0] if len(out) == 1 else jnp.concatenate(out, axis=1)

        away, keep = product(1), product(0)
        if others:
            away = tie(away, *others)
        cut = away.shape[0] // 2
        self.parts = [
            Scattering(
                [("fsdp", low)],
                away[place * cut : (place + 1) * cut],
                keep[place * cut : (place + 1) * cut],
                bits,
                firsts[place],
            )
            for place, low in enumerate((True, False))
        ]
        self.ctx = False

    def after(self, *others):
        for p in self.parts:
            p.came = tie(p.came, *others)

    def flight(self):
        return [p.came for p in self.parts]

    def held(self):
        return [p.held for p in self.parts]

    def over(self):
        return not self.parts[0].legs

    def step(self, *others):
        if others:
            self.after(*others)
        if not self.over():
            while not self.over():
                for p in self.parts:
                    p.step()
        elif not self.ctx:
            value = jnp.concatenate([p.end().astype(BF) for p in self.parts], axis=0)
            self.parts, self.ctx = [scatter_value(value, [("ctx", True)])], True

    def end(self, *others):
        if others:
            self.after(*others)
        return self.parts[0].end()


def scatter_offsets(pieces, axis, seen=None):
    n = lax.axis_size(axis)
    held = dict(enumerate(pieces))
    for bit in bits_of(axis, True):
        last = n == 2 << bit
        away = [held[k].astype(BF) for k in sorted(held) if k >> bit & 1]
        came = flip(away[0] if len(away) == 1 else jnp.concatenate(away, axis=0), axis, 1 << bit)
        rows = pieces[0].shape[0]
        if seen is not None:
            seen.append(came)
        held = {k: v for k, v in held.items() if not k >> bit & 1}
        for place, k in enumerate(sorted(held)):
            held[k] = held[k].astype(F32) + came[place * rows : (place + 1) * rows].astype(F32)
            if not last:
                held[k] = held[k].astype(BF)
    return held[0]


def lanes_of(head, shape):
    lane = lax.broadcasted_iota(jnp.int32, shape, len(shape) - 1)
    return (lane // HEAD_DIM) == head


def project_kernel(x_ref, scales, weight, kept, out):
    x = x_ref[...].astype(F32)
    width = x.shape[1]
    centred = x - jnp.sum(x, axis=1, keepdims=True) * (1.0 / width)
    spread = jnp.sum(centred * centred, axis=1, keepdims=True) * (1.0 / width)
    normed = centred * lax.rsqrt(spread + EPS)
    attn_in = (normed * scales[0:1, :] + scales[1:2, :]).astype(BF)
    kept[:, :width] = attn_in
    kept[:, width:] = normed.astype(BF)
    out[...] = nn(attn_in, weight[...]).astype(BF)


def project(x_all, scales, weight):
    slots, width = x_all.shape
    cols = weight.shape[1]
    block = min(256, slots)
    return pl.pallas_call(
        project_kernel,
        grid=(slots // block,),
        in_specs=[
            pl.BlockSpec((block, width), lambda i: (i, 0)),
            pl.BlockSpec((2, width), lambda i: (0, 0)),
            pl.BlockSpec((width, cols), lambda i: (0, 0)),
        ],
        out_specs=[
            pl.BlockSpec((block, 2 * width), lambda i: (i, 0)),
            pl.BlockSpec((block, cols), lambda i: (i, 0)),
        ],
        out_shape=[
            jax.ShapeDtypeStruct((slots, 2 * width), BF),
            jax.ShapeDtypeStruct((slots, cols), BF),
        ],
        compiler_params=pltpu.CompilerParams(vmem_limit_bytes=VMEM_LIMIT),
        cost_estimate=pl.CostEstimate(
            flops=slots * width * cols * 4, transcendentals=0, bytes_accessed=slots * width * 8
        ),
        name="project",
    )(x_all, scales, weight)


def self_forward_kernel(n, block, info, qkv, mixed, logs, q_s, k_s, v_s):
    limit, me_c, me_t = info[0], info[1], info[2]
    half = block // 2
    for c in range(n):
        for t in range(2):
            place = (me_c ^ c) * block + (me_t ^ t) * half
            place = pl.multiple_of(place, half)
            to = slice(c * block + t * half, c * block + t * half + half)
            rows = qkv[pl.ds(place, half), :]
            q_s[to, :] = rows[:, :PAIR] * jnp.asarray(HEAD_DIM**-0.5, BF)
            keys = rows[:, PAIR : 2 * PAIR]
            for h in range(2):
                k_s[h, to, :] = jnp.where(lanes_of(h, keys.shape), keys, jnp.zeros_like(keys))
            v_s[:, to] = rows[:, 2 * PAIR :].astype(F32).T.astype(BF)

    def one(i, _):
        at_q = pl.multiple_of(i * block, block)
        query = q_s[pl.ds(at_q, block), :]

        def step(masked, j, state):
            at_k = pl.multiple_of(j * block, block)
            out = []
            for h in range(2):
                top, tot, acc = state[h]
                score = nt(k_s[h, pl.ds(at_k, block), :], query)
                if masked:
                    key_at = at_k + lax.broadcasted_iota(jnp.int32, score.shape, 0)
                    slot_at = at_q + lax.broadcasted_iota(jnp.int32, score.shape, 1)
                    score = jnp.where((key_at <= slot_at) & (key_at < limit), score, LOW)
                new_top = jnp.maximum(top, jnp.max(score, axis=0, keepdims=True))
                fade = jnp.exp(top - new_top)
                chance = jnp.exp(score - new_top)
                tot = tot * fade + jnp.sum(chance, axis=0, keepdims=True)
                part = nn(
                    v_s[h * HEAD_DIM : (h + 1) * HEAD_DIM, pl.ds(at_k, block)], chance.astype(BF)
                )
                out.append((new_top, tot, acc * fade + part))
            return tuple(out)

        start = tuple(
            (
                jnp.full((1, block), LOW, F32),
                jnp.zeros((1, block), F32),
                jnp.zeros((HEAD_DIM, block), F32),
            )
            for _ in range(2)
        )
        whole = jnp.minimum(i, limit // block)
        last = jnp.minimum(i + 1, (limit + block - 1) // block)
        state = lax.fori_loop(0, whole, functools.partial(step, False), start)
        state = lax.fori_loop(whole, last, functools.partial(step, True), state)
        both = jnp.concatenate([acc / tot for _, tot, acc in state], axis=0)
        place = pl.multiple_of((me_c ^ i) * block, block)
        mixed[pl.ds(place, block), :] = both.T.astype(BF)
        for h in range(2):
            top, tot, _ = state[h]
            logs[h : h + 1, pl.ds(at_q, block)] = top + jnp.log(tot)
        return 0

    lax.fori_loop(0, n, one, 0)


def self_backward_kernel(
    n, block, info, qkv, mixed, grad, logs, grads, q_s, k_s, v_s, kt_s, d_s, delta_s, dq_s
):
    limit, me_c, me_t = info[0], info[1], info[2]
    half = block // 2
    for c in range(n):
        for t in range(2):
            place = (me_c ^ c) * block + (me_t ^ t) * half
            place = pl.multiple_of(place, half)
            to = slice(c * block + t * half, c * block + t * half + half)
            rows = qkv[pl.ds(place, half), :]
            q_s[to, :] = rows[:, :PAIR] * jnp.asarray(HEAD_DIM**-0.5, BF)
            keys = rows[:, PAIR : 2 * PAIR]
            values = rows[:, 2 * PAIR :]
            for h in range(2):
                k_s[h, to, :] = jnp.where(lanes_of(h, keys.shape), keys, jnp.zeros_like(keys))
                v_s[h, to, :] = jnp.where(lanes_of(h, keys.shape), values, jnp.zeros_like(keys))
            kt_s[:, to] = keys.astype(F32).T.astype(BF)
            at = pl.multiple_of((me_c ^ c) * block + t * half, half)
            dout = grad[pl.ds(at, half), :]
            d_s[to, :] = dout
            both = (dout.astype(F32) * mixed[pl.ds(at, half), :].astype(F32)).T
            for h in range(2):
                delta_s[h : h + 1, to] = jnp.sum(
                    both[h * HEAD_DIM : (h + 1) * HEAD_DIM, :], axis=0, keepdims=True
                )
    dq_s[...] = jnp.zeros_like(dq_s)

    def one(j, _):
        at_k = pl.multiple_of(j * block, block)

        def step(masked, i, state):
            at_q = pl.multiple_of(i * block, block)
            query = q_s[pl.ds(at_q, block), :]
            dout = d_s[pl.ds(at_q, block), :]
            out = []
            for h in range(2):
                dk, dv = state[h]
                score = nt(k_s[h, pl.ds(at_k, block), :], query)
                if masked:
                    key_at = at_k + lax.broadcasted_iota(jnp.int32, score.shape, 0)
                    slot_at = at_q + lax.broadcasted_iota(jnp.int32, score.shape, 1)
                    score = jnp.where((key_at <= slot_at) & (key_at < limit), score, LOW)
                chance = jnp.exp(score - logs[h : h + 1, pl.ds(at_q, block)])
                slopes = nt(v_s[h, pl.ds(at_k, block), :], dout)
                bend = (chance * (slopes - delta_s[h : h + 1, pl.ds(at_q, block)])).astype(BF)
                dv = dv + nn(chance.astype(BF), dout)
                dk = dk + nn(bend, query)
                side = slice(h * HEAD_DIM, (h + 1) * HEAD_DIM)
                dq_s[side, pl.ds(at_q, block)] += nn(kt_s[side, pl.ds(at_k, block)], bend)
                out.append((dk, dv))
            return tuple(out)

        start = tuple(
            (jnp.zeros((block, PAIR), F32), jnp.zeros((block, PAIR), F32)) for _ in range(2)
        )
        end = jnp.where(j * block < limit, n, j)
        middle = jnp.where((j + 1) * block <= limit, jnp.minimum(j + 1, end), end)
        state = lax.fori_loop(j, middle, functools.partial(step, True), start)
        state = lax.fori_loop(middle, end, functools.partial(step, False), state)
        first_head = lanes_of(0, (block, PAIR))
        dk = jnp.where(first_head, state[0][0], state[1][0]).astype(BF)
        dv = jnp.where(first_head, state[0][1], state[1][1]).astype(BF)
        for t in range(2):
            place = (me_c ^ j) * block + (me_t ^ t) * half
            place = pl.multiple_of(place, half)
            grads[pl.ds(place, half), PAIR : 2 * PAIR] = dk[t * half : (t + 1) * half, :]
            grads[pl.ds(place, half), 2 * PAIR :] = dv[t * half : (t + 1) * half, :]
        return 0

    lax.fori_loop(0, n, one, 0)
    for c in range(n):
        dq = (dq_s[:, c * block : (c + 1) * block] * HEAD_DIM**-0.5).T.astype(BF)
        for t in range(2):
            place = (me_c ^ c) * block + (me_t ^ t) * half
            place = pl.multiple_of(place, half)
            grads[pl.ds(place, half), :PAIR] = dq[t * half : (t + 1) * half, :]


def cross_scores(limit, keys, query):
    score = nt(keys, query)
    key_at = lax.broadcasted_iota(jnp.int32, score.shape, 0)
    return jnp.where(key_at < limit, score, LOW)


def masked_pair(values, head):
    return jnp.where(lanes_of(head, values.shape), values, jnp.zeros_like(values))


def cross_forward_kernel(info, query_ref, kv, mixed, logs):
    limit = info[0]
    query = query_ref[...] * jnp.asarray(HEAD_DIM**-0.5, BF)
    keys = kv[0, :, :PAIR]
    values = kv[0, :, PAIR:].astype(F32).T.astype(BF)
    outs = []
    for h in range(2):
        score = cross_scores(limit, masked_pair(keys, h), query)
        top = jnp.max(score, axis=0, keepdims=True)
        chance = jnp.exp(score - top)
        tot = jnp.sum(chance, axis=0, keepdims=True)
        outs.append(nn(values[h * HEAD_DIM : (h + 1) * HEAD_DIM, :], chance.astype(BF)) / tot)
        logs[0, h : h + 1, :] = top + jnp.log(tot)
    mixed[...] = jnp.concatenate(outs, axis=0).T.astype(BF)


def cross_backward_kernel(info, query_ref, kv, mixed, grad, logs, dq_ref, dkv):
    limit = info[0]
    query = query_ref[...] * jnp.asarray(HEAD_DIM**-0.5, BF)
    keys = kv[0, :, :PAIR]
    values = kv[0, :, PAIR:]
    keys_t = keys.astype(F32).T.astype(BF)
    dout = grad[...]
    both = (dout.astype(F32) * mixed[...].astype(F32)).T
    dqs, dks, dvs = [], [], []
    for h in range(2):
        side = slice(h * HEAD_DIM, (h + 1) * HEAD_DIM)
        delta = jnp.sum(both[side, :], axis=0, keepdims=True)
        score = cross_scores(limit, masked_pair(keys, h), query)
        chance = jnp.exp(score - logs[0, h : h + 1, :])
        slopes = nt(masked_pair(values, h), dout)
        bend = (chance * (slopes - delta)).astype(BF)
        dvs.append(nn(chance.astype(BF), dout))
        dks.append(nn(bend, query))
        dqs.append(nn(keys_t[side, :], bend))
    dq_ref[...] = (jnp.concatenate(dqs, axis=0) * HEAD_DIM**-0.5).T.astype(BF)
    first_head = lanes_of(0, dks[0].shape)
    dkv[0, :, :PAIR] = jnp.where(first_head, dks[0], dks[1]).astype(BF)
    dkv[0, :, PAIR:] = jnp.where(first_head, dvs[0], dvs[1]).astype(BF)


VMEM_LIMIT = 48 * 1024 * 1024


def vmem_spec():
    return pl.BlockSpec(memory_space=pltpu.VMEM)


def smem_spec():
    return pl.BlockSpec(memory_space=pltpu.SMEM)


def self_forward(info, qkv, n):
    slots = qkv.shape[0]
    block = slots // n
    pairs = slots * slots
    return pl.pallas_call(
        functools.partial(self_forward_kernel, n, block),
        out_shape=(
            jax.ShapeDtypeStruct((slots, PAIR), BF),
            jax.ShapeDtypeStruct((2, slots), F32),
        ),
        in_specs=[smem_spec(), vmem_spec()],
        out_specs=(vmem_spec(), vmem_spec()),
        scratch_shapes=[
            pltpu.VMEM((slots, PAIR), BF),
            pltpu.VMEM((2, slots, PAIR), BF),
            pltpu.VMEM((PAIR, slots), BF),
        ],
        compiler_params=pltpu.CompilerParams(vmem_limit_bytes=VMEM_LIMIT),
        cost_estimate=pl.CostEstimate(
            flops=pairs * PAIR * 4, transcendentals=pairs, bytes_accessed=slots * PAIR * 8
        ),
        name="self_forward",
    )(info, qkv)


def self_backward(info, qkv, mixed, grad, logs, n):
    slots = qkv.shape[0]
    block = slots // n
    pairs = slots * slots
    return pl.pallas_call(
        functools.partial(self_backward_kernel, n, block),
        out_shape=jax.ShapeDtypeStruct((slots, 3 * PAIR), BF),
        in_specs=[smem_spec()] + [vmem_spec()] * 4,
        out_specs=vmem_spec(),
        scratch_shapes=[
            pltpu.VMEM((slots, PAIR), BF),
            pltpu.VMEM((2, slots, PAIR), BF),
            pltpu.VMEM((2, slots, PAIR), BF),
            pltpu.VMEM((PAIR, slots), BF),
            pltpu.VMEM((slots, PAIR), BF),
            pltpu.VMEM((2, slots), F32),
            pltpu.VMEM((PAIR, slots), F32),
        ],
        compiler_params=pltpu.CompilerParams(vmem_limit_bytes=VMEM_LIMIT),
        cost_estimate=pl.CostEstimate(
            flops=pairs * PAIR * 10, transcendentals=pairs, bytes_accessed=slots * PAIR * 20
        ),
        name="self_backward",
    )(info, qkv, mixed, grad, logs)


def cross_forward(info, query, kv, n):
    rows, keys = query.shape[0], kv.shape[1]
    pairs = rows * keys * n
    grid_spec = pltpu.PrefetchScalarGridSpec(
        num_scalar_prefetch=1,
        grid=(n,),
        in_specs=[
            pl.BlockSpec((rows, PAIR), lambda j, info: (0, j)),
            pl.BlockSpec((1, keys, 2 * PAIR), lambda j, info: (info[1] ^ j, 0, 0)),
        ],
        out_specs=[
            pl.BlockSpec((rows, PAIR), lambda j, info: (0, j)),
            pl.BlockSpec((1, 2, rows), lambda j, info: (j, 0, 0)),
        ],
    )
    return pl.pallas_call(
        cross_forward_kernel,
        grid_spec=grid_spec,
        out_shape=(
            jax.ShapeDtypeStruct((rows, PAIR * n), BF),
            jax.ShapeDtypeStruct((n, 2, rows), F32),
        ),
        compiler_params=pltpu.CompilerParams(vmem_limit_bytes=VMEM_LIMIT),
        cost_estimate=pl.CostEstimate(
            flops=pairs * PAIR * 8, transcendentals=2 * pairs, bytes_accessed=rows * PAIR * n * 6
        ),
        name="cross_forward",
    )(info, query, kv)


def cross_backward(info, query, kv, mixed, grad, logs, n):
    rows, keys = query.shape[0], kv.shape[1]
    pairs = rows * keys * n
    col = pl.BlockSpec((rows, PAIR), lambda j, info: (0, j))
    grid_spec = pltpu.PrefetchScalarGridSpec(
        num_scalar_prefetch=1,
        grid=(n,),
        in_specs=[
            col,
            pl.BlockSpec((1, keys, 2 * PAIR), lambda j, info: (info[1] ^ j, 0, 0)),
            col,
            col,
            pl.BlockSpec((1, 2, rows), lambda j, info: (j, 0, 0)),
        ],
        out_specs=[
            col,
            pl.BlockSpec((1, keys, 2 * PAIR), lambda j, info: (info[1] ^ j, 0, 0)),
        ],
    )
    return pl.pallas_call(
        cross_backward_kernel,
        grid_spec=grid_spec,
        out_shape=(
            jax.ShapeDtypeStruct((rows, PAIR * n), BF),
            jax.ShapeDtypeStruct((n, keys, 2 * PAIR), BF),
        ),
        compiler_params=pltpu.CompilerParams(vmem_limit_bytes=VMEM_LIMIT),
        cost_estimate=pl.CostEstimate(
            flops=pairs * PAIR * 20, transcendentals=2 * pairs, bytes_accessed=rows * PAIR * n * 10
        ),
        name="cross_backward",
    )(info, query, kv, mixed, grad, logs)


def tp_total(partial):
    mine = partial.astype(BF)
    return mine.astype(F32) + swap(mine).astype(F32)


def tp_join(mine):
    me = lax.axis_index("tp")
    other = swap(mine)
    return jnp.concatenate(
        [jnp.where(me == 0, mine, other), jnp.where(me == 0, other, mine)], axis=0
    )


def body(
    inputs,
    encoder_states,
    seq_lengths,
    enc_lengths,
    cotangent,
    norm_gains,
    norm_biases,
    w_query,
    w_key,
    w_value,
    w_out,
    w_cross_query,
    w_cross_key,
    w_cross_value,
    w_cross_out,
    w_inner,
    w_outer,
):
    n, f = lax.axis_size("ctx"), lax.axis_size("fsdp")
    me_c, me_t = lax.axis_index("ctx"), lax.axis_index("tp")
    rows, width = inputs.shape[1], inputs.shape[2]
    half = rows // 2
    wide = w_query.shape[1]
    shard = w_query.shape[0]
    seq_limit, enc_limit = seq_lengths[0], enc_lengths[0]
    self_info = jnp.stack([seq_limit, me_c, me_t]).astype(jnp.int32)
    cross_info = jnp.stack([enc_limit, me_c, me_t]).astype(jnp.int32)

    enc_half = encoder_states.shape[1] // 2

    def side(t):
        return jnp.concatenate(
            [
                lax.dynamic_slice_in_dim(inputs[0], t * half, half, 0),
                lax.dynamic_slice_in_dim(encoder_states[0], t * enc_half, enc_half, 0),
            ],
            axis=0,
        )

    five = jnp.stack([w_query, w_key, w_value, w_cross_key, w_cross_value], axis=1)
    five = five.reshape(shard, 5, n, PAIR).transpose(2, 0, 1, 3).reshape(n, shard, 5 * PAIR)
    params = jnp.concatenate([norm_gains, norm_biases], axis=0).reshape(1, 1, 8 * shard)
    params = jnp.pad(params, ((0, 0), (0, 15), (0, 5 * PAIR - 8 * shard)))
    five = jnp.concatenate([five, jnp.broadcast_to(params, (n,) + params.shape[1:])], axis=1)
    five = natural(exchange_direct(five, "ctx"), "ctx")
    in_z = Gathering(w_inner, "ctx", False)
    in_seen = [in_z.start()]
    five = gather_direct(five, "fsdp")
    while len(in_z.order) > 1:
        in_seen.append(in_z.step())

    seen_x = []
    mine_rows = gather_offsets(tie(side(me_t), in_seen[0]), "ctx", False, seen_x, in_seen[-1])
    w_in = Doubling(in_z.end())

    w_three = jnp.concatenate([w_out.T, w_cross_query, w_cross_out.T], axis=1)
    three_z = Gathering(w_three, "ctx", False)
    three_z.start(seen_x[0])
    in_first = w_in.came
    while len(w_in.parts[0].order) > 1:
        w_in.step(seen_x[0])
    while len(three_z.order) > 1:
        three_z.step()
    outer_z = Gathering(w_outer.T, "ctx", False)
    outer_z.start(seen_x[-1])
    w_three = Doubling(three_z.end())

    came_rows = swap(tie(jnp.concatenate(mine_rows[1:], axis=0), *in_first, *w_in.came))
    size = half + enc_half
    five = five.reshape(f * n, shard + 16, 5 * PAIR)
    params = five[:, shard, : 8 * shard].reshape(f * n, 8, shard)
    params = params.transpose(1, 0, 2).reshape(8, width).astype(F32)
    gains, biases = params[:4], params[4:]
    five = five[:, :shard].reshape(width, 5 * PAIR)
    w_qkv, w_ckv = five[:, : 3 * PAIR], five[:, 3 * PAIR :]
    their_rows = [side(1 - me_t)] + [came_rows[k * size : (k + 1) * size] for k in range(n - 1)]
    x_all = jnp.concatenate([v[:half] for k in range(n) for v in (mine_rows[k], their_rows[k])])
    enc_found = [[v[half:] for v in (mine_rows[k], their_rows[k])] for k in range(n)]
    enc_at = [[lax.select_n(me_t, e[0], e[1]), lax.select_n(me_t, e[1], e[0])] for e in enc_found]
    enc_all = natural([jnp.concatenate(e, axis=0) for e in enc_at], "ctx")
    ckv_own = nn(enc_all, w_ckv).astype(BF)
    seen_ckv = []
    ckv = jnp.stack(gather_offsets(ckv_own, "ctx", False, seen_ckv), axis=0)

    scales = jnp.concatenate([gains[:1], biases[:1]], axis=0)
    kept, qkv = project(tie(x_all, ckv_own), scales, w_qkv)
    three_first = w_three.came
    while len(w_three.parts[0].order) > 1:
        w_three.step(came_rows)
    while len(outer_z.order) > 1:
        outer_z.step(came_rows)
    mixed, logs = self_forward(
        self_info, tie(qkv, *three_first, *w_in.came, seen_ckv[0]), n
    )
    outer_z.came = tie(outer_z.came, mixed)
    w_outer_t = Doubling(outer_z.end())
    mixed_out = tie(mixed, *w_three.came)
    w_in = w_in.end(mixed_out)
    w_three = w_three.end(mixed_out)
    w_out_t, w_cq, w_co_t = w_three[:, :wide], w_three[:, wide : 2 * wide], w_three[:, 2 * wide :]
    pieces = [mixed_out[:rows]]
    pieces += [flip(mixed_out[k * rows : (k + 1) * rows], "ctx", k) for k in range(1, n)]
    attn_flat = natural(pieces, "ctx", 1)
    while len(w_outer_t.parts[0].order) > 1:
        w_outer_t.step(attn_flat)
    hidden_x = inputs[0].astype(F32)
    first = hidden_x + tp_total(nt(attn_flat, w_out_t))

    normed_c, scale_c = norm_parts(first)
    cross_in = (normed_c * gains[1] + biases[1]).astype(BF)
    cross_query = nn(cross_in, w_cq).astype(BF)
    cross_flat, cross_logs = cross_forward(cross_info, cross_query, ckv, n)
    second = first + tp_total(nt(cross_flat, w_co_t))
    w_outer_t = w_outer_t.end(cross_flat)

    normed_f, scale_f = norm_parts(second)
    ffn_in = (normed_f * gains[2] + biases[2]).astype(BF)
    inner = nn(ffn_in, w_in)
    gated, gate_pullback = jax.vjp(smooth_gate, inner)
    active = gated.astype(BF)
    third = second + tp_total(nt(active, w_outer_t))

    positions = me_c * rows + lax.iota(jnp.int32, rows)
    valid = (positions < seq_limit).astype(F32)[:, None]
    normed_y, scale_y = norm_parts(third)
    output = (normed_y * gains[3] + biases[3]) * valid

    grad_y = cotangent[0].astype(F32) * valid
    grad_third, gain_y, bias_y = norm_back(grad_y, normed_y, scale_y, gains[3])
    g3 = grad_third.astype(BF)
    outer = Halving([(g3, active)])
    grad_active = gate_pullback(nn(g3, w_outer_t))[0].astype(BF)
    partial = nt(grad_active, w_in).astype(BF)
    inside = Halving([(tie(ffn_in, partial), grad_active)], *outer.flight())
    grad_ffn_in = partial.astype(F32) + swap(partial).astype(F32)
    part_f, gain_f, bias_f = norm_back(grad_ffn_in, normed_f, scale_f, gains[2])
    grad_second = grad_third + part_f
    g2 = grad_second.astype(BF)

    grad_cross = nn(g2, w_co_t).astype(BF)
    grad_cq, dkv = cross_backward(
        cross_info,
        cross_query,
        ckv,
        cross_flat,
        tie(grad_cross, *outer.held(), *inside.held()),
        cross_logs,
        n,
    )
    partial = nt(grad_cq, w_cq).astype(BF)
    outer.step(partial)
    grad_cross_in = partial.astype(F32) + swap(partial).astype(F32)
    grad_cross_in = tie(grad_cross_in, *outer.held())
    part_c, gain_c, bias_c = norm_back(grad_cross_in, normed_c, scale_c, gains[1])
    grad_first = grad_second + part_c
    g1 = grad_first.astype(BF)

    grad_attn = nn(g1, w_out_t).astype(BF)
    grad_attn = grad_attn.reshape(rows, n, PAIR).transpose(1, 0, 2)
    token = gate(grad_attn[0])
    dmixed = exchange_direct(grad_attn, "ctx")
    outer.step(token)
    three = Halving(
        [(tie(g1, token), attn_flat), (cross_in, grad_cq), (g2, cross_flat)], *inside.flight()
    )
    inside.step(token)

    seen_dkv = []
    grad_ckv = scatter_offsets([tie(dkv, token)[k] for k in range(n)], "ctx", seen_dkv).astype(BF)

    dmixed = tie(
        jnp.concatenate(dmixed, axis=0), *outer.held(), *inside.held(), *three.held(), seen_dkv[0]
    )
    dqkv = self_backward(self_info, qkv, mixed, dmixed, logs, n)

    part = nt(tie(dqkv, *three.flight(), *inside.flight(), *outer.flight()), w_qkv).astype(BF)
    away = jnp.concatenate([part[(2 * k + 1) * half : (2 * k + 2) * half] for k in range(n)])
    came_part = swap(away)
    for leg in outer.parts:
        leg.came = tie(leg.came, away)
        while leg.legs:
            leg.step()
    came_part = tie(came_part, *outer.held())
    part = [
        (
            part[2 * k * half : (2 * k + 1) * half].astype(F32)
            + came_part[k * half : (k + 1) * half].astype(F32)
        ).astype(BF)
        for k in range(n)
    ]
    dqkv_late = tie(dqkv, *part)
    order = bits_of("ctx", True)
    held, sent = dict(enumerate(part)), []
    for place, bit in enumerate(order):
        away = [held[k] for k in sorted(held) if k >> bit & 1]
        came = flip(away[0] if len(away) == 1 else jnp.concatenate(away, axis=0), "ctx", 1 << bit)
        if place == 0:
            both = tn(kept, dqkv_late)
            gain_a = jnp.sum(both[width:] * w_qkv.astype(F32), axis=1)
            bias_a = nt(jnp.sum(dqkv_late.astype(F32), axis=0, keepdims=True), w_qkv.astype(F32))[0]
            norm_grads = jnp.stack(
                [gain_a, 0.5 * gain_c, 0.5 * gain_f, 0.5 * gain_y]
                + [bias_a, 0.5 * bias_c, 0.5 * bias_f, 0.5 * bias_y]
            )
            norm_grads = norm_grads + swap(norm_grads)
            norm_grads = norm_grads.reshape(8, f * n, shard).transpose(1, 0, 2)
            norm_grads = norm_grads.reshape(f * n, 1, 8 * shard)
            norm_grads = jnp.pad(norm_grads, ((0, 0), (0, 15), (0, 5 * PAIR - 8 * shard)))
            dfive = jnp.concatenate([both[:width], tn(enc_all, grad_ckv)], axis=1)
            dfive = dfive.reshape(f * n, shard, 5 * PAIR)
            dfive = jnp.concatenate([dfive, norm_grads], axis=1).astype(BF)
            dfive = dfive.reshape(f * n * (shard + 16), 5 * PAIR)
            dfive = scatter_value(dfive, [("fsdp", True)])
            three.step(part[0])
            enc_part = tp_total(nt(tie(grad_ckv, both), w_ckv)).astype(BF)
            fill = [dfive.held, *three.held(), enc_part]
        elif place == 1:
            inside.step(sent[0])
            while dfive.legs:
                dfive.came = tie(dfive.came, sent[0])
                dfive.step()
            three.step(*inside.held())
            outer_sum = outer.end(sent[0])
            enc = scatter_value(tie(enc_part, sent[0]), [("ctx", True)])
            fill = [dfive.held, outer_sum, *three.held(), *inside.held(), enc.held]
        else:
            fill = []
        came = tie(came, *fill)
        sent.append(came)
        held = {k: v for k, v in held.items() if not k >> bit & 1}
        for at, k in enumerate(sorted(held)):
            held[k] = held[k].astype(F32) + came[at * half : (at + 1) * half].astype(F32)
            if place < len(order) - 1:
                held[k] = held[k].astype(BF)
    grad_attn_in = held[0]

    for leg in [enc] + inside.parts + three.parts:
        leg.came = tie(leg.came, grad_attn_in)
        while leg.legs:
            leg.step()
    three = three.end()
    grad_outer, grad_inner = outer_sum.T, inside.end()
    dfive = dfive.end().astype(BF).reshape(n, shard + 16, 5 * PAIR)
    dfive = lax.all_to_all(dfive, "ctx", 0, 0, tiled=False)
    norm_grads = jnp.sum(dfive[:, shard, : 8 * shard].astype(F32), axis=0).reshape(8, shard)
    dfive = dfive[:, :shard].reshape(n, shard, 5, PAIR).transpose(2, 1, 0, 3)
    dfive = dfive.reshape(5, shard, wide).astype(F32)
    grad_encoder = enc.end()

    def mine(values):
        return lax.dynamic_slice_in_dim(values, me_t * half, half, 0)

    normed_a, scale_a = norm_parts(mine(hidden_x))
    part_a, _, _ = norm_back(grad_attn_in, normed_a, scale_a, gains[0])
    grad_inputs = tp_join(mine(grad_first) + part_a)

    return (
        output[None],
        grad_inputs[None],
        grad_encoder[None],
        norm_grads[:4],
        norm_grads[4:],
        dfive[0],
        dfive[1],
        dfive[2],
        three[:, :wide].T,
        three[:, wide : 2 * wide],
        dfive[3],
        dfive[4],
        three[:, 2 * wide :].T,
        grad_inner,
        grad_outer,
    )


def solution(mesh):
    tokens = P("fsdp", "ctx", None)
    norms = P(None, ("fsdp", "ctx"))
    by_rows = P(("fsdp", "ctx"), "tp")
    by_cols = P("tp", ("fsdp", "ctx"))
    return jax.shard_map(
        body,
        mesh=mesh,
        in_specs=(
            tokens,
            tokens,
            P("fsdp"),
            P("fsdp"),
            tokens,
            norms,
            norms,
            by_rows,
            by_rows,
            by_rows,
            by_cols,
            by_rows,
            by_rows,
            by_rows,
            by_cols,
            by_rows,
            by_cols,
        ),
        out_specs=(
            tokens,
            tokens,
            tokens,
            norms,
            norms,
            by_rows,
            by_rows,
            by_rows,
            by_cols,
            by_rows,
            by_rows,
            by_rows,
            by_cols,
            by_rows,
            by_cols,
        ),
        check_vma=False,
    )
```

```python
import functools

import jax
import jax.numpy as jnp
from jax import lax
from jax.experimental import pallas as pl
from jax.experimental.pallas import tpu as pltpu
from jax.sharding import PartitionSpec as P

HEAD_DIM = 64
PAIR = 2 * HEAD_DIM
EPS = 1e-05
GELU_A = 0.7978845608028654
GELU_B = 0.044715
BF = jnp.bfloat16
F32 = jnp.float32
LOW = -1e30


def nn(left, right):
    return jnp.dot(left, right, preferred_element_type=F32)


def tn(left, right):
    return lax.dot_general(left, right, (((0,), (0,)), ((), ())), preferred_element_type=F32)


def nt(left, right):
    return lax.dot_general(left, right, (((1,), (1,)), ((), ())), preferred_element_type=F32)


def smooth_gate(values):
    return 0.5 * values * (1.0 + jnp.tanh(GELU_A * (values + GELU_B * values * values * values)))


def norm_parts(values):
    mean = jnp.mean(values, axis=-1, keepdims=True)
    centred = values - mean
    scale = lax.rsqrt(jnp.mean(centred * centred, axis=-1, keepdims=True) + EPS)
    return (centred * scale, scale)


def norm_back(grad_result, normed, scale, gain):
    grad_normed = grad_result * gain
    grad_input = scale * (
        grad_normed
        - jnp.mean(grad_normed, axis=-1, keepdims=True)
        - normed * jnp.mean(grad_normed * normed, axis=-1, keepdims=True)
    )
    return (grad_input, jnp.sum(grad_result * normed, axis=0), jnp.sum(grad_result, axis=0))


def flip(value, axis, mask):
    n = lax.axis_size(axis)
    return lax.ppermute(value, axis, [(i, i ^ mask) for i in range(n)])


def swap(value):
    return flip(value, "tp", 1)


def tie(value, *others):
    token = lax.optimization_barrier((lax.create_token(),) + others)[0]
    return lax.optimization_barrier((token, value))[1]


def gate(value):
    return swap(value[:16, :PAIR])


def bits_of(axis, low_first):
    n = lax.axis_size(axis)
    order = list(range(n.bit_length() - 1))
    return order if low_first else order[::-1]


def bit_at(axis, bit):
    return (lax.axis_index(axis) >> bit) & 1


class Gathering:
    def __init__(self, value, axis, low_first):
        self.axis, self.order = axis, bits_of(axis, low_first)
        self.blocks, self.came = {0: value}, None

    def start(self, *others):
        bit = self.order[0]
        keys = sorted(self.blocks)
        sent = [self.blocks[k] for k in keys]
        sent = sent[0] if len(sent) == 1 else jnp.concatenate(sent, axis=0)
        if others:
            sent = tie(sent, *others)
        self.came = flip(sent, self.axis, 1 << bit)
        return self.came

    def join(self):
        bit = self.order.pop(0)
        mine = bit_at(self.axis, bit)
        keys = sorted(self.blocks)
        rows = self.came.shape[0] // len(keys)
        blocks = {}
        for place, k in enumerate(keys):
            held, other = self.blocks[k], self.came[place * rows : (place + 1) * rows]
            blocks[k] = jnp.where(mine == 0, held, other)
            blocks[k | 1 << bit] = jnp.where(mine == 0, other, held)
        self.blocks = blocks

    def step(self, *others):
        self.join()
        return self.start(*others)

    def end(self):
        self.join()
        return jnp.concatenate([self.blocks[k] for k in sorted(self.blocks)], axis=0)


class Doubling:
    def __init__(self, value, *others):
        cut = value.shape[0] // 2
        self.parts = [
            Gathering(value[:cut], "fsdp", True),
            Gathering(value[cut:], "fsdp", False),
        ]
        self.start(*others)

    def start(self, *others):
        self.came = [g.start(*others) for g in self.parts]

    def after(self, *others):
        for g in self.parts:
            g.came = tie(g.came, *others)

    def step(self, *others):
        self.after(*others)
        for g in self.parts:
            g.join()
        self.start()

    def end(self, *others):
        self.after(*others)
        for g in self.parts:
            g.join()
        keys = sorted(self.parts[0].blocks)
        return jnp.concatenate([g.blocks[k] for k in keys for g in self.parts], axis=0)


def gather_offsets(value, axis, low_first, seen=None, late=None):
    found = {0: value}
    order = bits_of(axis, low_first)
    for bit in order:
        keys = sorted(found)
        sent = [found[k] for k in keys]
        sent = sent[0] if len(sent) == 1 else jnp.concatenate(sent, axis=0)
        if late is not None and bit == order[-1]:
            sent = tie(sent, late)
        came = flip(sent, axis, 1 << bit)
        rows = value.shape[0]
        if seen is not None:
            seen.append(came)
        for place, k in enumerate(keys):
            found[k ^ (1 << bit)] = came[place * rows : (place + 1) * rows]
    return [found[k] for k in range(lax.axis_size(axis))]


def natural(pieces, axis, dim=0):
    n = len(pieces)
    me = lax.axis_index(axis)
    return jnp.concatenate(
        [lax.select_n(me, *[pieces[j ^ m] for m in range(n)]) for j in range(n)], axis=dim
    )


def gather_direct(value, axis):
    n = lax.axis_size(axis)
    return natural([value] + [flip(value, axis, k) for k in range(1, n)], axis)


def exchange_direct(blocks, axis):
    me = lax.axis_index(axis)
    out = [lax.dynamic_index_in_dim(blocks, me ^ k, 0, keepdims=False) for k in range(len(blocks))]
    return out[:1] + [flip(out[k], axis, k) for k in range(1, len(blocks))]


def half_rows(held, index, bit, bits):
    rows = held.shape[0] // 2
    if bits[0] == bit:
        return lax.dynamic_slice_in_dim(held, index * rows, rows, 0)
    before = 1 << bits.index(bit)
    view = held.reshape(before, 2, rows // before, held.shape[1])
    return lax.dynamic_slice_in_dim(view, index, 1, 1).reshape(rows, held.shape[1])


class Scattering:
    def __init__(self, legs, away, held, bits, first):
        self.legs = [(axis, bit) for axis, low in legs for bit in bits_of(axis, low)][1:]
        self.bits = [b for b in bits if b != first]
        self.held, self.axis = held, legs[0][0]
        self.came = flip(away, legs[0][0], 1 << first)

    def step(self):
        axis, bit = self.legs.pop(0)
        if axis != self.axis:
            self.axis, self.bits = axis, bits_of(axis, False)
        mine = bit_at(axis, bit)

        def part(index):
            held = half_rows(self.held, index, bit, self.bits).astype(F32)
            return (held + half_rows(self.came, index, bit, self.bits).astype(F32)).astype(BF)

        away, held = part(1 - mine), part(mine)
        self.bits = [b for b in self.bits if b != bit]
        self.came, self.held = flip(away, axis, 1 << bit), held

    def end(self):
        return self.held.astype(F32) + self.came.astype(F32)


def scatter_value(value, legs):
    axis, low = legs[0]
    bit, bits = bits_of(axis, low)[0], bits_of(axis, False)
    mine = bit_at(axis, bit)
    return Scattering(
        legs, half_rows(value, 1 - mine, bit, bits), half_rows(value, mine, bit, bits), bits, bit
    )


class Halving:
    def __init__(self, pairs):
        n = lax.axis_size("fsdp")
        bits = bits_of("fsdp", False)
        firsts = [bits_of("fsdp", True)[0], bits_of("fsdp", False)[0]]

        def product(flipped):
            out = []
            for left, right in pairs:
                rows = left.shape[1] // n
                cut = rows // 2
                chosen = []
                for place, bit in enumerate(firsts):
                    index = bit_at("fsdp", bit) ^ flipped
                    sides = [
                        jnp.concatenate(
                            [
                                left[:, b * rows + place * cut : b * rows + (place + 1) * cut]
                                for b in range(n)
                                if b >> bit & 1 == v
                            ],
                            axis=1,
                        )
                        for v in range(2)
                    ]
                    chosen.append(jnp.where(index == 0, sides[0], sides[1]))
                out.append(tn(jnp.concatenate(chosen, axis=1), right).astype(BF))
            return out[0] if len(out) == 1 else jnp.concatenate(out, axis=1)

        self.away, self.keep = product(1), product(0)
        self.bits, self.firsts = bits, firsts
        self.ctx = False

    def launch(self, *others):
        away, keep = tie(self.away, *others) if others else self.away, self.keep
        cut = away.shape[0] // 2
        self.parts = [
            Scattering(
                [("fsdp", low)],
                away[place * cut : (place + 1) * cut],
                keep[place * cut : (place + 1) * cut],
                self.bits,
                self.firsts[place],
            )
            for place, low in enumerate((True, False))
        ]

    def after(self, *others):
        for p in self.parts:
            p.came = tie(p.came, *others)

    def flight(self):
        return [p.came for p in self.parts]

    def held(self):
        return [p.held for p in self.parts]

    def over(self):
        return not self.parts[0].legs

    def step(self, *others):
        if others:
            self.after(*others)
        if not self.over():
            while not self.over():
                for p in self.parts:
                    p.step()
        elif not self.ctx:
            value = jnp.concatenate([p.end().astype(BF) for p in self.parts], axis=0)
            self.parts, self.ctx = [scatter_value(value, [("ctx", True)])], True

    def end(self, *others):
        if others:
            self.after(*others)
        return self.parts[0].end()


def scatter_offsets(pieces, axis, seen=None):
    n = lax.axis_size(axis)
    held = dict(enumerate(pieces))
    for bit in bits_of(axis, True):
        last = n == 2 << bit
        away = [held[k].astype(BF) for k in sorted(held) if k >> bit & 1]
        came = flip(away[0] if len(away) == 1 else jnp.concatenate(away, axis=0), axis, 1 << bit)
        rows = pieces[0].shape[0]
        if seen is not None:
            seen.append(came)
        held = {k: v for k, v in held.items() if not k >> bit & 1}
        for place, k in enumerate(sorted(held)):
            held[k] = held[k].astype(F32) + came[place * rows : (place + 1) * rows].astype(F32)
            if not last:
                held[k] = held[k].astype(BF)
    return held[0]


def lanes_of(head, shape):
    lane = lax.broadcasted_iota(jnp.int32, shape, len(shape) - 1)
    return (lane // HEAD_DIM) == head


def project_kernel(x_ref, scales, weight, kept, out):
    x = x_ref[...].astype(F32)
    width = x.shape[1]
    centred = x - jnp.sum(x, axis=1, keepdims=True) * (1.0 / width)
    spread = jnp.sum(centred * centred, axis=1, keepdims=True) * (1.0 / width)
    normed = centred * lax.rsqrt(spread + EPS)
    attn_in = (normed * scales[0:1, :] + scales[1:2, :]).astype(BF)
    kept[:, :width] = attn_in
    kept[:, width:] = normed.astype(BF)
    out[...] = nn(attn_in, weight[...]).astype(BF)


def project(x_all, scales, weight):
    slots, width = x_all.shape
    cols = weight.shape[1]
    block = min(256, slots)
    return pl.pallas_call(
        project_kernel,
        grid=(slots // block,),
        in_specs=[
            pl.BlockSpec((block, width), lambda i: (i, 0)),
            pl.BlockSpec((2, width), lambda i: (0, 0)),
            pl.BlockSpec((width, cols), lambda i: (0, 0)),
        ],
        out_specs=[
            pl.BlockSpec((block, 2 * width), lambda i: (i, 0)),
            pl.BlockSpec((block, cols), lambda i: (i, 0)),
        ],
        out_shape=[
            jax.ShapeDtypeStruct((slots, 2 * width), BF),
            jax.ShapeDtypeStruct((slots, cols), BF),
        ],
        compiler_params=pltpu.CompilerParams(vmem_limit_bytes=VMEM_LIMIT),
        cost_estimate=pl.CostEstimate(
            flops=slots * width * cols * 4, transcendentals=0, bytes_accessed=slots * width * 8
        ),
        name="project",
    )(x_all, scales, weight)


def self_forward_kernel(n, block, info, qkv, mixed, logs, q_s, k_s, v_s):
    limit, me_c, me_t = (jnp.max(info[i : i + 1, :]) for i in range(3))
    half = block // 2
    for c in range(n):
        for t in range(2):
            place = (me_c ^ c) * block + (me_t ^ t) * half
            place = pl.multiple_of(place, half)
            to = slice(c * block + t * half, c * block + t * half + half)
            rows = qkv[pl.ds(place, half), :]
            q_s[to, :] = rows[:, :PAIR] * jnp.asarray(HEAD_DIM**-0.5, BF)
            keys = rows[:, PAIR : 2 * PAIR]
            for h in range(2):
                k_s[h, to, :] = jnp.where(lanes_of(h, keys.shape), keys, jnp.zeros_like(keys))
            v_s[:, to] = rows[:, 2 * PAIR :].astype(F32).T.astype(BF)

    def one(i, _):
        at_q = pl.multiple_of(i * block, block)
        query = q_s[pl.ds(at_q, block), :]

        def step(masked, j, state):
            at_k = pl.multiple_of(j * block, block)
            out = []
            for h in range(2):
                top, tot, acc = state[h]
                score = nt(k_s[h, pl.ds(at_k, block), :], query)
                if masked:
                    key_at = at_k + lax.broadcasted_iota(jnp.int32, score.shape, 0)
                    slot_at = at_q + lax.broadcasted_iota(jnp.int32, score.shape, 1)
                    score = jnp.where((key_at <= slot_at) & (key_at < limit), score, LOW)
                new_top = jnp.maximum(top, jnp.max(score, axis=0, keepdims=True))
                fade = jnp.exp(top - new_top)
                chance = jnp.exp(score - new_top)
                tot = tot * fade + jnp.sum(chance, axis=0, keepdims=True)
                part = nn(
                    v_s[h * HEAD_DIM : (h + 1) * HEAD_DIM, pl.ds(at_k, block)], chance.astype(BF)
                )
                out.append((new_top, tot, acc * fade + part))
            return tuple(out)

        start = tuple(
            (
                jnp.full((1, block), LOW, F32),
                jnp.zeros((1, block), F32),
                jnp.zeros((HEAD_DIM, block), F32),
            )
            for _ in range(2)
        )
        whole = jnp.minimum(i, limit // block)
        last = jnp.minimum(i + 1, (limit + block - 1) // block)
        state = lax.fori_loop(0, whole, functools.partial(step, False), start)
        state = lax.fori_loop(whole, last, functools.partial(step, True), state)
        both = jnp.concatenate([acc / tot for _, tot, acc in state], axis=0)
        place = pl.multiple_of((me_c ^ i) * block, block)
        mixed[pl.ds(place, block), :] = both.T.astype(BF)
        for h in range(2):
            top, tot, _ = state[h]
            logs[h : h + 1, pl.ds(at_q, block)] = top + jnp.log(tot)
        return 0

    lax.fori_loop(0, n, one, 0)


def self_backward_kernel(
    n, block, info, qkv, mixed, grad, logs, grads, q_s, k_s, v_s, kt_s, d_s, delta_s, dq_s
):
    limit, me_c, me_t = (jnp.max(info[i : i + 1, :]) for i in range(3))
    half = block // 2
    for c in range(n):
        for t in range(2):
            place = (me_c ^ c) * block + (me_t ^ t) * half
            place = pl.multiple_of(place, half)
            to = slice(c * block + t * half, c * block + t * half + half)
            rows = qkv[pl.ds(place, half), :]
            q_s[to, :] = rows[:, :PAIR] * jnp.asarray(HEAD_DIM**-0.5, BF)
            keys = rows[:, PAIR : 2 * PAIR]
            values = rows[:, 2 * PAIR :]
            for h in range(2):
                k_s[h, to, :] = jnp.where(lanes_of(h, keys.shape), keys, jnp.zeros_like(keys))
                v_s[h, to, :] = jnp.where(lanes_of(h, keys.shape), values, jnp.zeros_like(keys))
            kt_s[:, to] = keys.astype(F32).T.astype(BF)
            at = pl.multiple_of((me_c ^ c) * block + t * half, half)
            dout = grad[pl.ds(at, half), :]
            d_s[to, :] = dout
            both = (dout.astype(F32) * mixed[pl.ds(at, half), :].astype(F32)).T
            for h in range(2):
                delta_s[h : h + 1, to] = jnp.sum(
                    both[h * HEAD_DIM : (h + 1) * HEAD_DIM, :], axis=0, keepdims=True
                )
    dq_s[...] = jnp.zeros_like(dq_s)

    def one(j, _):
        at_k = pl.multiple_of(j * block, block)

        def step(masked, i, state):
            at_q = pl.multiple_of(i * block, block)
            query = q_s[pl.ds(at_q, block), :]
            dout = d_s[pl.ds(at_q, block), :]
            out = []
            for h in range(2):
                dk, dv = state[h]
                score = nt(k_s[h, pl.ds(at_k, block), :], query)
                if masked:
                    key_at = at_k + lax.broadcasted_iota(jnp.int32, score.shape, 0)
                    slot_at = at_q + lax.broadcasted_iota(jnp.int32, score.shape, 1)
                    score = jnp.where((key_at <= slot_at) & (key_at < limit), score, LOW)
                chance = jnp.exp(score - logs[h : h + 1, pl.ds(at_q, block)])
                slopes = nt(v_s[h, pl.ds(at_k, block), :], dout)
                bend = (chance * (slopes - delta_s[h : h + 1, pl.ds(at_q, block)])).astype(BF)
                dv = dv + nn(chance.astype(BF), dout)
                dk = dk + nn(bend, query)
                side = slice(h * HEAD_DIM, (h + 1) * HEAD_DIM)
                dq_s[side, pl.ds(at_q, block)] += nn(kt_s[side, pl.ds(at_k, block)], bend)
                out.append((dk, dv))
            return tuple(out)

        start = tuple(
            (jnp.zeros((block, PAIR), F32), jnp.zeros((block, PAIR), F32)) for _ in range(2)
        )
        end = jnp.where(j * block < limit, n, j)
        middle = jnp.where((j + 1) * block <= limit, jnp.minimum(j + 1, end), end)
        state = lax.fori_loop(j, middle, functools.partial(step, True), start)
        state = lax.fori_loop(middle, end, functools.partial(step, False), state)
        first_head = lanes_of(0, (block, PAIR))
        dk = jnp.where(first_head, state[0][0], state[1][0]).astype(BF)
        dv = jnp.where(first_head, state[0][1], state[1][1]).astype(BF)
        for t in range(2):
            place = (me_c ^ j) * block + (me_t ^ t) * half
            place = pl.multiple_of(place, half)
            grads[pl.ds(place, half), PAIR : 2 * PAIR] = dk[t * half : (t + 1) * half, :]
            grads[pl.ds(place, half), 2 * PAIR :] = dv[t * half : (t + 1) * half, :]
        return 0

    lax.fori_loop(0, n, one, 0)
    for c in range(n):
        dq = (dq_s[:, c * block : (c + 1) * block] * HEAD_DIM**-0.5).T.astype(BF)
        for t in range(2):
            place = (me_c ^ c) * block + (me_t ^ t) * half
            place = pl.multiple_of(place, half)
            grads[pl.ds(place, half), :PAIR] = dq[t * half : (t + 1) * half, :]


def cross_scores(limit, keys, query):
    score = nt(keys, query)
    key_at = lax.broadcasted_iota(jnp.int32, score.shape, 0)
    return jnp.where(key_at < limit, score, LOW)


def masked_pair(values, head):
    return jnp.where(lanes_of(head, values.shape), values, jnp.zeros_like(values))


def cross_forward_kernel(info, query_ref, kv, mixed, logs):
    limit = info[0]
    query = query_ref[...] * jnp.asarray(HEAD_DIM**-0.5, BF)
    keys = kv[0, :, :PAIR]
    values = kv[0, :, PAIR:].astype(F32).T.astype(BF)
    outs = []
    for h in range(2):
        score = cross_scores(limit, masked_pair(keys, h), query)
        top = jnp.max(score, axis=0, keepdims=True)
        chance = jnp.exp(score - top)
        tot = jnp.sum(chance, axis=0, keepdims=True)
        outs.append(nn(values[h * HEAD_DIM : (h + 1) * HEAD_DIM, :], chance.astype(BF)) / tot)
        logs[0, h : h + 1, :] = top + jnp.log(tot)
    mixed[...] = jnp.concatenate(outs, axis=0).T.astype(BF)


def cross_backward_kernel(info, query_ref, kv, mixed, grad, logs, dq_ref, dkv):
    limit = info[0]
    query = query_ref[...] * jnp.asarray(HEAD_DIM**-0.5, BF)
    keys = kv[0, :, :PAIR]
    values = kv[0, :, PAIR:]
    keys_t = keys.astype(F32).T.astype(BF)
    dout = grad[...]
    both = (dout.astype(F32) * mixed[...].astype(F32)).T
    dqs, dks, dvs = [], [], []
    for h in range(2):
        side = slice(h * HEAD_DIM, (h + 1) * HEAD_DIM)
        delta = jnp.sum(both[side, :], axis=0, keepdims=True)
        score = cross_scores(limit, masked_pair(keys, h), query)
        chance = jnp.exp(score - logs[0, h : h + 1, :])
        slopes = nt(masked_pair(values, h), dout)
        bend = (chance * (slopes - delta)).astype(BF)
        dvs.append(nn(chance.astype(BF), dout))
        dks.append(nn(bend, query))
        dqs.append(nn(keys_t[side, :], bend))
    dq_ref[...] = (jnp.concatenate(dqs, axis=0) * HEAD_DIM**-0.5).T.astype(BF)
    first_head = lanes_of(0, dks[0].shape)
    dkv[0, :, :PAIR] = jnp.where(first_head, dks[0], dks[1]).astype(BF)
    dkv[0, :, PAIR:] = jnp.where(first_head, dvs[0], dvs[1]).astype(BF)


VMEM_LIMIT = 48 * 1024 * 1024


def vmem_spec():
    return pl.BlockSpec(memory_space=pltpu.VMEM)


def smem_spec():
    return pl.BlockSpec(memory_space=pltpu.SMEM)


def self_forward(info, qkv, n):
    slots = qkv.shape[0]
    block = slots // n
    pairs = slots * slots
    return pl.pallas_call(
        functools.partial(self_forward_kernel, n, block),
        out_shape=(
            jax.ShapeDtypeStruct((slots, PAIR), BF),
            jax.ShapeDtypeStruct((2, slots), F32),
        ),
        in_specs=[vmem_spec(), vmem_spec()],
        out_specs=(vmem_spec(), vmem_spec()),
        scratch_shapes=[
            pltpu.VMEM((slots, PAIR), BF),
            pltpu.VMEM((2, slots, PAIR), BF),
            pltpu.VMEM((PAIR, slots), BF),
        ],
        compiler_params=pltpu.CompilerParams(vmem_limit_bytes=VMEM_LIMIT),
        cost_estimate=pl.CostEstimate(
            flops=pairs * PAIR * 4, transcendentals=pairs, bytes_accessed=slots * PAIR * 8
        ),
        name="self_forward",
    )(info, qkv)


def self_backward(info, qkv, mixed, grad, logs, n):
    slots = qkv.shape[0]
    block = slots // n
    pairs = slots * slots
    return pl.pallas_call(
        functools.partial(self_backward_kernel, n, block),
        out_shape=jax.ShapeDtypeStruct((slots, 3 * PAIR), BF),
        in_specs=[vmem_spec()] + [vmem_spec()] * 4,
        out_specs=vmem_spec(),
        scratch_shapes=[
            pltpu.VMEM((slots, PAIR), BF),
            pltpu.VMEM((2, slots, PAIR), BF),
            pltpu.VMEM((2, slots, PAIR), BF),
            pltpu.VMEM((PAIR, slots), BF),
            pltpu.VMEM((slots, PAIR), BF),
            pltpu.VMEM((2, slots), F32),
            pltpu.VMEM((PAIR, slots), F32),
        ],
        compiler_params=pltpu.CompilerParams(vmem_limit_bytes=VMEM_LIMIT),
        cost_estimate=pl.CostEstimate(
            flops=pairs * PAIR * 10, transcendentals=pairs, bytes_accessed=slots * PAIR * 20
        ),
        name="self_backward",
    )(info, qkv, mixed, grad, logs)


def cross_forward(info, query, kv, n):
    rows, keys = query.shape[0], kv.shape[1]
    pairs = rows * keys * n
    grid_spec = pltpu.PrefetchScalarGridSpec(
        num_scalar_prefetch=1,
        grid=(n,),
        in_specs=[
            pl.BlockSpec((rows, PAIR), lambda j, info: (0, j)),
            pl.BlockSpec((1, keys, 2 * PAIR), lambda j, info: (info[1] ^ j, 0, 0)),
        ],
        out_specs=[
            pl.BlockSpec((rows, PAIR), lambda j, info: (0, j)),
            pl.BlockSpec((1, 2, rows), lambda j, info: (j, 0, 0)),
        ],
    )
    return pl.pallas_call(
        cross_forward_kernel,
        grid_spec=grid_spec,
        out_shape=(
            jax.ShapeDtypeStruct((rows, PAIR * n), BF),
            jax.ShapeDtypeStruct((n, 2, rows), F32),
        ),
        compiler_params=pltpu.CompilerParams(vmem_limit_bytes=VMEM_LIMIT),
        cost_estimate=pl.CostEstimate(
            flops=pairs * PAIR * 8, transcendentals=2 * pairs, bytes_accessed=rows * PAIR * n * 6
        ),
        name="cross_forward",
    )(info, query, kv)


def cross_backward(info, query, kv, mixed, grad, logs, n):
    rows, keys = query.shape[0], kv.shape[1]
    pairs = rows * keys * n
    col = pl.BlockSpec((rows, PAIR), lambda j, info: (0, j))
    grid_spec = pltpu.PrefetchScalarGridSpec(
        num_scalar_prefetch=1,
        grid=(n,),
        in_specs=[
            col,
            pl.BlockSpec((1, keys, 2 * PAIR), lambda j, info: (info[1] ^ j, 0, 0)),
            col,
            col,
            pl.BlockSpec((1, 2, rows), lambda j, info: (j, 0, 0)),
        ],
        out_specs=[
            col,
            pl.BlockSpec((1, keys, 2 * PAIR), lambda j, info: (info[1] ^ j, 0, 0)),
        ],
    )
    return pl.pallas_call(
        cross_backward_kernel,
        grid_spec=grid_spec,
        out_shape=(
            jax.ShapeDtypeStruct((rows, PAIR * n), BF),
            jax.ShapeDtypeStruct((n, keys, 2 * PAIR), BF),
        ),
        compiler_params=pltpu.CompilerParams(vmem_limit_bytes=VMEM_LIMIT),
        cost_estimate=pl.CostEstimate(
            flops=pairs * PAIR * 20, transcendentals=2 * pairs, bytes_accessed=rows * PAIR * n * 10
        ),
        name="cross_backward",
    )(info, query, kv, mixed, grad, logs)


def tp_total(partial):
    mine = partial.astype(BF)
    return mine.astype(F32) + swap(mine).astype(F32)


def tp_join(mine):
    me = lax.axis_index("tp")
    other = swap(mine)
    return jnp.concatenate(
        [jnp.where(me == 0, mine, other), jnp.where(me == 0, other, mine)], axis=0
    )


def body(
    inputs,
    encoder_states,
    seq_lengths,
    enc_lengths,
    cotangent,
    norm_gains,
    norm_biases,
    w_query,
    w_key,
    w_value,
    w_out,
    w_cross_query,
    w_cross_key,
    w_cross_value,
    w_cross_out,
    w_inner,
    w_outer,
):
    n, f = lax.axis_size("ctx"), lax.axis_size("fsdp")
    me_c, me_t = lax.axis_index("ctx"), lax.axis_index("tp")
    rows, width = inputs.shape[1], inputs.shape[2]
    half = rows // 2
    wide = w_query.shape[1]
    shard = w_query.shape[0]
    seq_limit, enc_limit = seq_lengths[0], enc_lengths[0]
    self_info = jnp.stack([seq_limit, me_c, me_t] + [seq_limit] * 5).astype(jnp.int32)
    self_info = jnp.broadcast_to(self_info[:, None], (8, 128))
    cross_info = jnp.stack([enc_limit, me_c, me_t]).astype(jnp.int32)

    enc_half = encoder_states.shape[1] // 2

    def side(t):
        return jnp.concatenate(
            [
                lax.dynamic_slice_in_dim(inputs[0], t * half, half, 0),
                lax.dynamic_slice_in_dim(encoder_states[0], t * enc_half, enc_half, 0),
            ],
            axis=0,
        )

    five = jnp.stack([w_query, w_key, w_value, w_cross_key, w_cross_value], axis=1)
    five = five.reshape(shard, 5, n, PAIR).transpose(2, 0, 1, 3).reshape(n, shard, 5 * PAIR)
    params = jnp.concatenate([norm_gains, norm_biases], axis=0).reshape(1, 1, 8 * shard)
    params = jnp.pad(params, ((0, 0), (0, 15), (0, 5 * PAIR - 8 * shard)))
    five = jnp.concatenate([five, jnp.broadcast_to(params, (n,) + params.shape[1:])], axis=1)
    five = natural(exchange_direct(five, "ctx"), "ctx")
    in_z = Gathering(w_inner, "ctx", False)
    in_seen = [in_z.start()]
    five = gather_direct(five, "fsdp")
    while len(in_z.order) > 1:
        in_seen.append(in_z.step())

    seen_x = []
    mine_rows = gather_offsets(tie(side(me_t), in_seen[0]), "ctx", False, seen_x, in_seen[-1])
    w_in = Doubling(in_z.end())

    w_three = jnp.concatenate([w_out.T, w_cross_query, w_cross_out.T], axis=1)
    three_z = Gathering(w_three, "ctx", False)
    three_z.start(seen_x[0])
    in_first = w_in.came
    while len(w_in.parts[0].order) > 1:
        w_in.step(seen_x[0])
    while len(three_z.order) > 1:
        three_z.step()
    outer_z = Gathering(w_outer.T, "ctx", False)
    outer_z.start(seen_x[-1])

    w_three = Doubling(three_z.end())
    came_rows = swap(tie(jnp.concatenate(mine_rows[1:], axis=0), *in_first, *w_in.came))
    size = half + enc_half
    five = five.reshape(f * n, shard + 16, 5 * PAIR)
    params = five[:, shard, : 8 * shard].reshape(f * n, 8, shard)
    params = params.transpose(1, 0, 2).reshape(8, width).astype(F32)
    gains, biases = params[:4], params[4:]
    five = five[:, :shard].reshape(width, 5 * PAIR)
    w_qkv, w_ckv = five[:, : 3 * PAIR], five[:, 3 * PAIR :]
    their_rows = [side(1 - me_t)] + [came_rows[k * size : (k + 1) * size] for k in range(n - 1)]
    x_all = jnp.concatenate([v[:half] for k in range(n) for v in (mine_rows[k], their_rows[k])])
    enc_found = [[v[half:] for v in (mine_rows[k], their_rows[k])] for k in range(n)]
    enc_at = [[lax.select_n(me_t, e[0], e[1]), lax.select_n(me_t, e[1], e[0])] for e in enc_found]
    enc_all = natural([jnp.concatenate(e, axis=0) for e in enc_at], "ctx")
    ckv_own = nn(enc_all, w_ckv).astype(BF)
    seen_ckv = []
    ckv = jnp.stack(gather_offsets(ckv_own, "ctx", False, seen_ckv), axis=0)

    scales = jnp.concatenate([gains[:1], biases[:1]], axis=0)
    kept, qkv = project(tie(x_all, ckv_own), scales, w_qkv)
    three_first = w_three.came
    while len(w_three.parts[0].order) > 1:
        w_three.step(came_rows)
    while len(outer_z.order) > 1:
        outer_z.step(came_rows)
    mixed, logs = self_forward(
        self_info, tie(qkv, *three_first, *w_in.came, seen_ckv[0]), n
    )
    outer_z.came = tie(outer_z.came, mixed)
    w_outer_t = Doubling(outer_z.end())
    mixed_out = tie(mixed, *w_three.came)
    w_in = w_in.end(mixed_out)
    w_three = w_three.end(mixed_out)
    w_out_t, w_cq, w_co_t = w_three[:, :wide], w_three[:, wide : 2 * wide], w_three[:, 2 * wide :]
    pieces = [mixed_out[:rows]]
    pieces += [flip(mixed_out[k * rows : (k + 1) * rows], "ctx", k) for k in range(1, n)]
    attn_flat = natural(pieces, "ctx", 1)
    while len(w_outer_t.parts[0].order) > 1:
        w_outer_t.step(attn_flat)
    hidden_x = inputs[0].astype(F32)
    first = hidden_x + tp_total(nt(attn_flat, w_out_t))

    normed_c, scale_c = norm_parts(first)
    cross_in = (normed_c * gains[1] + biases[1]).astype(BF)
    cross_query = nn(cross_in, w_cq).astype(BF)
    cross_flat, cross_logs = cross_forward(cross_info, cross_query, ckv, n)
    second = first + tp_total(nt(cross_flat, w_co_t))

    w_outer_t = w_outer_t.end(cross_flat)
    normed_f, scale_f = norm_parts(second)
    ffn_in = (normed_f * gains[2] + biases[2]).astype(BF)
    inner = nn(ffn_in, w_in)
    gated, gate_pullback = jax.vjp(smooth_gate, inner)
    active = gated.astype(BF)
    third = second + tp_total(nt(active, w_outer_t))

    positions = me_c * rows + lax.iota(jnp.int32, rows)
    valid = (positions < seq_limit).astype(F32)[:, None]
    normed_y, scale_y = norm_parts(third)
    output = (normed_y * gains[3] + biases[3]) * valid

    grad_y = cotangent[0].astype(F32) * valid
    grad_third, gain_y, bias_y = norm_back(grad_y, normed_y, scale_y, gains[3])
    g3 = grad_third.astype(BF)
    outer = Halving([(g3, active)])
    outer.launch()
    grad_active = gate_pullback(nn(g3, w_outer_t))[0].astype(BF)
    partial = nt(grad_active, w_in).astype(BF)
    inside = Halving([(tie(ffn_in, partial), grad_active)])
    grad_ffn_in = partial.astype(F32) + swap(partial).astype(F32)
    part_f, gain_f, bias_f = norm_back(grad_ffn_in, normed_f, scale_f, gains[2])
    grad_second = grad_third + part_f
    g2 = grad_second.astype(BF)

    grad_cross = nn(g2, w_co_t).astype(BF)
    grad_cq, dkv = cross_backward(
        cross_info,
        cross_query,
        ckv,
        cross_flat,
        tie(grad_cross, *outer.held(), inside.keep, inside.away),
        cross_logs,
        n,
    )
    partial = nt(grad_cq, w_cq).astype(BF)
    grad_cross_in = partial.astype(F32) + swap(partial).astype(F32)
    part_c, gain_c, bias_c = norm_back(grad_cross_in, normed_c, scale_c, gains[1])
    grad_first = grad_second + part_c
    g1 = grad_first.astype(BF)
    inside.launch(g1, *outer.flight())
    outer.step(g1)

    grad_attn = nn(g1, w_out_t).astype(BF)
    grad_attn = grad_attn.reshape(rows, n, PAIR).transpose(1, 0, 2)
    token = gate(grad_attn[0])
    dmixed = exchange_direct(grad_attn, "ctx")
    three = Halving([(tie(g1, token), attn_flat), (cross_in, grad_cq), (g2, cross_flat)])
    seen_dkv = []
    grad_ckv = scatter_offsets([tie(dkv, token)[k] for k in range(n)], "ctx", seen_dkv).astype(BF)

    dmixed = tie(jnp.concatenate(dmixed, axis=0), three.keep, three.away, *outer.held())
    dqkv = self_backward(self_info, qkv, mixed, dmixed, logs, n)

    part = nt(tie(dqkv, *outer.flight()), w_qkv).astype(BF)
    enc_part = nt(grad_ckv, w_ckv).astype(BF)

    def block(k, u):
        place = ((me_c ^ k) * 2 + (me_t ^ u)) * enc_half
        return jnp.concatenate(
            [
                part[(2 * k + u) * half : (2 * k + u + 1) * half],
                lax.dynamic_slice_in_dim(enc_part, place, enc_half, 0),
            ],
            axis=0,
        )

    away = jnp.concatenate([block(k, 1) for k in range(n)], axis=0)
    came_part = swap(away)
    outer.step(away)
    inside.step(away)
    came_part = tie(came_part, *outer.held())
    part = [
        (
            block(k, 0).astype(F32) + came_part[k * size : (k + 1) * size].astype(F32)
        ).astype(BF)
        for k in range(n)
    ]
    dqkv_late = tie(dqkv, *part)
    order = bits_of("ctx", True)
    held, sent = dict(enumerate(part)), []
    for place, bit in enumerate(order):
        away = [held[k] for k in sorted(held) if k >> bit & 1]
        came = flip(away[0] if len(away) == 1 else jnp.concatenate(away, axis=0), "ctx", 1 << bit)
        if place == 0:
            both = tn(kept, dqkv_late)
            gain_a = jnp.sum(both[width:] * w_qkv.astype(F32), axis=1)
            bias_a = nt(jnp.sum(dqkv_late.astype(F32), axis=0, keepdims=True), w_qkv.astype(F32))[0]
            norm_grads = jnp.stack(
                [gain_a, 0.5 * gain_c, 0.5 * gain_f, 0.5 * gain_y]
                + [bias_a, 0.5 * bias_c, 0.5 * bias_f, 0.5 * bias_y]
            )
            norm_grads = norm_grads + swap(norm_grads)
            norm_grads = norm_grads.reshape(8, f * n, shard).transpose(1, 0, 2)
            norm_grads = norm_grads.reshape(f * n, 1, 8 * shard)
            norm_grads = jnp.pad(norm_grads, ((0, 0), (0, 15), (0, 5 * PAIR - 8 * shard)))
            dfive = jnp.concatenate([both[:width], tn(enc_all, grad_ckv)], axis=1)
            dfive = dfive.reshape(f * n, shard, 5 * PAIR)
            dfive = jnp.concatenate([dfive, norm_grads], axis=1).astype(BF)
            dfive = dfive.reshape(f * n * (shard + 16), 5 * PAIR)
            dfive = scatter_value(dfive, [("fsdp", True)])
            three.launch(part[0], *inside.flight())
            fill = [dfive.held]
        elif place == 1:
            inside.step(sent[0])
            for leg in outer.parts:
                leg.came = tie(leg.came, sent[0])
                while leg.legs:
                    leg.step()
            while dfive.legs:
                dfive.came = tie(dfive.came, sent[0])
                dfive.step()
            three.step(sent[0])
            fill = [dfive.held, *outer.held(), *inside.held(), *three.held()]
        else:
            fill = []
        came = tie(came, *fill)
        sent.append(came)
        held = {k: v for k, v in held.items() if not k >> bit & 1}
        for at, k in enumerate(sorted(held)):
            held[k] = held[k].astype(F32) + came[at * size : (at + 1) * size].astype(F32)
            if place < len(order) - 1:
                held[k] = held[k].astype(BF)
    grad_attn_in = held[0]

    three.step(grad_attn_in)
    before = [grad_attn_in]
    for leg in inside.parts + three.parts:
        leg.came = tie(leg.came, *before)
        while leg.legs:
            leg.step()
        before.append(leg.held)
    outer_sum = outer.end(*before)
    three, last = three.end(), three.held()
    grad_outer, grad_inner = outer_sum.T, inside.end(*last)
    dfive = dfive.end().astype(BF).reshape(n, shard + 16, 5 * PAIR)
    dfive = lax.all_to_all(dfive, "ctx", 0, 0, tiled=False)
    norm_grads = jnp.sum(dfive[:, shard, : 8 * shard].astype(F32), axis=0).reshape(8, shard)
    dfive = dfive[:, :shard].reshape(n, shard, 5, PAIR).transpose(2, 1, 0, 3)
    dfive = dfive.reshape(5, shard, wide).astype(F32)

    def mine(values):
        return lax.dynamic_slice_in_dim(values, me_t * half, half, 0)

    normed_a, scale_a = norm_parts(mine(hidden_x))
    part_a, _, _ = norm_back(grad_attn_in[:half], normed_a, scale_a, gains[0])
    ours = jnp.concatenate([mine(grad_first) + part_a, grad_attn_in[half:]], axis=0)
    theirs = swap(ours)

    def joined(low, high):
        pair = [ours[low:high], theirs[low:high]]
        return jnp.concatenate(
            [jnp.where(me_t == 0, pair[0], pair[1]), jnp.where(me_t == 0, pair[1], pair[0])], axis=0
        )

    grad_inputs, grad_encoder = joined(0, half), joined(half, size)

    return (
        output[None],
        grad_inputs[None],
        grad_encoder[None],
        norm_grads[:4],
        norm_grads[4:],
        dfive[0],
        dfive[1],
        dfive[2],
        three[:, :wide].T,
        three[:, wide : 2 * wide],
        dfive[3],
        dfive[4],
        three[:, 2 * wide :].T,
        grad_inner,
        grad_outer,
    )


def solution(mesh):
    tokens = P("fsdp", "ctx", None)
    norms = P(None, ("fsdp", "ctx"))
    by_rows = P(("fsdp", "ctx"), "tp")
    by_cols = P("tp", ("fsdp", "ctx"))
    return jax.shard_map(
        body,
        mesh=mesh,
        in_specs=(
            tokens,
            tokens,
            P("fsdp"),
            P("fsdp"),
            tokens,
            norms,
            norms,
            by_rows,
            by_rows,
            by_rows,
            by_cols,
            by_rows,
            by_rows,
            by_rows,
            by_cols,
            by_rows,
            by_cols,
        ),
        out_specs=(
            tokens,
            tokens,
            tokens,
            norms,
            norms,
            by_rows,
            by_rows,
            by_rows,
            by_cols,
            by_rows,
            by_rows,
            by_rows,
            by_cols,
            by_rows,
            by_cols,
        ),
        check_vma=False,
    )
```

```python
import functools

import jax
import jax.numpy as jnp
from jax import lax
from jax.experimental import pallas as pl
from jax.experimental.pallas import tpu as pltpu
from jax.sharding import PartitionSpec as P

HEAD_DIM = 64
PAIR = 2 * HEAD_DIM
EPS = 1e-05
GELU_A = 0.7978845608028654
GELU_B = 0.044715
BF = jnp.bfloat16
F32 = jnp.float32
LOW = -1e30


def nn(left, right):
    return jnp.dot(left, right, preferred_element_type=F32)


def tn(left, right):
    return lax.dot_general(left, right, (((0,), (0,)), ((), ())), preferred_element_type=F32)


def nt(left, right):
    return lax.dot_general(left, right, (((1,), (1,)), ((), ())), preferred_element_type=F32)


def smooth_gate(values):
    return 0.5 * values * (1.0 + jnp.tanh(GELU_A * (values + GELU_B * values * values * values)))


def norm_parts(values):
    mean = jnp.mean(values, axis=-1, keepdims=True)
    centred = values - mean
    scale = lax.rsqrt(jnp.mean(centred * centred, axis=-1, keepdims=True) + EPS)
    return (centred * scale, scale)


def norm_back(grad_result, normed, scale, gain):
    grad_normed = grad_result * gain
    grad_input = scale * (
        grad_normed
        - jnp.mean(grad_normed, axis=-1, keepdims=True)
        - normed * jnp.mean(grad_normed * normed, axis=-1, keepdims=True)
    )
    return (grad_input, jnp.sum(grad_result * normed, axis=0), jnp.sum(grad_result, axis=0))


def flip(value, axis, mask):
    n = lax.axis_size(axis)
    return lax.ppermute(value, axis, [(i, i ^ mask) for i in range(n)])


def swap(value):
    return flip(value, "tp", 1)


def tie(value, *others):
    token = lax.optimization_barrier((lax.create_token(),) + others)[0]
    return lax.optimization_barrier((token, value))[1]


def gate(value):
    return swap(value[:16, :PAIR])


def bits_of(axis, low_first):
    n = lax.axis_size(axis)
    order = list(range(n.bit_length() - 1))
    return order if low_first else order[::-1]


def bit_at(axis, bit):
    return (lax.axis_index(axis) >> bit) & 1


class Gathering:
    def __init__(self, value, axis, low_first):
        self.axis, self.order = axis, bits_of(axis, low_first)
        self.blocks, self.came = {0: value}, None

    def start(self, *others):
        bit = self.order[0]
        keys = sorted(self.blocks)
        sent = [self.blocks[k] for k in keys]
        sent = sent[0] if len(sent) == 1 else jnp.concatenate(sent, axis=0)
        if others:
            sent = tie(sent, *others)
        self.came = flip(sent, self.axis, 1 << bit)
        return self.came

    def join(self):
        bit = self.order.pop(0)
        mine = bit_at(self.axis, bit)
        keys = sorted(self.blocks)
        rows = self.came.shape[0] // len(keys)
        blocks = {}
        for place, k in enumerate(keys):
            held, other = self.blocks[k], self.came[place * rows : (place + 1) * rows]
            blocks[k] = jnp.where(mine == 0, held, other)
            blocks[k | 1 << bit] = jnp.where(mine == 0, other, held)
        self.blocks = blocks

    def step(self, *others):
        self.join()
        return self.start(*others)

    def end(self):
        self.join()
        return jnp.concatenate([self.blocks[k] for k in sorted(self.blocks)], axis=0)


class Doubling:
    def __init__(self, value, *others):
        cut = value.shape[0] // 2
        self.parts = [
            Gathering(value[:cut], "fsdp", True),
            Gathering(value[cut:], "fsdp", False),
        ]
        self.start(*others)

    def start(self, *others):
        self.came = [g.start(*others) for g in self.parts]

    def after(self, *others):
        for g in self.parts:
            g.came = tie(g.came, *others)

    def step(self, *others):
        self.after(*others)
        for g in self.parts:
            g.join()
        self.start()

    def end(self, *others):
        self.after(*others)
        for g in self.parts:
            g.join()
        keys = sorted(self.parts[0].blocks)
        return jnp.concatenate([g.blocks[k] for k in keys for g in self.parts], axis=0)


def gather_offsets(value, axis, low_first, seen=None, late=None):
    found = {0: value}
    order = bits_of(axis, low_first)
    for bit in order:
        keys = sorted(found)
        sent = [found[k] for k in keys]
        sent = sent[0] if len(sent) == 1 else jnp.concatenate(sent, axis=0)
        if late is not None and bit == order[-1]:
            sent = tie(sent, late)
        came = flip(sent, axis, 1 << bit)
        rows = value.shape[0]
        if seen is not None:
            seen.append(came)
        for place, k in enumerate(keys):
            found[k ^ (1 << bit)] = came[place * rows : (place + 1) * rows]
    return [found[k] for k in range(lax.axis_size(axis))]


def natural(pieces, axis, dim=0):
    n = len(pieces)
    me = lax.axis_index(axis)
    return jnp.concatenate(
        [lax.select_n(me, *[pieces[j ^ m] for m in range(n)]) for j in range(n)], axis=dim
    )


def gather_direct(value, axis):
    n = lax.axis_size(axis)
    return natural([value] + [flip(value, axis, k) for k in range(1, n)], axis)


def exchange_direct(blocks, axis):
    me = lax.axis_index(axis)
    out = [lax.dynamic_index_in_dim(blocks, me ^ k, 0, keepdims=False) for k in range(len(blocks))]
    return out[:1] + [flip(out[k], axis, k) for k in range(1, len(blocks))]


def half_rows(held, index, bit, bits):
    rows = held.shape[0] // 2
    if bits[0] == bit:
        return lax.dynamic_slice_in_dim(held, index * rows, rows, 0)
    before = 1 << bits.index(bit)
    view = held.reshape(before, 2, rows // before, held.shape[1])
    return lax.dynamic_slice_in_dim(view, index, 1, 1).reshape(rows, held.shape[1])


class Scattering:
    def __init__(self, legs, away, held, bits, first):
        self.legs = [(axis, bit) for axis, low in legs for bit in bits_of(axis, low)][1:]
        self.bits = [b for b in bits if b != first]
        self.held, self.axis = held, legs[0][0]
        self.came = flip(away, legs[0][0], 1 << first)

    def step(self):
        axis, bit = self.legs.pop(0)
        if axis != self.axis:
            self.axis, self.bits = axis, bits_of(axis, False)
        mine = bit_at(axis, bit)

        def part(index):
            held = half_rows(self.held, index, bit, self.bits).astype(F32)
            return (held + half_rows(self.came, index, bit, self.bits).astype(F32)).astype(BF)

        away, held = part(1 - mine), part(mine)
        self.bits = [b for b in self.bits if b != bit]
        self.came, self.held = flip(away, axis, 1 << bit), held

    def end(self):
        return self.held.astype(F32) + self.came.astype(F32)


def scatter_value(value, legs):
    axis, low = legs[0]
    bit, bits = bits_of(axis, low)[0], bits_of(axis, False)
    mine = bit_at(axis, bit)
    return Scattering(
        legs, half_rows(value, 1 - mine, bit, bits), half_rows(value, mine, bit, bits), bits, bit
    )


class Halving:
    def __init__(self, pairs):
        n = lax.axis_size("fsdp")
        bits = bits_of("fsdp", False)
        firsts = [bits_of("fsdp", True)[0], bits_of("fsdp", False)[0]]

        def product(flipped):
            out = []
            for left, right in pairs:
                rows = left.shape[1] // n
                cut = rows // 2
                chosen = []
                for place, bit in enumerate(firsts):
                    index = bit_at("fsdp", bit) ^ flipped
                    sides = [
                        jnp.concatenate(
                            [
                                left[:, b * rows + place * cut : b * rows + (place + 1) * cut]
                                for b in range(n)
                                if b >> bit & 1 == v
                            ],
                            axis=1,
                        )
                        for v in range(2)
                    ]
                    chosen.append(jnp.where(index == 0, sides[0], sides[1]))
                out.append(tn(jnp.concatenate(chosen, axis=1), right).astype(BF))
            return out[0] if len(out) == 1 else jnp.concatenate(out, axis=1)

        self.away, self.keep = product(1), product(0)
        self.bits, self.firsts = bits, firsts
        self.ctx = False

    def launch(self, *others):
        away, keep = tie(self.away, *others) if others else self.away, self.keep
        cut = away.shape[0] // 2
        self.parts = [
            Scattering(
                [("fsdp", low)],
                away[place * cut : (place + 1) * cut],
                keep[place * cut : (place + 1) * cut],
                self.bits,
                self.firsts[place],
            )
            for place, low in enumerate((True, False))
        ]

    def after(self, *others):
        for p in self.parts:
            p.came = tie(p.came, *others)

    def flight(self):
        return [p.came for p in self.parts]

    def held(self):
        return [p.held for p in self.parts]

    def over(self):
        return not self.parts[0].legs

    def step(self, *others):
        if others:
            self.after(*others)
        if not self.over():
            while not self.over():
                for p in self.parts:
                    p.step()
        elif not self.ctx:
            value = jnp.concatenate([p.end().astype(BF) for p in self.parts], axis=0)
            self.parts, self.ctx = [scatter_value(value, [("ctx", True)])], True

    def end(self, *others):
        if others:
            self.after(*others)
        return self.parts[0].end()


def scatter_offsets(pieces, axis, seen=None):
    n = lax.axis_size(axis)
    held = dict(enumerate(pieces))
    for bit in bits_of(axis, True):
        last = n == 2 << bit
        away = [held[k].astype(BF) for k in sorted(held) if k >> bit & 1]
        came = flip(away[0] if len(away) == 1 else jnp.concatenate(away, axis=0), axis, 1 << bit)
        rows = pieces[0].shape[0]
        if seen is not None:
            seen.append(came)
        held = {k: v for k, v in held.items() if not k >> bit & 1}
        for place, k in enumerate(sorted(held)):
            held[k] = held[k].astype(F32) + came[place * rows : (place + 1) * rows].astype(F32)
            if not last:
                held[k] = held[k].astype(BF)
    return held[0]


def lanes_of(head, shape):
    lane = lax.broadcasted_iota(jnp.int32, shape, len(shape) - 1)
    return (lane // HEAD_DIM) == head


def project_kernel(x_ref, scales, weight, kept, out):
    x = x_ref[...].astype(F32)
    width = x.shape[1]
    centred = x - jnp.sum(x, axis=1, keepdims=True) * (1.0 / width)
    spread = jnp.sum(centred * centred, axis=1, keepdims=True) * (1.0 / width)
    normed = centred * lax.rsqrt(spread + EPS)
    attn_in = (normed * scales[0:1, :] + scales[1:2, :]).astype(BF)
    kept[:, :width] = attn_in
    kept[:, width:] = normed.astype(BF)
    out[...] = nn(attn_in, weight[...]).astype(BF)


def project(x_all, scales, weight):
    slots, width = x_all.shape
    cols = weight.shape[1]
    block = min(256, slots)
    return pl.pallas_call(
        project_kernel,
        grid=(slots // block,),
        in_specs=[
            pl.BlockSpec((block, width), lambda i: (i, 0)),
            pl.BlockSpec((2, width), lambda i: (0, 0)),
            pl.BlockSpec((width, cols), lambda i: (0, 0)),
        ],
        out_specs=[
            pl.BlockSpec((block, 2 * width), lambda i: (i, 0)),
            pl.BlockSpec((block, cols), lambda i: (i, 0)),
        ],
        out_shape=[
            jax.ShapeDtypeStruct((slots, 2 * width), BF),
            jax.ShapeDtypeStruct((slots, cols), BF),
        ],
        compiler_params=pltpu.CompilerParams(vmem_limit_bytes=VMEM_LIMIT),
        cost_estimate=pl.CostEstimate(
            flops=slots * width * cols * 4, transcendentals=0, bytes_accessed=slots * width * 8
        ),
        name="project",
    )(x_all, scales, weight)


def self_forward_kernel(n, block, info, qkv, mixed, logs, q_s, k_s, v_s):
    limit, me_c, me_t = (jnp.max(info[i : i + 1, :]) for i in range(3))
    half = block // 2
    for c in range(n):
        for t in range(2):
            place = (me_c ^ c) * block + (me_t ^ t) * half
            place = pl.multiple_of(place, half)
            to = slice(c * block + t * half, c * block + t * half + half)
            rows = qkv[pl.ds(place, half), :]
            q_s[to, :] = rows[:, :PAIR] * jnp.asarray(HEAD_DIM**-0.5, BF)
            keys = rows[:, PAIR : 2 * PAIR]
            for h in range(2):
                k_s[h, to, :] = jnp.where(lanes_of(h, keys.shape), keys, jnp.zeros_like(keys))
            v_s[:, to] = rows[:, 2 * PAIR :].astype(F32).T.astype(BF)

    def one(i, _):
        at_q = pl.multiple_of(i * block, block)
        query = q_s[pl.ds(at_q, block), :]

        def step(masked, j, state):
            at_k = pl.multiple_of(j * block, block)
            out = []
            for h in range(2):
                top, tot, acc = state[h]
                score = nt(k_s[h, pl.ds(at_k, block), :], query)
                if masked:
                    key_at = at_k + lax.broadcasted_iota(jnp.int32, score.shape, 0)
                    slot_at = at_q + lax.broadcasted_iota(jnp.int32, score.shape, 1)
                    score = jnp.where((key_at <= slot_at) & (key_at < limit), score, LOW)
                new_top = jnp.maximum(top, jnp.max(score, axis=0, keepdims=True))
                fade = jnp.exp(top - new_top)
                chance = jnp.exp(score - new_top)
                tot = tot * fade + jnp.sum(chance, axis=0, keepdims=True)
                part = nn(
                    v_s[h * HEAD_DIM : (h + 1) * HEAD_DIM, pl.ds(at_k, block)], chance.astype(BF)
                )
                out.append((new_top, tot, acc * fade + part))
            return tuple(out)

        start = tuple(
            (
                jnp.full((1, block), LOW, F32),
                jnp.zeros((1, block), F32),
                jnp.zeros((HEAD_DIM, block), F32),
            )
            for _ in range(2)
        )
        whole = jnp.minimum(i, limit // block)
        last = jnp.minimum(i + 1, (limit + block - 1) // block)
        state = lax.fori_loop(0, whole, functools.partial(step, False), start)
        state = lax.fori_loop(whole, last, functools.partial(step, True), state)
        both = jnp.concatenate([acc / tot for _, tot, acc in state], axis=0)
        place = pl.multiple_of((me_c ^ i) * block, block)
        mixed[pl.ds(place, block), :] = both.T.astype(BF)
        for h in range(2):
            top, tot, _ = state[h]
            logs[h : h + 1, pl.ds(at_q, block)] = top + jnp.log(tot)
        return 0

    lax.fori_loop(0, n, one, 0)


def self_backward_kernel(
    n, block, info, qkv, mixed, grad, logs, grads, q_s, k_s, v_s, kt_s, d_s, delta_s, dq_s
):
    limit, me_c, me_t = (jnp.max(info[i : i + 1, :]) for i in range(3))
    half = block // 2
    for c in range(n):
        for t in range(2):
            place = (me_c ^ c) * block + (me_t ^ t) * half
            place = pl.multiple_of(place, half)
            to = slice(c * block + t * half, c * block + t * half + half)
            rows = qkv[pl.ds(place, half), :]
            q_s[to, :] = rows[:, :PAIR] * jnp.asarray(HEAD_DIM**-0.5, BF)
            keys = rows[:, PAIR : 2 * PAIR]
            values = rows[:, 2 * PAIR :]
            for h in range(2):
                k_s[h, to, :] = jnp.where(lanes_of(h, keys.shape), keys, jnp.zeros_like(keys))
                v_s[h, to, :] = jnp.where(lanes_of(h, keys.shape), values, jnp.zeros_like(keys))
            kt_s[:, to] = keys.astype(F32).T.astype(BF)
            at = pl.multiple_of((me_c ^ c) * block + t * half, half)
            dout = grad[pl.ds(at, half), :]
            d_s[to, :] = dout
            both = (dout.astype(F32) * mixed[pl.ds(at, half), :].astype(F32)).T
            for h in range(2):
                delta_s[h : h + 1, to] = jnp.sum(
                    both[h * HEAD_DIM : (h + 1) * HEAD_DIM, :], axis=0, keepdims=True
                )
    dq_s[...] = jnp.zeros_like(dq_s)

    def one(j, _):
        at_k = pl.multiple_of(j * block, block)

        def step(masked, i, state):
            at_q = pl.multiple_of(i * block, block)
            query = q_s[pl.ds(at_q, block), :]
            dout = d_s[pl.ds(at_q, block), :]
            out = []
            for h in range(2):
                dk, dv = state[h]
                score = nt(k_s[h, pl.ds(at_k, block), :], query)
                if masked:
                    key_at = at_k + lax.broadcasted_iota(jnp.int32, score.shape, 0)
                    slot_at = at_q + lax.broadcasted_iota(jnp.int32, score.shape, 1)
                    score = jnp.where((key_at <= slot_at) & (key_at < limit), score, LOW)
                chance = jnp.exp(score - logs[h : h + 1, pl.ds(at_q, block)])
                slopes = nt(v_s[h, pl.ds(at_k, block), :], dout)
                bend = (chance * (slopes - delta_s[h : h + 1, pl.ds(at_q, block)])).astype(BF)
                dv = dv + nn(chance.astype(BF), dout)
                dk = dk + nn(bend, query)
                side = slice(h * HEAD_DIM, (h + 1) * HEAD_DIM)
                dq_s[side, pl.ds(at_q, block)] += nn(kt_s[side, pl.ds(at_k, block)], bend)
                out.append((dk, dv))
            return tuple(out)

        start = tuple(
            (jnp.zeros((block, PAIR), F32), jnp.zeros((block, PAIR), F32)) for _ in range(2)
        )
        end = jnp.where(j * block < limit, n, j)
        middle = jnp.where((j + 1) * block <= limit, jnp.minimum(j + 1, end), end)
        state = lax.fori_loop(j, middle, functools.partial(step, True), start)
        state = lax.fori_loop(middle, end, functools.partial(step, False), state)
        first_head = lanes_of(0, (block, PAIR))
        dk = jnp.where(first_head, state[0][0], state[1][0]).astype(BF)
        dv = jnp.where(first_head, state[0][1], state[1][1]).astype(BF)
        for t in range(2):
            place = (me_c ^ j) * block + (me_t ^ t) * half
            place = pl.multiple_of(place, half)
            grads[pl.ds(place, half), PAIR : 2 * PAIR] = dk[t * half : (t + 1) * half, :]
            grads[pl.ds(place, half), 2 * PAIR :] = dv[t * half : (t + 1) * half, :]
        return 0

    lax.fori_loop(0, n, one, 0)
    for c in range(n):
        dq = (dq_s[:, c * block : (c + 1) * block] * HEAD_DIM**-0.5).T.astype(BF)
        for t in range(2):
            place = (me_c ^ c) * block + (me_t ^ t) * half
            place = pl.multiple_of(place, half)
            grads[pl.ds(place, half), :PAIR] = dq[t * half : (t + 1) * half, :]


def cross_scores(limit, keys, query):
    score = nt(keys, query)
    key_at = lax.broadcasted_iota(jnp.int32, score.shape, 0)
    return jnp.where(key_at < limit, score, LOW)


def masked_pair(values, head):
    return jnp.where(lanes_of(head, values.shape), values, jnp.zeros_like(values))


def cross_forward_kernel(info, query_ref, kv, mixed, logs):
    limit = info[0]
    query = query_ref[...] * jnp.asarray(HEAD_DIM**-0.5, BF)
    keys = kv[0, :, :PAIR]
    values = kv[0, :, PAIR:].astype(F32).T.astype(BF)
    outs = []
    for h in range(2):
        score = cross_scores(limit, masked_pair(keys, h), query)
        top = jnp.max(score, axis=0, keepdims=True)
        chance = jnp.exp(score - top)
        tot = jnp.sum(chance, axis=0, keepdims=True)
        outs.append(nn(values[h * HEAD_DIM : (h + 1) * HEAD_DIM, :], chance.astype(BF)) / tot)
        logs[0, h : h + 1, :] = top + jnp.log(tot)
    mixed[...] = jnp.concatenate(outs, axis=0).T.astype(BF)


def cross_backward_kernel(info, query_ref, kv, mixed, grad, logs, dq_ref, dkv):
    limit = info[0]
    query = query_ref[...] * jnp.asarray(HEAD_DIM**-0.5, BF)
    keys = kv[0, :, :PAIR]
    values = kv[0, :, PAIR:]
    keys_t = keys.astype(F32).T.astype(BF)
    dout = grad[...]
    both = (dout.astype(F32) * mixed[...].astype(F32)).T
    dqs, dks, dvs = [], [], []
    for h in range(2):
        side = slice(h * HEAD_DIM, (h + 1) * HEAD_DIM)
        delta = jnp.sum(both[side, :], axis=0, keepdims=True)
        score = cross_scores(limit, masked_pair(keys, h), query)
        chance = jnp.exp(score - logs[0, h : h + 1, :])
        slopes = nt(masked_pair(values, h), dout)
        bend = (chance * (slopes - delta)).astype(BF)
        dvs.append(nn(chance.astype(BF), dout))
        dks.append(nn(bend, query))
        dqs.append(nn(keys_t[side, :], bend))
    dq_ref[...] = (jnp.concatenate(dqs, axis=0) * HEAD_DIM**-0.5).T.astype(BF)
    first_head = lanes_of(0, dks[0].shape)
    dkv[0, :, :PAIR] = jnp.where(first_head, dks[0], dks[1]).astype(BF)
    dkv[0, :, PAIR:] = jnp.where(first_head, dvs[0], dvs[1]).astype(BF)


VMEM_LIMIT = 48 * 1024 * 1024


def vmem_spec():
    return pl.BlockSpec(memory_space=pltpu.VMEM)


def smem_spec():
    return pl.BlockSpec(memory_space=pltpu.SMEM)


def self_forward(info, qkv, n):
    slots = qkv.shape[0]
    block = slots // n
    pairs = slots * slots
    return pl.pallas_call(
        functools.partial(self_forward_kernel, n, block),
        out_shape=(
            jax.ShapeDtypeStruct((slots, PAIR), BF),
            jax.ShapeDtypeStruct((2, slots), F32),
        ),
        in_specs=[vmem_spec(), vmem_spec()],
        out_specs=(vmem_spec(), vmem_spec()),
        scratch_shapes=[
            pltpu.VMEM((slots, PAIR), BF),
            pltpu.VMEM((2, slots, PAIR), BF),
            pltpu.VMEM((PAIR, slots), BF),
        ],
        compiler_params=pltpu.CompilerParams(vmem_limit_bytes=VMEM_LIMIT),
        cost_estimate=pl.CostEstimate(
            flops=pairs * PAIR * 4, transcendentals=pairs, bytes_accessed=slots * PAIR * 8
        ),
        name="self_forward",
    )(info, qkv)


def self_backward(info, qkv, mixed, grad, logs, n):
    slots = qkv.shape[0]
    block = slots // n
    pairs = slots * slots
    return pl.pallas_call(
        functools.partial(self_backward_kernel, n, block),
        out_shape=jax.ShapeDtypeStruct((slots, 3 * PAIR), BF),
        in_specs=[vmem_spec()] + [vmem_spec()] * 4,
        out_specs=vmem_spec(),
        scratch_shapes=[
            pltpu.VMEM((slots, PAIR), BF),
            pltpu.VMEM((2, slots, PAIR), BF),
            pltpu.VMEM((2, slots, PAIR), BF),
            pltpu.VMEM((PAIR, slots), BF),
            pltpu.VMEM((slots, PAIR), BF),
            pltpu.VMEM((2, slots), F32),
            pltpu.VMEM((PAIR, slots), F32),
        ],
        compiler_params=pltpu.CompilerParams(vmem_limit_bytes=VMEM_LIMIT),
        cost_estimate=pl.CostEstimate(
            flops=pairs * PAIR * 10, transcendentals=pairs, bytes_accessed=slots * PAIR * 20
        ),
        name="self_backward",
    )(info, qkv, mixed, grad, logs)


def cross_forward(info, query, kv, n):
    rows, keys = query.shape[0], kv.shape[1]
    pairs = rows * keys * n
    grid_spec = pltpu.PrefetchScalarGridSpec(
        num_scalar_prefetch=1,
        grid=(n,),
        in_specs=[
            pl.BlockSpec((rows, PAIR), lambda j, info: (0, j)),
            pl.BlockSpec((1, keys, 2 * PAIR), lambda j, info: (info[1] ^ j, 0, 0)),
        ],
        out_specs=[
            pl.BlockSpec((rows, PAIR), lambda j, info: (0, j)),
            pl.BlockSpec((1, 2, rows), lambda j, info: (j, 0, 0)),
        ],
    )
    return pl.pallas_call(
        cross_forward_kernel,
        grid_spec=grid_spec,
        out_shape=(
            jax.ShapeDtypeStruct((rows, PAIR * n), BF),
            jax.ShapeDtypeStruct((n, 2, rows), F32),
        ),
        compiler_params=pltpu.CompilerParams(vmem_limit_bytes=VMEM_LIMIT),
        cost_estimate=pl.CostEstimate(
            flops=pairs * PAIR * 8, transcendentals=2 * pairs, bytes_accessed=rows * PAIR * n * 6
        ),
        name="cross_forward",
    )(info, query, kv)


def cross_backward(info, query, kv, mixed, grad, logs, n):
    rows, keys = query.shape[0], kv.shape[1]
    pairs = rows * keys * n
    col = pl.BlockSpec((rows, PAIR), lambda j, info: (0, j))
    grid_spec = pltpu.PrefetchScalarGridSpec(
        num_scalar_prefetch=1,
        grid=(n,),
        in_specs=[
            col,
            pl.BlockSpec((1, keys, 2 * PAIR), lambda j, info: (info[1] ^ j, 0, 0)),
            col,
            col,
            pl.BlockSpec((1, 2, rows), lambda j, info: (j, 0, 0)),
        ],
        out_specs=[
            col,
            pl.BlockSpec((1, keys, 2 * PAIR), lambda j, info: (info[1] ^ j, 0, 0)),
        ],
    )
    return pl.pallas_call(
        cross_backward_kernel,
        grid_spec=grid_spec,
        out_shape=(
            jax.ShapeDtypeStruct((rows, PAIR * n), BF),
            jax.ShapeDtypeStruct((n, keys, 2 * PAIR), BF),
        ),
        compiler_params=pltpu.CompilerParams(vmem_limit_bytes=VMEM_LIMIT),
        cost_estimate=pl.CostEstimate(
            flops=pairs * PAIR * 20, transcendentals=2 * pairs, bytes_accessed=rows * PAIR * n * 10
        ),
        name="cross_backward",
    )(info, query, kv, mixed, grad, logs)


def tp_total(partial):
    mine = partial.astype(BF)
    return mine.astype(F32) + swap(mine).astype(F32)


def tp_join(mine):
    me = lax.axis_index("tp")
    other = swap(mine)
    return jnp.concatenate(
        [jnp.where(me == 0, mine, other), jnp.where(me == 0, other, mine)], axis=0
    )


def body(
    inputs,
    encoder_states,
    seq_lengths,
    enc_lengths,
    cotangent,
    norm_gains,
    norm_biases,
    w_query,
    w_key,
    w_value,
    w_out,
    w_cross_query,
    w_cross_key,
    w_cross_value,
    w_cross_out,
    w_inner,
    w_outer,
):
    n, f = lax.axis_size("ctx"), lax.axis_size("fsdp")
    me_c, me_t = lax.axis_index("ctx"), lax.axis_index("tp")
    rows, width = inputs.shape[1], inputs.shape[2]
    half = rows // 2
    wide = w_query.shape[1]
    shard = w_query.shape[0]
    seq_limit, enc_limit = seq_lengths[0], enc_lengths[0]
    self_info = jnp.stack([seq_limit, me_c, me_t] + [seq_limit] * 5).astype(jnp.int32)
    self_info = jnp.broadcast_to(self_info[:, None], (8, 128))
    cross_info = jnp.stack([enc_limit, me_c, me_t]).astype(jnp.int32)

    enc_half = encoder_states.shape[1] // 2

    def side(t):
        return jnp.concatenate(
            [
                lax.dynamic_slice_in_dim(inputs[0], t * half, half, 0),
                lax.dynamic_slice_in_dim(encoder_states[0], t * enc_half, enc_half, 0),
            ],
            axis=0,
        )

    five = jnp.stack([w_query, w_key, w_value, w_cross_key, w_cross_value], axis=1)
    five = five.reshape(shard, 5, n, PAIR).transpose(2, 0, 1, 3).reshape(n, shard, 5 * PAIR)
    params = jnp.concatenate([norm_gains, norm_biases], axis=0).reshape(1, 1, 8 * shard)
    params = jnp.pad(params, ((0, 0), (0, 15), (0, 5 * PAIR - 8 * shard)))
    five = jnp.concatenate([five, jnp.broadcast_to(params, (n,) + params.shape[1:])], axis=1)
    five = natural(exchange_direct(five, "ctx"), "ctx")
    in_z = Gathering(w_inner, "ctx", False)
    in_seen = [in_z.start()]
    five = gather_direct(five, "fsdp")
    while len(in_z.order) > 1:
        in_seen.append(in_z.step())

    seen_x = []
    mine_rows = gather_offsets(tie(side(me_t), in_seen[0]), "ctx", False, seen_x, in_seen[-1])
    w_in = Doubling(in_z.end())

    w_three = jnp.concatenate([w_out.T, w_cross_query, w_cross_out.T], axis=1)
    three_z = Gathering(w_three, "ctx", False)
    three_z.start(seen_x[0])
    in_first = w_in.came
    while len(w_in.parts[0].order) > 1:
        w_in.step(seen_x[0])
    while len(three_z.order) > 1:
        three_z.step()
    outer_z = Gathering(w_outer.T, "ctx", False)
    outer_z.start(seen_x[-1])

    w_three = Doubling(three_z.end())
    came_rows = swap(tie(jnp.concatenate(mine_rows[1:], axis=0), *in_first, *w_in.came))
    size = half + enc_half
    five = five.reshape(f * n, shard + 16, 5 * PAIR)
    params = five[:, shard, : 8 * shard].reshape(f * n, 8, shard)
    params = params.transpose(1, 0, 2).reshape(8, width).astype(F32)
    gains, biases = params[:4], params[4:]
    five = five[:, :shard].reshape(width, 5 * PAIR)
    w_qkv, w_ckv = five[:, : 3 * PAIR], five[:, 3 * PAIR :]
    their_rows = [side(1 - me_t)] + [came_rows[k * size : (k + 1) * size] for k in range(n - 1)]
    x_all = jnp.concatenate([v[:half] for k in range(n) for v in (mine_rows[k], their_rows[k])])
    enc_found = [[v[half:] for v in (mine_rows[k], their_rows[k])] for k in range(n)]
    enc_at = [[lax.select_n(me_t, e[0], e[1]), lax.select_n(me_t, e[1], e[0])] for e in enc_found]
    enc_all = natural([jnp.concatenate(e, axis=0) for e in enc_at], "ctx")
    ckv_own = nn(enc_all, w_ckv).astype(BF)
    seen_ckv = []
    ckv = jnp.stack(gather_offsets(ckv_own, "ctx", False, seen_ckv), axis=0)

    scales = jnp.concatenate([gains[:1], biases[:1]], axis=0)
    kept, qkv = project(tie(x_all, ckv_own), scales, w_qkv)
    three_first = w_three.came
    while len(w_three.parts[0].order) > 1:
        w_three.step(came_rows)
    while len(outer_z.order) > 1:
        outer_z.step(came_rows)
    mixed, logs = self_forward(
        self_info, tie(qkv, *three_first, *w_in.came, seen_ckv[0]), n
    )
    outer_z.came = tie(outer_z.came, mixed)
    w_outer_t = Doubling(outer_z.end())
    mixed_out = tie(mixed, *w_three.came)
    w_in = w_in.end(mixed_out)
    w_three = w_three.end(mixed_out)
    w_out_t, w_cq, w_co_t = w_three[:, :wide], w_three[:, wide : 2 * wide], w_three[:, 2 * wide :]
    pieces = [mixed_out[:rows]]
    pieces += [flip(mixed_out[k * rows : (k + 1) * rows], "ctx", k) for k in range(1, n)]
    attn_flat = natural(pieces, "ctx", 1)
    while len(w_outer_t.parts[0].order) > 1:
        w_outer_t.step(attn_flat)
    hidden_x = inputs[0].astype(F32)
    first = hidden_x + tp_total(nt(attn_flat, w_out_t))

    normed_c, scale_c = norm_parts(first)
    cross_in = (normed_c * gains[1] + biases[1]).astype(BF)
    cross_query = nn(cross_in, w_cq).astype(BF)
    cross_flat, cross_logs = cross_forward(cross_info, cross_query, ckv, n)
    second = first + tp_total(nt(cross_flat, w_co_t))

    w_outer_t = w_outer_t.end(cross_flat)
    normed_f, scale_f = norm_parts(second)
    ffn_in = (normed_f * gains[2] + biases[2]).astype(BF)
    inner = nn(ffn_in, w_in)
    gated, gate_pullback = jax.vjp(smooth_gate, inner)
    active = gated.astype(BF)
    third = second + tp_total(nt(active, w_outer_t))

    positions = me_c * rows + lax.iota(jnp.int32, rows)
    valid = (positions < seq_limit).astype(F32)[:, None]
    normed_y, scale_y = norm_parts(third)
    output = (normed_y * gains[3] + biases[3]) * valid

    grad_y = cotangent[0].astype(F32) * valid
    grad_third, gain_y, bias_y = norm_back(grad_y, normed_y, scale_y, gains[3])
    g3 = grad_third.astype(BF)
    outer = Halving([(g3, active)])
    outer.launch()
    grad_active = gate_pullback(nn(g3, w_outer_t))[0].astype(BF)
    partial = nt(grad_active, w_in).astype(BF)
    inside = Halving([(tie(ffn_in, partial), grad_active)])
    grad_ffn_in = partial.astype(F32) + swap(partial).astype(F32)
    part_f, gain_f, bias_f = norm_back(grad_ffn_in, normed_f, scale_f, gains[2])
    grad_second = grad_third + part_f
    g2 = grad_second.astype(BF)

    grad_cross = nn(g2, w_co_t).astype(BF)
    grad_cq, dkv = cross_backward(
        cross_info,
        cross_query,
        ckv,
        cross_flat,
        tie(grad_cross, *outer.held(), inside.keep, inside.away),
        cross_logs,
        n,
    )
    partial = nt(grad_cq, w_cq).astype(BF)
    grad_cross_in = partial.astype(F32) + swap(partial).astype(F32)
    part_c, gain_c, bias_c = norm_back(grad_cross_in, normed_c, scale_c, gains[1])
    grad_first = grad_second + part_c
    g1 = grad_first.astype(BF)
    inside.launch(g1, *outer.flight())
    outer.step(g1)

    grad_attn = nn(g1, w_out_t).astype(BF)
    grad_attn = grad_attn.reshape(rows, n, PAIR).transpose(1, 0, 2)
    token = gate(grad_attn[0])
    dmixed = exchange_direct(grad_attn, "ctx")
    three = Halving([(tie(g1, token), attn_flat), (cross_in, grad_cq), (g2, cross_flat)])
    seen_dkv = []
    grad_ckv = scatter_offsets([tie(dkv, token)[k] for k in range(n)], "ctx", seen_dkv).astype(BF)

    dmixed = tie(jnp.concatenate(dmixed, axis=0), three.keep, three.away, *outer.held())
    dqkv = self_backward(self_info, qkv, mixed, dmixed, logs, n)

    part = nt(tie(dqkv, *outer.flight()), w_qkv).astype(BF)
    enc_part = nt(grad_ckv, w_ckv).astype(BF)

    def block(k, u):
        place = ((me_c ^ k) * 2 + (me_t ^ u)) * enc_half
        return jnp.concatenate(
            [
                part[(2 * k + u) * half : (2 * k + u + 1) * half],
                lax.dynamic_slice_in_dim(enc_part, place, enc_half, 0),
            ],
            axis=0,
        )

    away = jnp.concatenate([block(k, 1) for k in range(n)], axis=0)
    came_part = swap(away)
    outer.step(away)
    inside.step(away)
    came_part = tie(came_part, *outer.held())
    part = [
        (
            block(k, 0).astype(F32) + came_part[k * size : (k + 1) * size].astype(F32)
        ).astype(BF)
        for k in range(n)
    ]
    dqkv_late = tie(dqkv, *part)
    order = bits_of("ctx", True)
    held, sent = dict(enumerate(part)), []
    for place, bit in enumerate(order):
        away = [held[k] for k in sorted(held) if k >> bit & 1]
        came = flip(away[0] if len(away) == 1 else jnp.concatenate(away, axis=0), "ctx", 1 << bit)
        if place == 0:
            both = tn(kept, dqkv_late)
            gain_a = jnp.sum(both[width:] * w_qkv.astype(F32), axis=1)
            bias_a = nt(jnp.sum(dqkv_late.astype(F32), axis=0, keepdims=True), w_qkv.astype(F32))[0]
            norm_grads = jnp.stack(
                [gain_a, 0.5 * gain_c, 0.5 * gain_f, 0.5 * gain_y]
                + [bias_a, 0.5 * bias_c, 0.5 * bias_f, 0.5 * bias_y]
            )
            norm_grads = norm_grads + swap(norm_grads)
            norm_grads = norm_grads.reshape(8, f * n, shard).transpose(1, 0, 2)
            norm_grads = norm_grads.reshape(f * n, 1, 8 * shard)
            norm_grads = jnp.pad(norm_grads, ((0, 0), (0, 15), (0, 5 * PAIR - 8 * shard)))
            dfive = jnp.concatenate([both[:width], tn(enc_all, grad_ckv)], axis=1)
            dfive = dfive.reshape(f * n, shard, 5 * PAIR)
            dfive = jnp.concatenate([dfive, norm_grads], axis=1).astype(BF)
            dfive = dfive.reshape(f * n * (shard + 16), 5 * PAIR)
            dfive = scatter_value(dfive, [("fsdp", True)])
            three.launch(part[0], *inside.flight())
            fill = [dfive.held]
        elif place == 1:
            inside.step(sent[0])
            three.step(sent[0])
            while dfive.legs:
                dfive.came = tie(dfive.came, sent[0], *inside.held(), *three.held())
                dfive.step()
            for leg in outer.parts:
                leg.came = tie(leg.came, dfive.held)
                while leg.legs:
                    leg.step()
            fill = [dfive.held, *outer.held(), *inside.held(), *three.held()]
        else:
            fill = []
        came = tie(came, *fill)
        sent.append(came)
        held = {k: v for k, v in held.items() if not k >> bit & 1}
        for at, k in enumerate(sorted(held)):
            held[k] = held[k].astype(F32) + came[at * size : (at + 1) * size].astype(F32)
            if place < len(order) - 1:
                held[k] = held[k].astype(BF)
    grad_attn_in = held[0]

    three.step(grad_attn_in)
    before = [grad_attn_in]
    for leg in inside.parts + three.parts:
        leg.came = tie(leg.came, *before)
        while leg.legs:
            leg.step()
        before.append(leg.held)
    outer_sum = outer.end(*before)
    three, last = three.end(), three.held()
    grad_outer, grad_inner = outer_sum.T, inside.end(*last)
    dfive = dfive.end().astype(BF).reshape(n, shard + 16, 5 * PAIR)
    dfive = lax.all_to_all(dfive, "ctx", 0, 0, tiled=False)
    norm_grads = jnp.sum(dfive[:, shard, : 8 * shard].astype(F32), axis=0).reshape(8, shard)
    dfive = dfive[:, :shard].reshape(n, shard, 5, PAIR).transpose(2, 1, 0, 3)
    dfive = dfive.reshape(5, shard, wide).astype(F32)

    def mine(values):
        return lax.dynamic_slice_in_dim(values, me_t * half, half, 0)

    normed_a, scale_a = norm_parts(mine(hidden_x))
    part_a, _, _ = norm_back(grad_attn_in[:half], normed_a, scale_a, gains[0])
    ours = jnp.concatenate([mine(grad_first) + part_a, grad_attn_in[half:]], axis=0)
    theirs = swap(ours)

    def joined(low, high):
        pair = [ours[low:high], theirs[low:high]]
        return jnp.concatenate(
            [jnp.where(me_t == 0, pair[0], pair[1]), jnp.where(me_t == 0, pair[1], pair[0])], axis=0
        )

    grad_inputs, grad_encoder = joined(0, half), joined(half, size)

    return (
        output[None],
        grad_inputs[None],
        grad_encoder[None],
        norm_grads[:4],
        norm_grads[4:],
        dfive[0],
        dfive[1],
        dfive[2],
        three[:, :wide].T,
        three[:, wide : 2 * wide],
        dfive[3],
        dfive[4],
        three[:, 2 * wide :].T,
        grad_inner,
        grad_outer,
    )


def solution(mesh):
    tokens = P("fsdp", "ctx", None)
    norms = P(None, ("fsdp", "ctx"))
    by_rows = P(("fsdp", "ctx"), "tp")
    by_cols = P("tp", ("fsdp", "ctx"))
    return jax.shard_map(
        body,
        mesh=mesh,
        in_specs=(
            tokens,
            tokens,
            P("fsdp"),
            P("fsdp"),
            tokens,
            norms,
            norms,
            by_rows,
            by_rows,
            by_rows,
            by_cols,
            by_rows,
            by_rows,
            by_rows,
            by_cols,
            by_rows,
            by_cols,
        ),
        out_specs=(
            tokens,
            tokens,
            tokens,
            norms,
            norms,
            by_rows,
            by_rows,
            by_rows,
            by_cols,
            by_rows,
            by_rows,
            by_rows,
            by_cols,
            by_rows,
            by_cols,
        ),
        check_vma=False,
    )
```

```python
import functools

import jax
import jax.numpy as jnp
from jax import lax
from jax.experimental import pallas as pl
from jax.experimental.pallas import tpu as pltpu
from jax.sharding import PartitionSpec as P

HEAD_DIM = 64
PAIR = 2 * HEAD_DIM
EPS = 1e-05
GELU_A = 0.7978845608028654
GELU_B = 0.044715
BF = jnp.bfloat16
F32 = jnp.float32
LOW = -1e30


def nn(left, right):
    return jnp.dot(left, right, preferred_element_type=F32)


def tn(left, right):
    return lax.dot_general(left, right, (((0,), (0,)), ((), ())), preferred_element_type=F32)


def nt(left, right):
    return lax.dot_general(left, right, (((1,), (1,)), ((), ())), preferred_element_type=F32)


def smooth_gate(values):
    return 0.5 * values * (1.0 + jnp.tanh(GELU_A * (values + GELU_B * values * values * values)))


def norm_parts(values):
    mean = jnp.mean(values, axis=-1, keepdims=True)
    centred = values - mean
    scale = lax.rsqrt(jnp.mean(centred * centred, axis=-1, keepdims=True) + EPS)
    return (centred * scale, scale)


def norm_back(grad_result, normed, scale, gain):
    grad_normed = grad_result * gain
    grad_input = scale * (
        grad_normed
        - jnp.mean(grad_normed, axis=-1, keepdims=True)
        - normed * jnp.mean(grad_normed * normed, axis=-1, keepdims=True)
    )
    return (grad_input, jnp.sum(grad_result * normed, axis=0), jnp.sum(grad_result, axis=0))


def flip(value, axis, mask):
    n = lax.axis_size(axis)
    return lax.ppermute(value, axis, [(i, i ^ mask) for i in range(n)])


def swap(value):
    return flip(value, "tp", 1)


def tie(value, *others):
    token = lax.optimization_barrier((lax.create_token(),) + others)[0]
    return lax.optimization_barrier((token, value))[1]


def gate(value):
    return swap(value[:16, :PAIR])


def bits_of(axis, low_first):
    n = lax.axis_size(axis)
    order = list(range(n.bit_length() - 1))
    return order if low_first else order[::-1]


def bit_at(axis, bit):
    return (lax.axis_index(axis) >> bit) & 1


class Gathering:
    def __init__(self, value, axis, low_first):
        self.axis, self.order = axis, bits_of(axis, low_first)
        self.blocks, self.came = {0: value}, None

    def start(self, *others):
        bit = self.order[0]
        keys = sorted(self.blocks)
        sent = [self.blocks[k] for k in keys]
        sent = sent[0] if len(sent) == 1 else jnp.concatenate(sent, axis=0)
        if others:
            sent = tie(sent, *others)
        self.came = flip(sent, self.axis, 1 << bit)
        return self.came

    def join(self):
        bit = self.order.pop(0)
        mine = bit_at(self.axis, bit)
        keys = sorted(self.blocks)
        rows = self.came.shape[0] // len(keys)
        blocks = {}
        for place, k in enumerate(keys):
            held, other = self.blocks[k], self.came[place * rows : (place + 1) * rows]
            blocks[k] = jnp.where(mine == 0, held, other)
            blocks[k | 1 << bit] = jnp.where(mine == 0, other, held)
        self.blocks = blocks

    def step(self, *others):
        self.join()
        return self.start(*others)

    def end(self):
        self.join()
        return jnp.concatenate([self.blocks[k] for k in sorted(self.blocks)], axis=0)


class Doubling:
    def __init__(self, value, *others):
        cut = value.shape[0] // 2
        self.parts = [
            Gathering(value[:cut], "fsdp", True),
            Gathering(value[cut:], "fsdp", False),
        ]
        self.start(*others)

    def start(self, *others):
        self.came = [g.start(*others) for g in self.parts]

    def after(self, *others):
        for g in self.parts:
            g.came = tie(g.came, *others)

    def step(self, *others):
        self.after(*others)
        for g in self.parts:
            g.join()
        self.start()

    def end(self, *others):
        self.after(*others)
        for g in self.parts:
            g.join()
        keys = sorted(self.parts[0].blocks)
        return jnp.concatenate([g.blocks[k] for k in keys for g in self.parts], axis=0)


def gather_offsets(value, axis, low_first, seen=None, late=None):
    found = {0: value}
    order = bits_of(axis, low_first)
    for bit in order:
        keys = sorted(found)
        sent = [found[k] for k in keys]
        sent = sent[0] if len(sent) == 1 else jnp.concatenate(sent, axis=0)
        if late is not None and bit == order[-1]:
            sent = tie(sent, late)
        came = flip(sent, axis, 1 << bit)
        rows = value.shape[0]
        if seen is not None:
            seen.append(came)
        for place, k in enumerate(keys):
            found[k ^ (1 << bit)] = came[place * rows : (place + 1) * rows]
    return [found[k] for k in range(lax.axis_size(axis))]


def natural(pieces, axis, dim=0):
    n = len(pieces)
    me = lax.axis_index(axis)
    return jnp.concatenate(
        [lax.select_n(me, *[pieces[j ^ m] for m in range(n)]) for j in range(n)], axis=dim
    )


def gather_direct(value, axis):
    n = lax.axis_size(axis)
    return natural([value] + [flip(value, axis, k) for k in range(1, n)], axis)


def exchange_direct(blocks, axis):
    me = lax.axis_index(axis)
    out = [lax.dynamic_index_in_dim(blocks, me ^ k, 0, keepdims=False) for k in range(len(blocks))]
    return out[:1] + [flip(out[k], axis, k) for k in range(1, len(blocks))]


def half_rows(held, index, bit, bits):
    rows = held.shape[0] // 2
    if bits[0] == bit:
        return lax.dynamic_slice_in_dim(held, index * rows, rows, 0)
    before = 1 << bits.index(bit)
    view = held.reshape(before, 2, rows // before, held.shape[1])
    return lax.dynamic_slice_in_dim(view, index, 1, 1).reshape(rows, held.shape[1])


class Scattering:
    def __init__(self, legs, away, held, bits, first):
        self.legs = [(axis, bit) for axis, low in legs for bit in bits_of(axis, low)][1:]
        self.bits = [b for b in bits if b != first]
        self.held, self.axis = held, legs[0][0]
        self.came = flip(away, legs[0][0], 1 << first)

    def step(self):
        axis, bit = self.legs.pop(0)
        if axis != self.axis:
            self.axis, self.bits = axis, bits_of(axis, False)
        mine = bit_at(axis, bit)

        def part(index):
            held = half_rows(self.held, index, bit, self.bits).astype(F32)
            return (held + half_rows(self.came, index, bit, self.bits).astype(F32)).astype(BF)

        away, held = part(1 - mine), part(mine)
        self.bits = [b for b in self.bits if b != bit]
        self.came, self.held = flip(away, axis, 1 << bit), held

    def end(self):
        return self.held.astype(F32) + self.came.astype(F32)


def scatter_value(value, legs):
    axis, low = legs[0]
    bit, bits = bits_of(axis, low)[0], bits_of(axis, False)
    mine = bit_at(axis, bit)
    return Scattering(
        legs, half_rows(value, 1 - mine, bit, bits), half_rows(value, mine, bit, bits), bits, bit
    )


class Halving:
    def __init__(self, pairs):
        n = lax.axis_size("fsdp")
        bits = bits_of("fsdp", False)
        firsts = [bits_of("fsdp", True)[0], bits_of("fsdp", False)[0]]

        def product(flipped):
            out = []
            for left, right in pairs:
                rows = left.shape[1] // n
                cut = rows // 2
                chosen = []
                for place, bit in enumerate(firsts):
                    index = bit_at("fsdp", bit) ^ flipped
                    sides = [
                        jnp.concatenate(
                            [
                                left[:, b * rows + place * cut : b * rows + (place + 1) * cut]
                                for b in range(n)
                                if b >> bit & 1 == v
                            ],
                            axis=1,
                        )
                        for v in range(2)
                    ]
                    chosen.append(jnp.where(index == 0, sides[0], sides[1]))
                out.append(tn(jnp.concatenate(chosen, axis=1), right).astype(BF))
            return out[0] if len(out) == 1 else jnp.concatenate(out, axis=1)

        self.away, self.keep = product(1), product(0)
        self.bits, self.firsts = bits, firsts
        self.ctx = False

    def launch(self, *others):
        away, keep = tie(self.away, *others) if others else self.away, self.keep
        cut = away.shape[0] // 2
        self.parts = [
            Scattering(
                [("fsdp", low)],
                away[place * cut : (place + 1) * cut],
                keep[place * cut : (place + 1) * cut],
                self.bits,
                self.firsts[place],
            )
            for place, low in enumerate((True, False))
        ]

    def after(self, *others):
        for p in self.parts:
            p.came = tie(p.came, *others)

    def flight(self):
        return [p.came for p in self.parts]

    def held(self):
        return [p.held for p in self.parts]

    def over(self):
        return not self.parts[0].legs

    def step(self, *others):
        if others:
            self.after(*others)
        if not self.over():
            while not self.over():
                for p in self.parts:
                    p.step()
        elif not self.ctx:
            value = jnp.concatenate([p.end().astype(BF) for p in self.parts], axis=0)
            self.parts, self.ctx = [scatter_value(value, [("ctx", True)])], True

    def end(self, *others):
        if others:
            self.after(*others)
        return self.parts[0].end()


def scatter_offsets(pieces, axis, seen=None):
    n = lax.axis_size(axis)
    held = dict(enumerate(pieces))
    for bit in bits_of(axis, True):
        last = n == 2 << bit
        away = [held[k].astype(BF) for k in sorted(held) if k >> bit & 1]
        came = flip(away[0] if len(away) == 1 else jnp.concatenate(away, axis=0), axis, 1 << bit)
        rows = pieces[0].shape[0]
        if seen is not None:
            seen.append(came)
        held = {k: v for k, v in held.items() if not k >> bit & 1}
        for place, k in enumerate(sorted(held)):
            held[k] = held[k].astype(F32) + came[place * rows : (place + 1) * rows].astype(F32)
            if not last:
                held[k] = held[k].astype(BF)
    return held[0]


def lanes_of(head, shape):
    lane = lax.broadcasted_iota(jnp.int32, shape, len(shape) - 1)
    return (lane // HEAD_DIM) == head


def project_kernel(x_ref, scales, weight, kept, out):
    x = x_ref[...].astype(F32)
    width = x.shape[1]
    centred = x - jnp.sum(x, axis=1, keepdims=True) * (1.0 / width)
    spread = jnp.sum(centred * centred, axis=1, keepdims=True) * (1.0 / width)
    normed = centred * lax.rsqrt(spread + EPS)
    attn_in = (normed * scales[0:1, :] + scales[1:2, :]).astype(BF)
    kept[:, :width] = attn_in
    kept[:, width:] = normed.astype(BF)
    out[...] = nn(attn_in, weight[...]).astype(BF)


def project(x_all, scales, weight):
    slots, width = x_all.shape
    cols = weight.shape[1]
    block = min(256, slots)
    return pl.pallas_call(
        project_kernel,
        grid=(slots // block,),
        in_specs=[
            pl.BlockSpec((block, width), lambda i: (i, 0)),
            pl.BlockSpec((2, width), lambda i: (0, 0)),
            pl.BlockSpec((width, cols), lambda i: (0, 0)),
        ],
        out_specs=[
            pl.BlockSpec((block, 2 * width), lambda i: (i, 0)),
            pl.BlockSpec((block, cols), lambda i: (i, 0)),
        ],
        out_shape=[
            jax.ShapeDtypeStruct((slots, 2 * width), BF),
            jax.ShapeDtypeStruct((slots, cols), BF),
        ],
        compiler_params=pltpu.CompilerParams(vmem_limit_bytes=VMEM_LIMIT),
        cost_estimate=pl.CostEstimate(
            flops=slots * width * cols * 4, transcendentals=0, bytes_accessed=slots * width * 8
        ),
        name="project",
    )(x_all, scales, weight)


def self_forward_kernel(n, block, info, qkv, mixed, logs, q_s, k_s, v_s):
    limit, me_c, me_t = (jnp.max(info[i : i + 1, :]) for i in range(3))
    half = block // 2
    for c in range(n):
        for t in range(2):
            place = (me_c ^ c) * block + (me_t ^ t) * half
            place = pl.multiple_of(place, half)
            to = slice(c * block + t * half, c * block + t * half + half)
            rows = qkv[pl.ds(place, half), :]
            q_s[to, :] = rows[:, :PAIR] * jnp.asarray(HEAD_DIM**-0.5, BF)
            keys = rows[:, PAIR : 2 * PAIR]
            for h in range(2):
                k_s[h, to, :] = jnp.where(lanes_of(h, keys.shape), keys, jnp.zeros_like(keys))
            v_s[:, to] = rows[:, 2 * PAIR :].astype(F32).T.astype(BF)

    def one(i, _):
        at_q = pl.multiple_of(i * block, block)
        query = q_s[pl.ds(at_q, block), :]

        def step(masked, j, state):
            at_k = pl.multiple_of(j * block, block)
            out = []
            for h in range(2):
                top, tot, acc = state[h]
                score = nt(k_s[h, pl.ds(at_k, block), :], query)
                if masked:
                    key_at = at_k + lax.broadcasted_iota(jnp.int32, score.shape, 0)
                    slot_at = at_q + lax.broadcasted_iota(jnp.int32, score.shape, 1)
                    score = jnp.where((key_at <= slot_at) & (key_at < limit), score, LOW)
                new_top = jnp.maximum(top, jnp.max(score, axis=0, keepdims=True))
                fade = jnp.exp(top - new_top)
                chance = jnp.exp(score - new_top)
                tot = tot * fade + jnp.sum(chance, axis=0, keepdims=True)
                part = nn(
                    v_s[h * HEAD_DIM : (h + 1) * HEAD_DIM, pl.ds(at_k, block)], chance.astype(BF)
                )
                out.append((new_top, tot, acc * fade + part))
            return tuple(out)

        start = tuple(
            (
                jnp.full((1, block), LOW, F32),
                jnp.zeros((1, block), F32),
                jnp.zeros((HEAD_DIM, block), F32),
            )
            for _ in range(2)
        )
        last = jnp.minimum(i + 1, (limit + block - 1) // block)
        state = lax.fori_loop(0, last, functools.partial(step, True), start)
        both = jnp.concatenate([acc / tot for _, tot, acc in state], axis=0)
        place = pl.multiple_of((me_c ^ i) * block, block)
        mixed[pl.ds(place, block), :] = both.T.astype(BF)
        for h in range(2):
            top, tot, _ = state[h]
            logs[h : h + 1, pl.ds(at_q, block)] = top + jnp.log(tot)
        return 0

    lax.fori_loop(0, n, one, 0)


def self_backward_kernel(
    n, block, info, qkv, mixed, grad, logs, grads, q_s, k_s, v_s, kt_s, d_s, delta_s, dq_s
):
    limit, me_c, me_t = (jnp.max(info[i : i + 1, :]) for i in range(3))
    half = block // 2
    for c in range(n):
        for t in range(2):
            place = (me_c ^ c) * block + (me_t ^ t) * half
            place = pl.multiple_of(place, half)
            to = slice(c * block + t * half, c * block + t * half + half)
            rows = qkv[pl.ds(place, half), :]
            q_s[to, :] = rows[:, :PAIR] * jnp.asarray(HEAD_DIM**-0.5, BF)
            keys = rows[:, PAIR : 2 * PAIR]
            values = rows[:, 2 * PAIR :]
            for h in range(2):
                k_s[h, to, :] = jnp.where(lanes_of(h, keys.shape), keys, jnp.zeros_like(keys))
                v_s[h, to, :] = jnp.where(lanes_of(h, keys.shape), values, jnp.zeros_like(keys))
            kt_s[:, to] = keys.astype(F32).T.astype(BF)
            at = pl.multiple_of((me_c ^ c) * block + t * half, half)
            dout = grad[pl.ds(at, half), :]
            d_s[to, :] = dout
            both = (dout.astype(F32) * mixed[pl.ds(at, half), :].astype(F32)).T
            for h in range(2):
                delta_s[h : h + 1, to] = jnp.sum(
                    both[h * HEAD_DIM : (h + 1) * HEAD_DIM, :], axis=0, keepdims=True
                )
    dq_s[...] = jnp.zeros_like(dq_s)

    def one(j, _):
        at_k = pl.multiple_of(j * block, block)

        def step(masked, i, state):
            at_q = pl.multiple_of(i * block, block)
            query = q_s[pl.ds(at_q, block), :]
            dout = d_s[pl.ds(at_q, block), :]
            out = []
            for h in range(2):
                dk, dv = state[h]
                score = nt(k_s[h, pl.ds(at_k, block), :], query)
                if masked:
                    key_at = at_k + lax.broadcasted_iota(jnp.int32, score.shape, 0)
                    slot_at = at_q + lax.broadcasted_iota(jnp.int32, score.shape, 1)
                    score = jnp.where((key_at <= slot_at) & (key_at < limit), score, LOW)
                chance = jnp.exp(score - logs[h : h + 1, pl.ds(at_q, block)])
                slopes = nt(v_s[h, pl.ds(at_k, block), :], dout)
                bend = (chance * (slopes - delta_s[h : h + 1, pl.ds(at_q, block)])).astype(BF)
                dv = dv + nn(chance.astype(BF), dout)
                dk = dk + nn(bend, query)
                side = slice(h * HEAD_DIM, (h + 1) * HEAD_DIM)
                dq_s[side, pl.ds(at_q, block)] += nn(kt_s[side, pl.ds(at_k, block)], bend)
                out.append((dk, dv))
            return tuple(out)

        start = tuple(
            (jnp.zeros((block, PAIR), F32), jnp.zeros((block, PAIR), F32)) for _ in range(2)
        )
        end = jnp.where(j * block < limit, n, j)
        state = lax.fori_loop(j, end, functools.partial(step, True), start)
        first_head = lanes_of(0, (block, PAIR))
        dk = jnp.where(first_head, state[0][0], state[1][0]).astype(BF)
        dv = jnp.where(first_head, state[0][1], state[1][1]).astype(BF)
        for t in range(2):
            place = (me_c ^ j) * block + (me_t ^ t) * half
            place = pl.multiple_of(place, half)
            grads[pl.ds(place, half), PAIR : 2 * PAIR] = dk[t * half : (t + 1) * half, :]
            grads[pl.ds(place, half), 2 * PAIR :] = dv[t * half : (t + 1) * half, :]
        return 0

    lax.fori_loop(0, n, one, 0)
    for c in range(n):
        dq = (dq_s[:, c * block : (c + 1) * block] * HEAD_DIM**-0.5).T.astype(BF)
        for t in range(2):
            place = (me_c ^ c) * block + (me_t ^ t) * half
            place = pl.multiple_of(place, half)
            grads[pl.ds(place, half), :PAIR] = dq[t * half : (t + 1) * half, :]


def cross_scores(limit, keys, query):
    score = nt(keys, query)
    key_at = lax.broadcasted_iota(jnp.int32, score.shape, 0)
    return jnp.where(key_at < limit, score, LOW)


def masked_pair(values, head):
    return jnp.where(lanes_of(head, values.shape), values, jnp.zeros_like(values))


def cross_forward_kernel(info, query_ref, kv, mixed, logs):
    limit = info[0]
    query = query_ref[...] * jnp.asarray(HEAD_DIM**-0.5, BF)
    keys = kv[0, :, :PAIR]
    values = kv[0, :, PAIR:].astype(F32).T.astype(BF)
    outs = []
    for h in range(2):
        score = cross_scores(limit, masked_pair(keys, h), query)
        top = jnp.max(score, axis=0, keepdims=True)
        chance = jnp.exp(score - top)
        tot = jnp.sum(chance, axis=0, keepdims=True)
        outs.append(nn(values[h * HEAD_DIM : (h + 1) * HEAD_DIM, :], chance.astype(BF)) / tot)
        logs[0, h : h + 1, :] = top + jnp.log(tot)
    mixed[...] = jnp.concatenate(outs, axis=0).T.astype(BF)


def cross_backward_kernel(info, query_ref, kv, mixed, grad, logs, dq_ref, dkv):
    limit = info[0]
    query = query_ref[...] * jnp.asarray(HEAD_DIM**-0.5, BF)
    keys = kv[0, :, :PAIR]
    values = kv[0, :, PAIR:]
    keys_t = keys.astype(F32).T.astype(BF)
    dout = grad[...]
    both = (dout.astype(F32) * mixed[...].astype(F32)).T
    dqs, dks, dvs = [], [], []
    for h in range(2):
        side = slice(h * HEAD_DIM, (h + 1) * HEAD_DIM)
        delta = jnp.sum(both[side, :], axis=0, keepdims=True)
        score = cross_scores(limit, masked_pair(keys, h), query)
        chance = jnp.exp(score - logs[0, h : h + 1, :])
        slopes = nt(masked_pair(values, h), dout)
        bend = (chance * (slopes - delta)).astype(BF)
        dvs.append(nn(chance.astype(BF), dout))
        dks.append(nn(bend, query))
        dqs.append(nn(keys_t[side, :], bend))
    dq_ref[...] = (jnp.concatenate(dqs, axis=0) * HEAD_DIM**-0.5).T.astype(BF)
    first_head = lanes_of(0, dks[0].shape)
    dkv[0, :, :PAIR] = jnp.where(first_head, dks[0], dks[1]).astype(BF)
    dkv[0, :, PAIR:] = jnp.where(first_head, dvs[0], dvs[1]).astype(BF)


VMEM_LIMIT = 48 * 1024 * 1024


def vmem_spec():
    return pl.BlockSpec(memory_space=pltpu.VMEM)


def smem_spec():
    return pl.BlockSpec(memory_space=pltpu.SMEM)


def self_forward(info, qkv, n):
    slots = qkv.shape[0]
    block = slots // n
    pairs = slots * slots
    return pl.pallas_call(
        functools.partial(self_forward_kernel, n, block),
        out_shape=(
            jax.ShapeDtypeStruct((slots, PAIR), BF),
            jax.ShapeDtypeStruct((2, slots), F32),
        ),
        in_specs=[vmem_spec(), vmem_spec()],
        out_specs=(vmem_spec(), vmem_spec()),
        scratch_shapes=[
            pltpu.VMEM((slots, PAIR), BF),
            pltpu.VMEM((2, slots, PAIR), BF),
            pltpu.VMEM((PAIR, slots), BF),
        ],
        compiler_params=pltpu.CompilerParams(vmem_limit_bytes=VMEM_LIMIT),
        cost_estimate=pl.CostEstimate(
            flops=pairs * PAIR * 4, transcendentals=pairs, bytes_accessed=slots * PAIR * 8
        ),
        name="self_forward",
    )(info, qkv)


def self_backward(info, qkv, mixed, grad, logs, n):
    slots = qkv.shape[0]
    block = slots // n
    pairs = slots * slots
    return pl.pallas_call(
        functools.partial(self_backward_kernel, n, block),
        out_shape=jax.ShapeDtypeStruct((slots, 3 * PAIR), BF),
        in_specs=[vmem_spec()] + [vmem_spec()] * 4,
        out_specs=vmem_spec(),
        scratch_shapes=[
            pltpu.VMEM((slots, PAIR), BF),
            pltpu.VMEM((2, slots, PAIR), BF),
            pltpu.VMEM((2, slots, PAIR), BF),
            pltpu.VMEM((PAIR, slots), BF),
            pltpu.VMEM((slots, PAIR), BF),
            pltpu.VMEM((2, slots), F32),
            pltpu.VMEM((PAIR, slots), F32),
        ],
        compiler_params=pltpu.CompilerParams(vmem_limit_bytes=VMEM_LIMIT),
        cost_estimate=pl.CostEstimate(
            flops=pairs * PAIR * 10, transcendentals=pairs, bytes_accessed=slots * PAIR * 20
        ),
        name="self_backward",
    )(info, qkv, mixed, grad, logs)


def cross_forward(info, query, kv, n):
    rows, keys = query.shape[0], kv.shape[1]
    pairs = rows * keys * n
    grid_spec = pltpu.PrefetchScalarGridSpec(
        num_scalar_prefetch=1,
        grid=(n,),
        in_specs=[
            pl.BlockSpec((rows, PAIR), lambda j, info: (0, j)),
            pl.BlockSpec((1, keys, 2 * PAIR), lambda j, info: (info[1] ^ j, 0, 0)),
        ],
        out_specs=[
            pl.BlockSpec((rows, PAIR), lambda j, info: (0, j)),
            pl.BlockSpec((1, 2, rows), lambda j, info: (j, 0, 0)),
        ],
    )
    return pl.pallas_call(
        cross_forward_kernel,
        grid_spec=grid_spec,
        out_shape=(
            jax.ShapeDtypeStruct((rows, PAIR * n), BF),
            jax.ShapeDtypeStruct((n, 2, rows), F32),
        ),
        compiler_params=pltpu.CompilerParams(vmem_limit_bytes=VMEM_LIMIT),
        cost_estimate=pl.CostEstimate(
            flops=pairs * PAIR * 8, transcendentals=2 * pairs, bytes_accessed=rows * PAIR * n * 6
        ),
        name="cross_forward",
    )(info, query, kv)


def cross_backward(info, query, kv, mixed, grad, logs, n):
    rows, keys = query.shape[0], kv.shape[1]
    pairs = rows * keys * n
    col = pl.BlockSpec((rows, PAIR), lambda j, info: (0, j))
    grid_spec = pltpu.PrefetchScalarGridSpec(
        num_scalar_prefetch=1,
        grid=(n,),
        in_specs=[
            col,
            pl.BlockSpec((1, keys, 2 * PAIR), lambda j, info: (info[1] ^ j, 0, 0)),
            col,
            col,
            pl.BlockSpec((1, 2, rows), lambda j, info: (j, 0, 0)),
        ],
        out_specs=[
            col,
            pl.BlockSpec((1, keys, 2 * PAIR), lambda j, info: (info[1] ^ j, 0, 0)),
        ],
    )
    return pl.pallas_call(
        cross_backward_kernel,
        grid_spec=grid_spec,
        out_shape=(
            jax.ShapeDtypeStruct((rows, PAIR * n), BF),
            jax.ShapeDtypeStruct((n, keys, 2 * PAIR), BF),
        ),
        compiler_params=pltpu.CompilerParams(vmem_limit_bytes=VMEM_LIMIT),
        cost_estimate=pl.CostEstimate(
            flops=pairs * PAIR * 20, transcendentals=2 * pairs, bytes_accessed=rows * PAIR * n * 10
        ),
        name="cross_backward",
    )(info, query, kv, mixed, grad, logs)


def tp_total(partial):
    mine = partial.astype(BF)
    return mine.astype(F32) + swap(mine).astype(F32)


def tp_join(mine):
    me = lax.axis_index("tp")
    other = swap(mine)
    return jnp.concatenate(
        [jnp.where(me == 0, mine, other), jnp.where(me == 0, other, mine)], axis=0
    )


def body(
    inputs,
    encoder_states,
    seq_lengths,
    enc_lengths,
    cotangent,
    norm_gains,
    norm_biases,
    w_query,
    w_key,
    w_value,
    w_out,
    w_cross_query,
    w_cross_key,
    w_cross_value,
    w_cross_out,
    w_inner,
    w_outer,
):
    n, f = lax.axis_size("ctx"), lax.axis_size("fsdp")
    me_c, me_t = lax.axis_index("ctx"), lax.axis_index("tp")
    rows, width = inputs.shape[1], inputs.shape[2]
    half = rows // 2
    wide = w_query.shape[1]
    shard = w_query.shape[0]
    seq_limit, enc_limit = seq_lengths[0], enc_lengths[0]
    self_info = jnp.stack([seq_limit, me_c, me_t] + [seq_limit] * 5).astype(jnp.int32)
    self_info = jnp.broadcast_to(self_info[:, None], (8, 128))
    cross_info = jnp.stack([enc_limit, me_c, me_t]).astype(jnp.int32)

    enc_half = encoder_states.shape[1] // 2

    def side(t):
        return jnp.concatenate(
            [
                lax.dynamic_slice_in_dim(inputs[0], t * half, half, 0),
                lax.dynamic_slice_in_dim(encoder_states[0], t * enc_half, enc_half, 0),
            ],
            axis=0,
        )

    five = jnp.stack([w_query, w_key, w_value, w_cross_key, w_cross_value], axis=1)
    five = five.reshape(shard, 5, n, PAIR).transpose(2, 0, 1, 3).reshape(n, shard, 5 * PAIR)
    params = jnp.concatenate([norm_gains, norm_biases], axis=0).reshape(1, 1, 8 * shard)
    params = jnp.pad(params, ((0, 0), (0, 15), (0, 5 * PAIR - 8 * shard)))
    five = jnp.concatenate([five, jnp.broadcast_to(params, (n,) + params.shape[1:])], axis=1)
    five = natural(exchange_direct(five, "ctx"), "ctx")
    in_z = Gathering(w_inner, "ctx", False)
    in_seen = [in_z.start()]
    five = gather_direct(five, "fsdp")
    while len(in_z.order) > 1:
        in_seen.append(in_z.step())

    seen_x = []
    mine_rows = gather_offsets(tie(side(me_t), in_seen[0]), "ctx", False, seen_x, in_seen[-1])
    w_in = Doubling(in_z.end())

    w_three = jnp.concatenate([w_out.T, w_cross_query, w_cross_out.T], axis=1)
    three_z = Gathering(w_three, "ctx", False)
    three_z.start(seen_x[0])
    in_first = w_in.came
    while len(w_in.parts[0].order) > 1:
        w_in.step(seen_x[0])
    while len(three_z.order) > 1:
        three_z.step()
    outer_z = Gathering(w_outer.T, "ctx", False)
    outer_z.start(seen_x[-1])

    w_three = Doubling(three_z.end())
    came_rows = swap(tie(jnp.concatenate(mine_rows[1:], axis=0), *in_first, *w_in.came))
    size = half + enc_half
    five = five.reshape(f * n, shard + 16, 5 * PAIR)
    params = five[:, shard, : 8 * shard].reshape(f * n, 8, shard)
    params = params.transpose(1, 0, 2).reshape(8, width).astype(F32)
    gains, biases = params[:4], params[4:]
    five = five[:, :shard].reshape(width, 5 * PAIR)
    w_qkv, w_ckv = five[:, : 3 * PAIR], five[:, 3 * PAIR :]
    their_rows = [side(1 - me_t)] + [came_rows[k * size : (k + 1) * size] for k in range(n - 1)]
    x_all = jnp.concatenate([v[:half] for k in range(n) for v in (mine_rows[k], their_rows[k])])
    enc_found = [[v[half:] for v in (mine_rows[k], their_rows[k])] for k in range(n)]
    enc_at = [[lax.select_n(me_t, e[0], e[1]), lax.select_n(me_t, e[1], e[0])] for e in enc_found]
    enc_all = natural([jnp.concatenate(e, axis=0) for e in enc_at], "ctx")
    ckv_own = nn(enc_all, w_ckv).astype(BF)
    seen_ckv = []
    ckv = jnp.stack(gather_offsets(ckv_own, "ctx", False, seen_ckv), axis=0)

    scales = jnp.concatenate([gains[:1], biases[:1]], axis=0)
    kept, qkv = project(tie(x_all, ckv_own), scales, w_qkv)
    three_first = w_three.came
    while len(w_three.parts[0].order) > 1:
        w_three.step(came_rows)
    while len(outer_z.order) > 1:
        outer_z.step(came_rows)
    mixed, logs = self_forward(
        self_info, tie(qkv, *three_first, *w_in.came, seen_ckv[0]), n
    )
    outer_z.came = tie(outer_z.came, mixed)
    w_outer_t = Doubling(outer_z.end())
    mixed_out = tie(mixed, *w_three.came)
    w_in = w_in.end(mixed_out)
    w_three = w_three.end(mixed_out)
    w_out_t, w_cq, w_co_t = w_three[:, :wide], w_three[:, wide : 2 * wide], w_three[:, 2 * wide :]
    pieces = [mixed_out[:rows]]
    pieces += [flip(mixed_out[k * rows : (k + 1) * rows], "ctx", k) for k in range(1, n)]
    attn_flat = natural(pieces, "ctx", 1)
    while len(w_outer_t.parts[0].order) > 1:
        w_outer_t.step(attn_flat)
    hidden_x = inputs[0].astype(F32)
    first = hidden_x + tp_total(nt(attn_flat, w_out_t))

    normed_c, scale_c = norm_parts(first)
    cross_in = (normed_c * gains[1] + biases[1]).astype(BF)
    cross_query = nn(cross_in, w_cq).astype(BF)
    cross_flat, cross_logs = cross_forward(cross_info, cross_query, ckv, n)
    second = first + tp_total(nt(cross_flat, w_co_t))

    w_outer_t = w_outer_t.end(cross_flat)
    normed_f, scale_f = norm_parts(second)
    ffn_in = (normed_f * gains[2] + biases[2]).astype(BF)
    inner = nn(ffn_in, w_in)
    gated, gate_pullback = jax.vjp(smooth_gate, inner)
    active = gated.astype(BF)
    third = second + tp_total(nt(active, w_outer_t))

    positions = me_c * rows + lax.iota(jnp.int32, rows)
    valid = (positions < seq_limit).astype(F32)[:, None]
    normed_y, scale_y = norm_parts(third)
    output = (normed_y * gains[3] + biases[3]) * valid

    grad_y = cotangent[0].astype(F32) * valid
    grad_third, gain_y, bias_y = norm_back(grad_y, normed_y, scale_y, gains[3])
    g3 = grad_third.astype(BF)
    outer = Halving([(g3, active)])
    outer.launch()
    grad_active = gate_pullback(nn(g3, w_outer_t))[0].astype(BF)
    partial = nt(grad_active, w_in).astype(BF)
    inside = Halving([(tie(ffn_in, partial), grad_active)])
    grad_ffn_in = partial.astype(F32) + swap(partial).astype(F32)
    part_f, gain_f, bias_f = norm_back(grad_ffn_in, normed_f, scale_f, gains[2])
    grad_second = grad_third + part_f
    g2 = grad_second.astype(BF)

    grad_cross = nn(g2, w_co_t).astype(BF)
    grad_cq, dkv = cross_backward(
        cross_info,
        cross_query,
        ckv,
        cross_flat,
        tie(grad_cross, *outer.held(), inside.keep, inside.away),
        cross_logs,
        n,
    )
    partial = nt(grad_cq, w_cq).astype(BF)
    grad_cross_in = partial.astype(F32) + swap(partial).astype(F32)
    part_c, gain_c, bias_c = norm_back(grad_cross_in, normed_c, scale_c, gains[1])
    grad_first = grad_second + part_c
    g1 = grad_first.astype(BF)
    inside.launch(g1, *outer.flight())
    outer.step(g1)

    grad_attn = nn(g1, w_out_t).astype(BF)
    grad_attn = grad_attn.reshape(rows, n, PAIR).transpose(1, 0, 2)
    token = gate(grad_attn[0])
    dmixed = exchange_direct(grad_attn, "ctx")
    three = Halving([(tie(g1, token), attn_flat), (cross_in, grad_cq), (g2, cross_flat)])
    seen_dkv = []
    grad_ckv = scatter_offsets([tie(dkv, token)[k] for k in range(n)], "ctx", seen_dkv).astype(BF)

    dmixed = tie(jnp.concatenate(dmixed, axis=0), three.keep, three.away, *outer.held())
    dqkv = self_backward(self_info, qkv, mixed, dmixed, logs, n)

    part = nt(tie(dqkv, *outer.flight()), w_qkv).astype(BF)
    enc_part = nt(grad_ckv, w_ckv).astype(BF)

    def block(k, u):
        place = ((me_c ^ k) * 2 + (me_t ^ u)) * enc_half
        return jnp.concatenate(
            [
                part[(2 * k + u) * half : (2 * k + u + 1) * half],
                lax.dynamic_slice_in_dim(enc_part, place, enc_half, 0),
            ],
            axis=0,
        )

    away = jnp.concatenate([block(k, 1) for k in range(n)], axis=0)
    came_part = swap(away)
    outer.step(away)
    inside.step(away)
    came_part = tie(came_part, *outer.held())
    part = [
        (
            block(k, 0).astype(F32) + came_part[k * size : (k + 1) * size].astype(F32)
        ).astype(BF)
        for k in range(n)
    ]
    dqkv_late = tie(dqkv, *part)
    order = bits_of("ctx", True)
    held, sent = dict(enumerate(part)), []
    for place, bit in enumerate(order):
        away = [held[k] for k in sorted(held) if k >> bit & 1]
        came = flip(away[0] if len(away) == 1 else jnp.concatenate(away, axis=0), "ctx", 1 << bit)
        if place == 0:
            both = tn(kept, dqkv_late)
            gain_a = jnp.sum(both[width:] * w_qkv.astype(F32), axis=1)
            bias_a = nt(jnp.sum(dqkv_late.astype(F32), axis=0, keepdims=True), w_qkv.astype(F32))[0]
            norm_grads = jnp.stack(
                [gain_a, 0.5 * gain_c, 0.5 * gain_f, 0.5 * gain_y]
                + [bias_a, 0.5 * bias_c, 0.5 * bias_f, 0.5 * bias_y]
            )
            norm_grads = norm_grads + swap(norm_grads)
            norm_grads = norm_grads.reshape(8, f * n, shard).transpose(1, 0, 2)
            norm_grads = norm_grads.reshape(f * n, 1, 8 * shard)
            norm_grads = jnp.pad(norm_grads, ((0, 0), (0, 15), (0, 5 * PAIR - 8 * shard)))
            dfive = jnp.concatenate([both[:width], tn(enc_all, grad_ckv)], axis=1)
            dfive = dfive.reshape(f * n, shard, 5 * PAIR)
            dfive = jnp.concatenate([dfive, norm_grads], axis=1).astype(BF)
            dfive = dfive.reshape(f * n * (shard + 16), 5 * PAIR)
            dfive = scatter_value(dfive, [("fsdp", True)])
            three.launch(part[0], *inside.flight())
            fill = [dfive.held]
        elif place == 1:
            inside.step(sent[0])
            for leg in outer.parts:
                leg.came = tie(leg.came, sent[0])
                while leg.legs:
                    leg.step()
            while dfive.legs:
                dfive.came = tie(dfive.came, sent[0])
                dfive.step()
            three.step(sent[0])
            fill = [dfive.held, *outer.held(), *inside.held(), *three.held()]
        else:
            fill = []
        came = tie(came, *fill)
        sent.append(came)
        held = {k: v for k, v in held.items() if not k >> bit & 1}
        for at, k in enumerate(sorted(held)):
            held[k] = held[k].astype(F32) + came[at * size : (at + 1) * size].astype(F32)
            if place < len(order) - 1:
                held[k] = held[k].astype(BF)
    grad_attn_in = held[0]

    three.step(grad_attn_in)
    before = [grad_attn_in]
    for leg in inside.parts + three.parts:
        leg.came = tie(leg.came, *before)
        while leg.legs:
            leg.step()
        before.append(leg.held)
    outer_sum = outer.end(*before)
    three, last = three.end(), three.held()
    grad_outer, grad_inner = outer_sum.T, inside.end(*last)
    dfive = dfive.end().astype(BF).reshape(n, shard + 16, 5 * PAIR)
    dfive = lax.all_to_all(dfive, "ctx", 0, 0, tiled=False)
    norm_grads = jnp.sum(dfive[:, shard, : 8 * shard].astype(F32), axis=0).reshape(8, shard)
    dfive = dfive[:, :shard].reshape(n, shard, 5, PAIR).transpose(2, 1, 0, 3)
    dfive = dfive.reshape(5, shard, wide).astype(F32)

    def mine(values):
        return lax.dynamic_slice_in_dim(values, me_t * half, half, 0)

    normed_a, scale_a = norm_parts(mine(hidden_x))
    part_a, _, _ = norm_back(grad_attn_in[:half], normed_a, scale_a, gains[0])
    ours = jnp.concatenate([mine(grad_first) + part_a, grad_attn_in[half:]], axis=0)
    theirs = swap(ours)

    def joined(low, high):
        pair = [ours[low:high], theirs[low:high]]
        return jnp.concatenate(
            [jnp.where(me_t == 0, pair[0], pair[1]), jnp.where(me_t == 0, pair[1], pair[0])], axis=0
        )

    grad_inputs, grad_encoder = joined(0, half), joined(half, size)

    return (
        output[None],
        grad_inputs[None],
        grad_encoder[None],
        norm_grads[:4],
        norm_grads[4:],
        dfive[0],
        dfive[1],
        dfive[2],
        three[:, :wide].T,
        three[:, wide : 2 * wide],
        dfive[3],
        dfive[4],
        three[:, 2 * wide :].T,
        grad_inner,
        grad_outer,
    )


def solution(mesh):
    tokens = P("fsdp", "ctx", None)
    norms = P(None, ("fsdp", "ctx"))
    by_rows = P(("fsdp", "ctx"), "tp")
    by_cols = P("tp", ("fsdp", "ctx"))
    return jax.shard_map(
        body,
        mesh=mesh,
        in_specs=(
            tokens,
            tokens,
            P("fsdp"),
            P("fsdp"),
            tokens,
            norms,
            norms,
            by_rows,
            by_rows,
            by_rows,
            by_cols,
            by_rows,
            by_rows,
            by_rows,
            by_cols,
            by_rows,
            by_cols,
        ),
        out_specs=(
            tokens,
            tokens,
            tokens,
            norms,
            norms,
            by_rows,
            by_rows,
            by_rows,
            by_cols,
            by_rows,
            by_rows,
            by_rows,
            by_cols,
            by_rows,
            by_cols,
        ),
        check_vma=False,
    )
```
